32 devices in a mesh: groups: 2 (over y), seq: 4 (over z), head: 2 (over x), rep: 2 (over core).
Axes of the slice: x: 2, y: 2, z: 4, core: 2. Of those that a mesh axis runs over, the one named last changes fastest.
Arguments:
- tokens: bfloat16 [4096, 5376], P(('groups', 'seq'), ('head', 'rep')), parts along dimension 0, may hold values from -6 to 6
- query_matrix: bfloat16 [5376, 2048], P(None, ('head', 'rep')), may hold values from -0.078125 to 0.078125
- key_matrix: bfloat16 [5376, 1024], P(None, 'head'), may hold values from -0.078125 to 0.078125
- value_matrix: bfloat16 [5376, 1024], P(None, 'head'), may hold values from -0.078125 to 0.078125
- output_matrix: bfloat16 [2048, 5376], P(None, ('head', 'rep')), may hold values from -0.125 to 0.125
- query_gain: float32 [128], replicated, may hold values from 0.1 to 1.9
- key_norm_gain: float32 [128], replicated, may hold values from 0.1 to 1.9
- adapter_down: bfloat16 [8, 5376, 96], P('seq', ('head', 'rep')), may hold values from -0.078125 to 0.078125
- adapter_up_query: bfloat16 [8, 32, 2048], P('seq', None, ('head', 'rep')), may hold values from -1 to 1
- key_value_up_panels: bfloat16 [8, 2, 32, 1024], P('seq', None, None, 'head'), may hold values from -1 to 1
- adapter_out_down: bfloat16 [8, 2048, 32], P('seq', ('head', 'rep')), may hold values from -0.125 to 0.125
- adapter_out_up: bfloat16 [8, 32, 5376], P('seq', None, ('head', 'rep')), may hold values from -1 to 1
- request_of_block: int32 [32], P('groups'), parts along dimension 0, may hold values from 0 to 1, never falling along the last dimension, each value on 1 to 12 neighbouring positions
- adapter_of_request: int32 [4], P('groups'), parts along dimension 0, may hold values from 0 to 7
Outputs:
- result: bfloat16 [4096, 5376], P(('groups', 'seq'), ('head', 'rep')), parts along dimension 0
The draws below stay inside these ranges and needn't reach their ends.
There are 2 independent parts, one for each index of `groups`. The reference program is written for one: setup_inputs(seed, part) draws one part's arguments, and reference() takes and returns one part's arrays. A program takes and returns all parts, laid end to end along the dimension named above; an argument that names none is the same for every part. Nothing has to cross between parts.
Inputs may be any that keep to these rules, and one draw needn't show every extreme that they name: `request_of_block`: never falls from one block to the next; every request has 1 to 12 blocks.
All inputs are finite; a program needn't handle non-finite values.
Results may differ from the reference program's by a relative error of at most 0.014.
Values may be sent and summed in bfloat16 or wider, within the bound.
No kernel may reach another device: no remote copies, remote signals or barrier semaphores. Data moves between devices by JAX's collectives and lax.ppermute only.
A program may use at most 128 MiB of HBM per device.

```python
import math
import jax
import jax.numpy as jnp
import numpy as np
from jax import lax

MODEL_WIDTH = 5376
QUERY_HEAD_COUNT = 16
KEY_VALUE_HEADS = 8
HEAD_SIZE = 128
ADAPTER_RANK = 32
KEY_WINDOW = 1024
BLOCK = 128
NREQ = 2
TOKEN_TOTAL = 2048
NBLK = 16
MOSTB = 12
ADAPTER_COUNT = 8


def steps_of(stream_key, extent, pieces, least, high):
    loudness, own = 1.0, jax.random.fold_in(stream_key, 6)
    for axis_at, blocks in pieces:
        heights = jnp.exp(jax.random.uniform(jax.random.fold_in(own, axis_at), (blocks,), jnp.float32, least / len(pieces), high / len(pieces)))
        loudness = loudness * jnp.repeat(heights, extent[axis_at] // blocks).reshape([-1 if axis == axis_at else 1 for axis in range(len(extent))])
    return loudness


def cumulative_ranks(amount, skew):
    loads = [(1 << 20) // math.isqrt(standing ** skew) + 1 for standing in range(1, amount + 1)]
    deviation = 1 + sum(loads) // (1 << 30)
    return np.cumsum(np.array([max(1, weight // deviation) for weight in loads]))


def skewed_ids(rng, extent, number_of, skew):
    table = cumulative_ranks(number_of, skew)
    lot = jax.random.randint(jax.random.fold_in(rng, 1), extent, 0, int(table[number_of - 1]))
    standing = jnp.searchsorted(jnp.asarray(table, jnp.int32), lot, side="right")
    return jax.random.permutation(jax.random.fold_in(rng, 2), number_of)[standing].astype(jnp.int32)


def split_up(number_of, total, limit, lean):
    weights = [(1 << 20) // math.isqrt(grade ** lean) + 1 for grade in range(2, number_of + 1)]
    surplus, counts = total - limit - (number_of - 1), [1] * (number_of - 1)
    while surplus > 0:
        free = [i for i in range(number_of - 1) if counts[i] < limit]
        pool, left = sum([weights[i] for i in free]), surplus
        for i in free:
            addition = min(limit - counts[i], max(1, left * weights[i] // pool), surplus)
            counts[i] = counts[i] + addition
            surplus = surplus - addition
    return np.array([limit] + counts)


def uneven(stream_key, number_of, total, most, lean):
    if number_of == 2:
        one = jax.random.randint(stream_key, (), max(1, total - most), min(most, total - 1) + 1)
        return jnp.stack([one, total - one])
    tallies = jnp.asarray(split_up(number_of, total, most, lean), jnp.int32)
    pairs = (number_of - 1) // 2
    donor, receiver = tallies[1:1 + 2 * pairs:2], tallies[2:2 + 2 * pairs:2]
    margin = jnp.minimum(donor - 1, most - receiver)
    moved = jax.random.randint(jax.random.fold_in(stream_key, 1), (pairs,), 0, 1 << 20) % (margin + 1)
    tallies = tallies.at[1:1 + 2 * pairs:2].set(donor - moved).at[2:2 + 2 * pairs:2].set(receiver + moved)
    return tallies[jax.random.permutation(jax.random.fold_in(stream_key, 2), number_of)]


def noise(own_key, extent, scale, reach, cuts=(), kind=jnp.bfloat16):
    factor_of = steps_of(own_key, extent, cuts, -0.22, 0.18) if cuts else 1.0
    values = jax.random.normal(own_key, extent, jnp.float32) * scale * factor_of
    return jnp.minimum(jnp.maximum(values, -reach), reach).astype(kind)


def setup_inputs(seed: int = 0, part: int = 0) -> dict:
    streams_of = jax.random.split(jax.random.key(seed), 15)
    part_keys = jax.random.split(jax.random.fold_in(streams_of[14], part), 15)
    tokens = noise(part_keys[0], (TOKEN_TOTAL, MODEL_WIDTH), 1.0, 6.0, ((0, 4), (1, 4)))
    query_matrix = noise(streams_of[1], (MODEL_WIDTH, QUERY_HEAD_COUNT * HEAD_SIZE), MODEL_WIDTH ** -0.5, 0.078125, ((1, 4),))
    key_matrix = noise(streams_of[2], (MODEL_WIDTH, KEY_VALUE_HEADS * HEAD_SIZE), MODEL_WIDTH ** -0.5, 0.078125, ((1, 2),))
    value_matrix = noise(streams_of[3], (MODEL_WIDTH, KEY_VALUE_HEADS * HEAD_SIZE), MODEL_WIDTH ** -0.5, 0.078125, ((1, 2),))
    output_matrix = noise(streams_of[4], (QUERY_HEAD_COUNT * HEAD_SIZE, MODEL_WIDTH), (QUERY_HEAD_COUNT * HEAD_SIZE) ** -0.5, 0.125, ((1, 4),))
    query_gain = jnp.clip(1.0 + 0.18 * jax.random.normal(streams_of[5], (HEAD_SIZE,), jnp.float32), 0.1, 1.9)
    key_norm_gain = jnp.clip(1.0 + 0.18 * jax.random.normal(streams_of[6], (HEAD_SIZE,), jnp.float32), 0.1, 1.9)
    adapter_down = noise(streams_of[7], (ADAPTER_COUNT, MODEL_WIDTH, 3 * ADAPTER_RANK), MODEL_WIDTH ** -0.5, 0.078125, ((0, 4), (1, 4)))
    adapter_up_query = noise(streams_of[8], (ADAPTER_COUNT, ADAPTER_RANK, QUERY_HEAD_COUNT * HEAD_SIZE), ADAPTER_RANK ** -0.5, 1.0, ((0, 4), (2, 4)))
    key_value_up_panels = noise(streams_of[9], (ADAPTER_COUNT, 2, ADAPTER_RANK, KEY_VALUE_HEADS * HEAD_SIZE), ADAPTER_RANK ** -0.5, 1.0, ((0, 4), (3, 2)))
    adapter_out_down = noise(streams_of[10], (ADAPTER_COUNT, QUERY_HEAD_COUNT * HEAD_SIZE, ADAPTER_RANK), (QUERY_HEAD_COUNT * HEAD_SIZE) ** -0.5, 0.125, ((0, 4), (1, 4)))
    adapter_out_up = noise(streams_of[11], (ADAPTER_COUNT, ADAPTER_RANK, MODEL_WIDTH), ADAPTER_RANK ** -0.5, 1.0, ((0, 4), (2, 4)))
    request_of_block = jnp.searchsorted(jnp.cumsum(uneven(part_keys[12], NREQ, NBLK, MOSTB, 2)), jnp.arange(NBLK), side="right").astype(jnp.int32)
    adapter_of_request = skewed_ids(part_keys[13], (NREQ,), ADAPTER_COUNT, 2)
    return dict(tokens=tokens, query_matrix=query_matrix, key_matrix=key_matrix, value_matrix=value_matrix, output_matrix=output_matrix, query_gain=query_gain, key_norm_gain=key_norm_gain, adapter_down=adapter_down, adapter_up_query=adapter_up_query, key_value_up_panels=key_value_up_panels, adapter_out_down=adapter_out_down, adapter_out_up=adapter_out_up, request_of_block=request_of_block, adapter_of_request=adapter_of_request)


norm_epsilon = 1e-06
rope_base = 10000.0
score_scale = 168.0 ** (-0.5)
adapter_scale = 2.0

def per_head_norm(values, scale_gain):
    mean_square = lax.optimization_barrier(jnp.mean(values * values, axis=-1, keepdims=True))
    return values * lax.rsqrt(mean_square + norm_epsilon) * scale_gain

def rope_tables(positions, head_dim):
    half_dim = head_dim // 2
    frequency = jnp.power(rope_base, -jnp.arange(half_dim, dtype=jnp.float32) * 2.0 / head_dim)
    angles = positions.astype(jnp.float32)[:, None] * frequency[None, :]
    return (jnp.cos(angles), jnp.sin(angles))

def rotate_feature_pairs(values, cosine_table, sine_values):
    half_dim = values.shape[-1] // 2
    first_half = values[..., :half_dim]
    second_half = values[..., half_dim:]
    cosine_table = cosine_table[:, None, :]
    sine_values = sine_values[:, None, :]
    return jnp.concatenate([first_half * cosine_table - second_half * sine_values, second_half * cosine_table + first_half * sine_values], axis=-1)

def request_starts(block_requests, all_requests):
    earlier = (all_requests[None, :] < block_requests[:, None]).astype(jnp.int32)
    return (lax.optimization_barrier(jnp.sum(earlier, axis=1)) * BLOCK).astype(jnp.int32)

def reference(tokens, query_matrix, key_matrix, value_matrix, output_matrix, query_gain, key_norm_gain, adapter_down, adapter_up_query, key_value_up_panels, adapter_out_down, adapter_out_up, request_of_block, adapter_of_request):
    block_adapter = adapter_of_request[request_of_block]
    token_block_list = tokens.reshape(NBLK, BLOCK, MODEL_WIDTH).astype(jnp.float32)
    picked_down_panels = adapter_down[block_adapter].astype(jnp.float32)
    reduced_rank_rows = jnp.einsum('myj,mjc->myc', token_block_list, picked_down_panels)
    reduced_rank_rows = lax.optimization_barrier(reduced_rank_rows.astype(jnp.bfloat16)).astype(jnp.float32)
    picked_query_panels = adapter_up_query[block_adapter].astype(jnp.float32)
    picked_key_panels = key_value_up_panels[block_adapter].astype(jnp.float32)
    query_linear = jnp.dot(tokens, query_matrix, preferred_element_type=jnp.float32) + adapter_scale * jnp.einsum('tlq,tqo->tlo', reduced_rank_rows[..., :ADAPTER_RANK], picked_query_panels).reshape(TOKEN_TOTAL, QUERY_HEAD_COUNT * HEAD_SIZE)
    key_linear = jnp.dot(tokens, key_matrix, preferred_element_type=jnp.float32) + adapter_scale * jnp.einsum('tlq,tqo->tlo', reduced_rank_rows[..., ADAPTER_RANK:2 * ADAPTER_RANK], picked_key_panels[:, 0]).reshape(TOKEN_TOTAL, KEY_VALUE_HEADS * HEAD_SIZE)
    value_linear = jnp.dot(tokens, value_matrix, preferred_element_type=jnp.float32) + adapter_scale * jnp.einsum('tlq,tqo->tlo', reduced_rank_rows[..., 2 * ADAPTER_RANK:], picked_key_panels[:, 1]).reshape(TOKEN_TOTAL, KEY_VALUE_HEADS * HEAD_SIZE)
    key_before_rotation = key_linear.astype(jnp.bfloat16)
    value_vectors = value_linear.astype(jnp.bfloat16)
    token_index = jnp.arange(TOKEN_TOTAL, dtype=jnp.int32)
    token_request = jnp.repeat(request_of_block, BLOCK)
    token_start = jnp.repeat(request_starts(request_of_block, request_of_block), BLOCK)
    cosine_table, sine_values = rope_tables(token_index - token_start, HEAD_SIZE)
    query_rows = (rotate_feature_pairs(per_head_norm(query_linear.reshape(TOKEN_TOTAL, QUERY_HEAD_COUNT, HEAD_SIZE), query_gain), cosine_table, sine_values) * score_scale).astype(jnp.bfloat16)
    rotated_keys = rotate_feature_pairs(per_head_norm(key_before_rotation.astype(jnp.float32).reshape(TOKEN_TOTAL, KEY_VALUE_HEADS, HEAD_SIZE), key_norm_gain), cosine_table, sine_values).astype(jnp.bfloat16)
    query_extent = math.gcd(TOKEN_TOTAL, 512)
    keys_with_padding = jnp.concatenate([jnp.zeros((KEY_WINDOW, KEY_VALUE_HEADS, HEAD_SIZE), jnp.bfloat16), rotated_keys], axis=0)
    values_with_padding = jnp.concatenate([jnp.zeros((KEY_WINDOW, KEY_VALUE_HEADS, HEAD_SIZE), jnp.bfloat16), value_vectors.reshape(TOKEN_TOTAL, KEY_VALUE_HEADS, HEAD_SIZE)], axis=0)

    def attend_block(block_leading):
        block_leading = block_leading.astype(jnp.int32)
        query_portion = lax.dynamic_slice_in_dim(query_rows, block_leading, query_extent, 0).reshape(query_extent, KEY_VALUE_HEADS, 2, HEAD_SIZE).astype(jnp.float32)
        key_part = lax.dynamic_slice_in_dim(keys_with_padding, block_leading, KEY_WINDOW + query_extent, 0).astype(jnp.float32)
        value_part = lax.dynamic_slice_in_dim(values_with_padding, block_leading, KEY_WINDOW + query_extent, 0).astype(jnp.float32)
        query_position = block_leading + jnp.arange(query_extent, dtype=jnp.int32)
        key_position = block_leading - KEY_WINDOW + jnp.arange(KEY_WINDOW + query_extent, dtype=jnp.int32)
        query_request = lax.dynamic_slice_in_dim(token_request, block_leading, query_extent, 0)
        key_request = token_request[jnp.clip(key_position, 0, TOKEN_TOTAL - 1)]
        distance = query_position[:, None] - key_position[None, :]
        allowed = (key_position[None, :] >= 0) & (distance >= 0) & (distance < KEY_WINDOW) & (query_request[:, None] == key_request[None, :])
        scores = jnp.einsum('tgpd,kgd->gptk', query_portion, key_part)
        weights = jnp.where(allowed[None, None], jnp.exp(scores), 0.0)
        denominator = lax.optimization_barrier(jnp.sum(weights, axis=-1))
        rounded = lax.optimization_barrier(weights.astype(jnp.bfloat16)).astype(jnp.float32)
        summed = jnp.einsum('gptk,kgd->tgpd', rounded, value_part)
        normalized = summed / jnp.transpose(denominator, (2, 0, 1))[..., None]
        return normalized.astype(jnp.bfloat16).reshape(query_extent, QUERY_HEAD_COUNT * HEAD_SIZE)
    block_starts = jnp.arange(TOKEN_TOTAL // query_extent, dtype=jnp.int32) * query_extent
    attention_result = lax.map(attend_block, block_starts).reshape(TOKEN_TOTAL, QUERY_HEAD_COUNT * HEAD_SIZE)
    chosen_out_down = adapter_out_down[block_adapter].astype(jnp.float32)
    output_reduced_rank = jnp.einsum('bkc,bcr->bkr', attention_result.reshape(NBLK, BLOCK, QUERY_HEAD_COUNT * HEAD_SIZE).astype(jnp.float32), chosen_out_down)
    output_reduced_rank = lax.optimization_barrier(output_reduced_rank.astype(jnp.bfloat16)).astype(jnp.float32)
    picked_output_up = adapter_out_up[block_adapter].astype(jnp.float32)
    result = jnp.dot(attention_result, output_matrix, preferred_element_type=jnp.float32) + adapter_scale * jnp.einsum('zch,zhp->zcp', output_reduced_rank, picked_output_up).reshape(TOKEN_TOTAL, MODEL_WIDTH)
    return result.astype(jnp.bfloat16)
```

```python
import math

import jax
import jax.numpy as jnp
from jax import lax
from jax.experimental import pallas as pl
from jax.experimental.pallas import tpu as pltpu
from jax.sharding import PartitionSpec as P

HEAD_SIZE = 128
ADAPTER_RANK = 32
KEY_WINDOW = 1024
BLOCK = 128


norm_epsilon = 1e-06
rope_base = 10000.0
score_scale = 168.0 ** (-0.5)
adapter_scale = 2.0


def shifted(value, axis, by):
    size = lax.axis_size(axis)
    pairs = [(i, i + by) for i in range(size) if 0 <= i + by < size]
    return lax.ppermute(value, axis, pairs)


def per_head_norm(values, scale_gain):
    mean_square = jnp.mean(values * values, axis=-1, keepdims=True)
    return values * lax.rsqrt(mean_square + norm_epsilon) * scale_gain


def rope_tables(positions, head_dim):
    half_dim = head_dim // 2
    frequency = jnp.power(rope_base, -jnp.arange(half_dim, dtype=jnp.float32) * 2.0 / head_dim)
    angles = positions.astype(jnp.float32)[:, None] * frequency[None, :]
    return (jnp.cos(angles), jnp.sin(angles))


def rotate_feature_pairs(values, cosine_table, sine_values):
    half_dim = values.shape[-1] // 2
    first_half = values[..., :half_dim]
    second_half = values[..., half_dim:]
    cosine_table = cosine_table[:, None, :]
    sine_values = sine_values[:, None, :]
    return jnp.concatenate(
        [
            first_half * cosine_table - second_half * sine_values,
            second_half * cosine_table + first_half * sine_values,
        ],
        axis=-1,
    )


def request_starts(block_requests, all_requests):
    earlier = (all_requests[None, :] < block_requests[:, None]).astype(jnp.int32)
    return jnp.sum(earlier, axis=1) * BLOCK


def per_device_general(
    tokens,
    query_matrix,
    key_matrix,
    value_matrix,
    output_matrix,
    query_gain,
    key_norm_gain,
    adapter_down,
    adapter_up_query,
    key_value_up_panels,
    adapter_out_down,
    adapter_out_up,
    request_of_block,
    adapter_of_request,
):
    tok_rows, width_part = tokens.shape
    query_cols = query_matrix.shape[1]
    key_cols = key_matrix.shape[1]
    query_heads = query_cols // HEAD_SIZE
    block_count = tok_rows // BLOCK
    all_blocks = request_of_block.shape[0]
    request_total = adapter_of_request.shape[0]
    seq_index = lax.axis_index("seq")
    rep_index = lax.axis_index("rep")
    first_row = seq_index * tok_rows
    own_requests = lax.dynamic_slice_in_dim(
        request_of_block, seq_index * block_count, block_count, 0
    )
    request_match = own_requests[:, None] == jnp.arange(request_total, dtype=jnp.int32)[None, :]
    own_adapters = jnp.sum(jnp.where(request_match, adapter_of_request[None, :], 0), axis=1)
    pool_part = (
        lax.all_gather(adapter_down, "seq", axis=0, tiled=True),
        lax.all_gather(adapter_up_query, "seq", axis=0, tiled=True),
        lax.all_gather(key_value_up_panels, "seq", axis=0, tiled=True),
        lax.all_gather(adapter_out_down, "seq", axis=0, tiled=True),
        lax.all_gather(adapter_out_up, "seq", axis=0, tiled=True),
    )
    held_count = pool_part[0].shape[0]
    select = (own_adapters[:, None] == jnp.arange(held_count, dtype=jnp.int32)[None, :]).astype(
        jnp.bfloat16
    )
    (
        picked_down_panels,
        picked_query_panels,
        picked_key_panels,
        chosen_out_down,
        picked_output_up,
    ) = tuple(
        (
            jnp.einsum(
                "bn,n...->b...", select, panel_part, preferred_element_type=jnp.float32
            ).astype(jnp.bfloat16)
            for panel_part in pool_part
        )
    )
    token_block_list = tokens.reshape(block_count, BLOCK, width_part)
    partial_low = jnp.einsum(
        "myj,mjc->myc", token_block_list, picked_down_panels, preferred_element_type=jnp.float32
    ).reshape(tok_rows, 3 * ADAPTER_RANK)
    reduced_rank_rows = (
        lax.psum(partial_low, ("head", "rep"))
        .astype(jnp.bfloat16)
        .reshape(block_count, BLOCK, 3 * ADAPTER_RANK)
    )
    feature_part = lax.all_gather(tokens, ("head", "rep"), axis=1, tiled=True)
    query_add = jnp.dot(feature_part, query_matrix, preferred_element_type=jnp.float32)
    key_add = jnp.dot(feature_part, key_matrix, preferred_element_type=jnp.float32)
    value_add = jnp.dot(feature_part, value_matrix, preferred_element_type=jnp.float32)
    query_linear = query_add
    key_linear = key_add
    value_linear = value_add
    query_linear = query_linear + adapter_scale * jnp.einsum(
        "tlq,tqo->tlo",
        reduced_rank_rows[..., :ADAPTER_RANK],
        picked_query_panels,
        preferred_element_type=jnp.float32,
    ).reshape(tok_rows, query_cols)
    key_linear = key_linear + adapter_scale * jnp.einsum(
        "tlq,tqo->tlo",
        reduced_rank_rows[..., ADAPTER_RANK : 2 * ADAPTER_RANK],
        picked_key_panels[:, 0],
        preferred_element_type=jnp.float32,
    ).reshape(tok_rows, key_cols)
    value_linear = value_linear + adapter_scale * jnp.einsum(
        "tlq,tqo->tlo",
        reduced_rank_rows[..., 2 * ADAPTER_RANK :],
        picked_key_panels[:, 1],
        preferred_element_type=jnp.float32,
    ).reshape(tok_rows, key_cols)
    key_full = key_linear.astype(jnp.bfloat16)
    value_full = value_linear.astype(jnp.bfloat16)
    key_heads = key_cols // HEAD_SIZE
    token_index = first_row + jnp.arange(tok_rows, dtype=jnp.int32)
    token_request = jnp.repeat(own_requests, BLOCK)
    token_start = jnp.repeat(request_starts(own_requests, request_of_block), BLOCK)
    cosine_table, sine_values = rope_tables(token_index - token_start, HEAD_SIZE)
    query_rows = (
        rotate_feature_pairs(
            per_head_norm(query_linear.reshape(tok_rows, query_heads, HEAD_SIZE), query_gain),
            cosine_table,
            sine_values,
        )
        * score_scale
    ).astype(jnp.bfloat16)
    rotated_keys = rotate_feature_pairs(
        per_head_norm(
            key_full.astype(jnp.float32).reshape(tok_rows, key_heads, HEAD_SIZE), key_norm_gain
        ),
        cosine_table,
        sine_values,
    ).astype(jnp.bfloat16)
    group_heads = max(query_heads // 2, 1)
    group_size = query_heads // group_heads
    head_first = rep_index * query_heads // 2
    keys_used = lax.dynamic_slice_in_dim(rotated_keys, head_first, group_heads, 1).reshape(
        tok_rows, group_heads * HEAD_SIZE
    )
    values_used = lax.dynamic_slice_in_dim(
        value_full.reshape(tok_rows, key_heads, HEAD_SIZE), head_first, group_heads, 1
    ).reshape(tok_rows, group_heads * HEAD_SIZE)
    query_groups = query_rows.reshape(tok_rows, group_heads, group_size, HEAD_SIZE)
    block_table = jnp.arange(all_blocks, dtype=jnp.int32)
    empty_state = (
        jnp.zeros((tok_rows, group_heads, group_size, HEAD_SIZE), jnp.float32),
        jnp.zeros((group_heads, group_size, tok_rows), jnp.float32),
    )
    reach_blocks = KEY_WINDOW // tok_rows
    stacked = jnp.stack((keys_used, values_used))
    earlier = []
    for step_back in range(reach_blocks, 0, -1):
        earlier.append(shifted(stacked, "seq", step_back))
    window_stack = jnp.concatenate(earlier + [stacked], axis=1)
    fold_state = empty_state
    offset = first_row - reach_blocks * tok_rows
    key_block = window_stack[0]
    value_block = window_stack[1]
    key_length = key_block.shape[0]
    step_length = math.gcd(key_length, 512)
    steps_count = key_length // step_length
    key_steps = key_block.reshape(steps_count, step_length, group_heads, HEAD_SIZE)
    value_steps = value_block.reshape(steps_count, step_length, group_heads, HEAD_SIZE)

    def one_step(carry_state, step_inputs):
        step_keys, step_values, step_index = step_inputs
        key_position = offset + step_index * step_length + jnp.arange(step_length, dtype=jnp.int32)
        key_block_id = jnp.clip(key_position, 0, all_blocks * BLOCK - 1) // BLOCK
        key_request = jnp.sum(
            jnp.where(key_block_id[:, None] == block_table[None, :], request_of_block[None, :], 0),
            axis=1,
        )
        distance = token_index[:, None] - key_position[None, :]
        allowed = (
            (key_position[None, :] >= 0)
            & (distance >= 0)
            & (distance < KEY_WINDOW)
            & (token_request[:, None] == key_request[None, :])
        )
        scores = jnp.einsum(
            "tcpd,kcd->cptk", query_groups, step_keys, preferred_element_type=jnp.float32
        )
        weights = jnp.where(allowed[None, None], jnp.exp(scores), 0.0)
        numerator, denominator = carry_state
        denominator = denominator + jnp.sum(weights, axis=-1)
        numerator = numerator + jnp.einsum(
            "cptk,kcd->tcpd",
            weights.astype(jnp.bfloat16),
            step_values,
            preferred_element_type=jnp.float32,
        )
        return ((numerator, denominator), None)

    fold_state, unused_out = lax.scan(
        one_step, fold_state, (key_steps, value_steps, jnp.arange(steps_count, dtype=jnp.int32))
    )
    numerator, denominator = fold_state
    attention_result = (
        (numerator / jnp.transpose(denominator, (2, 0, 1))[..., None])
        .astype(jnp.bfloat16)
        .reshape(tok_rows, query_cols)
    )
    output_zero = (
        jnp.zeros((tok_rows, width_part), jnp.float32),
        jnp.zeros((tok_rows, ADAPTER_RANK), jnp.float32),
    )
    projected_rows = jnp.dot(
        lax.all_gather(attention_result, ("head", "rep"), axis=1, tiled=True),
        output_matrix,
        preferred_element_type=jnp.float32,
    )
    projected_rows, lowered = (projected_rows, output_zero[1])
    local_low = jnp.einsum(
        "bkc,bcr->bkr",
        attention_result.reshape(block_count, BLOCK, query_cols),
        chosen_out_down,
        preferred_element_type=jnp.float32,
    ).reshape(tok_rows, ADAPTER_RANK)
    output_reduced_rank = lax.psum(local_low, ("head", "rep")).astype(jnp.bfloat16)
    result = projected_rows + adapter_scale * jnp.einsum(
        "zch,zhp->zcp",
        output_reduced_rank.reshape(block_count, BLOCK, ADAPTER_RANK),
        picked_output_up,
        preferred_element_type=jnp.float32,
    ).reshape(tok_rows, width_part)
    return result.astype(jnp.bfloat16)


F32 = jnp.float32
BF16 = jnp.bfloat16
VMEM_SMALL = 16 * 1024 * 1024
VMEM_LARGE = 56 * 1024 * 1024
SWAP = [(0, 1), (1, 0)]
SHARD_BLOCKS = 4
CHUNK = 256
CHUNK_BLOCKS = CHUNK // BLOCK
META_ADAPTER = 3
META_REQUEST = 5


def dot(a, b):
    return lax.dot_general(a, b, (((1,), (0,)), ((), ())), preferred_element_type=F32)


def dot_t(a, b):
    return lax.dot_general(a, b, (((0,), (0,)), ((), ())), preferred_element_type=F32)


VM = pl.BlockSpec(memory_space=pltpu.VMEM)
SM = pl.BlockSpec(memory_space=pltpu.SMEM)
HB = pl.BlockSpec(memory_space=pl.ANY)
FAR = pl.BlockSpec(memory_space=pltpu.HBM)


def shape(dims, dtype=BF16):
    return jax.ShapeDtypeStruct(dims, dtype)


def call(kernel, name, out_shape, in_specs, args, scratch=(), out_specs=None, grid=None, after=()):
    count = len(in_specs)

    def body(*refs):
        kernel(*refs[:count], *refs[count + len(after) :])

    outs = out_specs
    if outs is None:
        outs = VM if isinstance(out_shape, jax.ShapeDtypeStruct) else tuple(VM for _ in out_shape)
    more = dict(grid=grid) if grid else {}
    return pl.pallas_call(
        body,
        out_shape=out_shape,
        in_specs=list(in_specs) + [HB] * len(after),
        out_specs=outs,
        scratch_shapes=list(scratch),
        compiler_params=pltpu.CompilerParams(vmem_limit_bytes=VMEM_LARGE if FAR in in_specs else VMEM_SMALL),
        cost_estimate=pl.CostEstimate(flops=1000, bytes_accessed=1000, transcendentals=0),
        name=name,
        **more,
    )(*args, *after)


def split_kernel(tokens, *chunks):
    for c, chunk in enumerate(chunks):
        chunk[...] = tokens[:, c * CHUNK : (c + 1) * CHUNK]


def picked(meta, held, quarter):
    request = lax.div(quarter, 2)
    slot = meta[META_ADAPTER + request] - meta[0] * held
    here = jnp.logical_and(slot >= 0, slot < held)
    keep = jnp.where(here, 1.0, 0.0).astype(F32)
    return jnp.clip(slot, 0, held - 1), keep, lax.rem(quarter, 2)


def pack_kernel(meta, down_far, up_q_far, up_kv_far, *refs):
    quarters, (down, up_q, up_kv, sems) = refs[:4], refs[4:]
    copies = [
        pltpu.make_async_copy(a, b, sems.at[i])
        for i, (a, b) in enumerate(((down_far, down), (up_q_far, up_q), (up_kv_far, up_kv)))
    ]
    for copy in copies:
        copy.start()
    for copy in copies:
        copy.wait()
    half = up_kv.shape[3] // 2
    cols = up_q.shape[2]
    width = down.shape[2]
    for step, out in enumerate(quarters):
        slot, keep, part = picked(meta, down.shape[0], jnp.bitwise_xor(meta[0], step))
        rows = pl.ds(pl.multiple_of(part * 48, 16), 48)
        ranks = pl.ds(pl.multiple_of(part * 16, 16), 16)
        out[0:48, :] = (down[slot, rows, :].astype(F32) * keep).astype(BF16)
        out[48:64, 0:cols] = (up_q[slot, ranks, :].astype(F32) * keep).astype(BF16)
        for which in range(2):
            both = up_kv[slot, which, ranks, :].astype(F32) * keep
            mine = jnp.where(meta[1] == 0, both[:, :half], both[:, half:])
            out[48:64, cols + which * half : cols + (which + 1) * half] = mine.astype(BF16)
        out[48:64, 1024:width] = jnp.zeros((16, width - 1024), BF16)


def pack_out_kernel(meta, down, up, *quarters):
    width = up.shape[2]
    for step, out in enumerate(quarters):
        slot, keep, part = picked(meta, down.shape[0], jnp.bitwise_xor(meta[0], step))
        ranks = pl.ds(pl.multiple_of(part * 16, 16), 16)
        out[:, 0:width] = (up[slot, ranks, :].astype(F32) * keep).astype(BF16)
        out[:, width:1408] = jnp.zeros((16, 1408 - width), BF16)
        out[:, 1408:1920] = (down[slot, ranks, :].astype(F32) * keep).astype(BF16)


def sum_kernel(a, b, c, d, out):
    out[...] = a[...] + b[...] + c[...] + d[...]


def place_quarters(meta, quarters, panel):
    me = meta[0]
    low_side = me < 2
    at = (me, jnp.bitwise_xor(me, 1), jnp.where(low_side, 2, 1), jnp.where(low_side, 3, 0))
    for index, quarter in zip(at, quarters):
        panel[index] = quarter[...]


def low_kernel(meta, tok0, tok1, p0, p1, p2, p3, low_t, ups, panel):
    place_quarters(meta, (p0, p1, p2, p3), panel)
    down = jnp.concatenate([panel[j, 0:48, :] for j in range(4)], axis=0)
    both = jnp.concatenate([dot(down, tok0[...]), dot(down, tok1[...])], axis=1)
    for b in range(SHARD_BLOCKS):
        request = meta[META_REQUEST + meta[0] * SHARD_BLOCKS + b]
        at = slice(b * BLOCK, (b + 1) * BLOCK)
        fa = jnp.where(request == 0, 1.0, 0.0).astype(F32)
        low_t[:, at] = both[0:96, at] * fa + both[96:192, at] * (1.0 - fa)
    ups[...] = jnp.concatenate([panel[j, 48:64, 0:1024] for j in range(4)], axis=0)


def weight_copies(meta, weights, buffers, sems, chip, width):
    half = weights[0].shape[1] // 2
    lane = pl.ds(pl.multiple_of(meta[1] * half, BLOCK), half)
    copies = []
    for i, (w, buf) in enumerate(zip(weights, buffers)):
        lanes = lane if i < 2 else slice(None)
        pair = []
        for n, part in enumerate((chip + meta[1], chip + 1 - meta[1])):
            rows = pl.ds(pl.multiple_of(part * width, 16), width)
            pair.append(pltpu.make_async_copy(w.at[rows, lanes], buf.at[n], sems.at[i, n]))
        copies.append(pair)
    for pair in copies:
        for copy in pair:
            copy.start()
    return copies


WEIGHT_AT = (slice(0, 256), slice(256, 512), slice(512, 1024))


def near_kernel(meta, own0, own1, other, wq, wk, wv, *refs):
    outs, buffers, sems = refs[:-4], refs[-4:-1], refs[-1]
    copies = weight_copies(meta, (wk, wv, wq), buffers, sems, meta[2] * 2, other.shape[0])
    for at, pair, buf in zip(WEIGHT_AT, copies, buffers):
        pair[0].wait()
        pair[1].wait()
        for c, out in enumerate(outs):
            tok = slice(c * CHUNK, (c + 1) * CHUNK)
            out[:, at] = dot_t((own0, own1)[c][...], buf[0]) + dot_t(other[:, tok], buf[1])


def far_kernel(meta, part, own, other, wq, wk, wv, q_out, kv_out, *refs):
    buffers, sems = refs[:-1], refs[-1]
    copies = weight_copies(meta, (wk, wv, wq), buffers, sems, (1 - meta[2]) * 2, own.shape[0])
    for i, (at, pair, buf) in enumerate(zip(WEIGHT_AT, copies, buffers)):
        pair[0].wait()
        pair[1].wait()
        turned = jnp.transpose(part[:, at] + dot_t(own[...], buf[0]) + dot_t(other[...], buf[1]))
        if i == 2:
            q_out[...] = turned
        else:
            kv_out[at, :] = turned.astype(BF16)


def block_request(meta, block):
    return meta[META_REQUEST + jnp.maximum(block, 0)]


def by_request(meta, low, first_block):
    flags = []
    for b in range(SHARD_BLOCKS):
        request = block_request(meta, first_block + b)
        flags.append(jnp.full((1, BLOCK), jnp.where(request == 0, 1.0, 0.0).astype(F32)))
    flag = jnp.concatenate(flags, axis=1)
    rows = low.astype(BF16).astype(F32)
    return jnp.concatenate([rows * flag, rows * (1.0 - flag)], axis=0).astype(BF16)


def norm_rotate(x, gain, cosine, sine):
    mean_square = jnp.mean(x * x, axis=0, keepdims=True)
    u = x * lax.rsqrt(mean_square + norm_epsilon) * gain
    a = u[0:64]
    b = u[64:128]
    return jnp.concatenate([a * cosine - b * sine, b * cosine + a * sine], axis=0)


def finish_keys(meta, chunks, low_k, low_v, ups, gain, cosine, sine, keys, values, first):
    base = (meta[0] - 2) * SHARD_BLOCKS + first
    k_term = dot_t(ups[:, 512:768], by_request(meta, low_k, base))
    v_term = dot_t(ups[:, 768:1024], by_request(meta, low_v, base))
    for b in range(SHARD_BLOCKS):
        at = slice((first + b) * BLOCK, (first + b + 1) * BLOCK)
        here = slice(b * BLOCK, (b + 1) * BLOCK)
        chunk = chunks[b // CHUNK_BLOCKS]
        lanes = slice(b % CHUNK_BLOCKS * BLOCK, (b % CHUNK_BLOCKS + 1) * BLOCK)
        for g in range(2):
            head = slice(g * HEAD_SIZE, (g + 1) * HEAD_SIZE)
            k = chunk[head, lanes].astype(F32) + adapter_scale * k_term[head, here]
            k = k.astype(BF16).astype(F32)
            turned = norm_rotate(k, gain, cosine[:, at], sine[:, at])
            keys[at, head] = jnp.transpose(turned).astype(BF16)
        values[:, at] = (chunk[256:512, lanes].astype(F32) + adapter_scale * v_term[:, here]).astype(BF16)


def attend(meta, q, keys, values, c, g, low_block, high_block):
    base = (meta[0] - 2) * SHARD_BLOCKS
    mine = block_request(meta, base + 8 + c)
    head = slice(g * HEAD_SIZE, (g + 1) * HEAD_SIZE)
    at = slice(low_block * BLOCK, (high_block + 1) * BLOCK)
    scores = dot(keys[at, head], q)
    key = lax.broadcasted_iota(jnp.int32, (BLOCK, 2 * BLOCK), 0)
    query = jnp.bitwise_and(lax.broadcasted_iota(jnp.int32, (BLOCK, 2 * BLOCK), 1), BLOCK - 1)
    den = jnp.zeros((BLOCK, 2 * BLOCK), F32)
    pieces = []
    for j in range(low_block, high_block + 1):
        block = base + j
        ok = jnp.logical_and(block >= 0, block_request(meta, block) == mine)
        piece = jnp.exp(scores[(j - low_block) * BLOCK : (j - low_block + 1) * BLOCK])
        piece = piece * jnp.where(ok, 1.0, 0.0).astype(F32)
        if j == c + 8:
            piece = jnp.where(query >= key, piece, 0.0)
        if j == c:
            piece = jnp.where(query < key, piece, 0.0)
        den = den + piece
        pieces.append(piece.astype(BF16))
    num = dot(values[head, at], jnp.concatenate(pieces, axis=0))
    return num, jnp.sum(den, axis=0, keepdims=True)


def attend_near_kernel(
    meta, q0, q1, o0, o1, h0, h1, low, low_h, ups, q_gain, k_gain, cosine, sine,
    q_rot, num_out, den_out, keys, values,
):
    gain = k_gain[...]
    finish_keys(meta, (o0, o1), low[32:64, :], low[64:96, :], ups, gain, cosine, sine, keys, values, 8)
    finish_keys(meta, (h0, h1), low_h[0:32, :], low_h[32:64, :], ups, gain, cosine, sine, keys, values, 4)
    q_term = dot_t(ups[:, 0:512], by_request(meta, low[0:32, :], meta[0] * SHARD_BLOCKS))
    for c in range(SHARD_BLOCKS):
        q = (q0, q1)[c // CHUNK_BLOCKS]
        lanes = slice(c % CHUNK_BLOCKS * BLOCK, (c % CHUNK_BLOCKS + 1) * BLOCK)
        rows = slice(c * BLOCK, (c + 1) * BLOCK)
        at = slice((8 + c) * BLOCK, (9 + c) * BLOCK)
        for h in range(4):
            head = slice(h * HEAD_SIZE, (h + 1) * HEAD_SIZE)
            x = q[head, lanes] + adapter_scale * q_term[head, rows]
            q_rot[head, rows] = (norm_rotate(x, q_gain[...], cosine[:, at], sine[:, at]) * score_scale).astype(BF16)
    for g in range(2):
        for c in range(SHARD_BLOCKS):
            rows = slice(c * BLOCK, (c + 1) * BLOCK)
            heads = [slice((2 * g + h) * HEAD_SIZE, (2 * g + h + 1) * HEAD_SIZE) for h in range(2)]
            q = jnp.concatenate([q_rot[head, rows] for head in heads], axis=1)
            num, den = attend(meta, q, keys, values, c, g, max(4, c + 1), c + 8)
            for h in range(2):
                part = slice(h * BLOCK, (h + 1) * BLOCK)
                num_out[heads[h], rows] = num[:, part]
                den_out[2 * g + h : 2 * g + h + 1, rows] = den[:, part]


def attend_far_kernel(
    meta, q_rot, num_in, den_in, h0, h1, low_h, ups, k_gain, cosine, sine, p0, p1, p2, p3, out, keys, values, panel
):
    place_quarters(meta, (p0, p1, p2, p3), panel)
    cols = q_rot.shape[0]
    out[cols : cols + 64, :] = jnp.concatenate([panel[j, :, 1408:1920] for j in range(4)], axis=0)
    finish_keys(
        meta, (h0, h1), low_h[0:32, :], low_h[32:64, :], ups, k_gain[...], cosine, sine, keys, values, 0
    )
    for g in range(2):
        for c in range(SHARD_BLOCKS):
            rows = slice(c * BLOCK, (c + 1) * BLOCK)
            heads = [slice((2 * g + h) * HEAD_SIZE, (2 * g + h + 1) * HEAD_SIZE) for h in range(2)]
            q = jnp.concatenate([q_rot[head, rows] for head in heads], axis=1)
            num, den = attend(meta, q, keys, values, c, g, c, 3)
            for h in range(2):
                part = slice(h * BLOCK, (h + 1) * BLOCK)
                total = den_in[2 * g + h : 2 * g + h + 1, rows] + den[:, part]
                out[heads[h], rows] = ((num_in[heads[h], rows] + num[:, part]) / total).astype(BF16)


def out_copies(meta, w, buf, sems, chip, depth):
    rows = w.shape[0] // 2
    copies = []
    for half in range(2):
        at = slice(half * rows, (half + 1) * rows)
        pair = []
        for n, p in enumerate((chip + meta[1], chip + 1 - meta[1])):
            lanes = pl.ds(pl.multiple_of(p * depth, BLOCK), depth)
            pair.append(pltpu.make_async_copy(w.at[at, lanes], buf.at[n, at, :], sems.at[half, n]))
            pair[-1].start()
        copies.append((at, pair))
    return copies


def out_near_kernel(meta, own, other, w, part, low, buf, sems):
    cols = own.shape[1]
    copies = out_copies(meta, w, buf, sems, meta[2] * 2, cols)
    mine = own[0:cols, :]
    theirs = other[0:cols, :]
    low[...] = dot(own[cols : cols + 64, :], mine) + dot(other[cols : cols + 64, :], theirs)
    for at, pair in copies:
        pair[0].wait()
        pair[1].wait()
        part[at, :] = dot(buf[0, at, :], mine) + dot(buf[1, at, :], theirs)


def out_far_kernel(meta, own, other, w, part, low, p0, p1, p2, p3, out, panel, buf, sems):
    copies = out_copies(meta, w, buf, sems, (1 - meta[2]) * 2, own.shape[1])
    place_quarters(meta, (p0, p1, p2, p3), panel)
    cols = own.shape[1]
    mine = own[0:cols, :]
    theirs = other[0:cols, :]
    lows = low[...] + dot(own[cols : cols + 64, :], mine) + dot(other[cols : cols + 64, :], theirs)
    lows = lows.astype(BF16).astype(F32)
    flags = []
    for b in range(SHARD_BLOCKS):
        request = block_request(meta, meta[0] * SHARD_BLOCKS + b)
        flags.append(jnp.full((1, BLOCK), jnp.where(request == 0, 1.0, 0.0).astype(F32)))
    flag = jnp.concatenate(flags, axis=1)
    chosen = jnp.concatenate([lows[0:32] * flag, lows[32:64] * (1.0 - flag)], axis=0).astype(BF16)
    up = jnp.concatenate([panel[j, :, 0 : w.shape[0]] for j in range(4)], axis=0)
    for at, pair in copies:
        total = part[at, :] + adapter_scale * dot_t(up[:, at], chosen)
        pair[0].wait()
        pair[1].wait()
        out[at, :] = (total + dot(buf[0, at, :], mine) + dot(buf[1, at, :], theirs)).astype(BF16)


def exchange_quarters(quarters):
    return [quarters[0]] + [lax.ppermute(quarters[s], "seq", [(j, j ^ s) for j in range(4)]) for s in (1, 2, 3)]


def share_quarter(total):
    pairs = ([(0, 1), (1, 0), (2, 3), (3, 2)], [(1, 2), (2, 1)], [(0, 2), (3, 1)])
    return [total] + [lax.ppermute(total, "seq", pair) for pair in pairs]


def per_device(
    tokens,
    query_matrix,
    key_matrix,
    value_matrix,
    output_matrix,
    query_gain,
    key_norm_gain,
    adapter_down,
    adapter_up_query,
    key_value_up_panels,
    adapter_out_down,
    adapter_out_up,
    request_of_block,
    adapter_of_request,
):
    rows, width = tokens.shape
    cols = query_matrix.shape[1]
    seq, rep, head = (lax.axis_index(name).astype(jnp.int32) for name in ("seq", "rep", "head"))
    meta = jnp.concatenate([jnp.stack([seq, rep, head]), adapter_of_request, request_of_block])
    tokens = tokens.T

    def across(value):
        return lax.ppermute(value, "head", SWAP)

    def core(value):
        return lax.ppermute(value, "rep", SWAP)

    def up(value, by=1):
        return lax.ppermute(value, "seq", [(i, (i + by) % 4) for i in range(4)])

    def after(value, *others):
        return lax.optimization_barrier((value, *others))[0]

    down_pool = jnp.swapaxes(adapter_down, 1, 2)
    quarters = call(
        pack_kernel,
        "pack",
        (shape((64, width)),) * 4,
        [SM, FAR, FAR, FAR],
        [meta, down_pool, adapter_up_query, key_value_up_panels],
        [pltpu.VMEM(a.shape, BF16) for a in (down_pool, adapter_up_query, key_value_up_panels)]
        + [pltpu.SemaphoreType.DMA((3,))],
    )
    received = exchange_quarters(quarters)

    chunks = rows // CHUNK
    token_chunks = call(
        split_kernel, "split", (shape((width, CHUNK)),) * chunks, [VM], [tokens], after=[quarters[0]]
    )
    far_own = [across(chunk) for chunk in token_chunks]
    near_other = core(tokens)

    weights = [query_matrix, key_matrix, value_matrix]
    weight_scratch = [
        pltpu.VMEM((2, width, 256), BF16),
        pltpu.VMEM((2, width, 256), BF16),
        pltpu.VMEM((2, width, cols), BF16),
        pltpu.SemaphoreType.DMA((3, 2)),
    ]
    near = call(
        near_kernel,
        "near",
        (shape((CHUNK, 1024), F32),) * chunks,
        [SM, VM, VM, VM, FAR, FAR, FAR],
        [meta, *token_chunks, near_other, *weights],
        weight_scratch,
        after=[quarters[0]],
    )

    def project(c, prior):
        return call(
            far_kernel,
            "far",
            (shape((cols, CHUNK), F32), shape((512, CHUNK))),
            [SM, VM, VM, VM, FAR, FAR, FAR],
            [meta, near[c], far_own[c], core(after(far_own[c], prior)), *weights],
            weight_scratch,
            after=[prior],
        )

    quarter = call(sum_kernel, "sum", shape((64, width)), [VM] * 4, received, after=[near[0]])
    pieces = share_quarter(quarter)

    first_q, first_kv = project(0, quarter)

    all_blocks = request_of_block.shape[0]
    window = jnp.arange(3 * rows, dtype=jnp.int32) + (seq - 2) * rows
    window = jnp.clip(window, 0, all_blocks * BLOCK - 1)
    second_start = jnp.sum((request_of_block < 1).astype(jnp.int32)) * BLOCK
    position = jnp.where(window >= second_start, window - second_start, window)
    half_dim = HEAD_SIZE // 2
    frequency = jnp.power(rope_base, -jnp.arange(half_dim, dtype=F32) * 2.0 / HEAD_SIZE)
    angles = frequency[:, None] * position.astype(F32)[None, :]
    cosine, sine = jnp.cos(angles), jnp.sin(angles)
    q_gain = query_gain.reshape(HEAD_SIZE, 1)
    k_gain = key_norm_gain.reshape(HEAD_SIZE, 1)

    out_quarters = call(
        pack_out_kernel,
        "pack_out",
        (shape((16, 1920)),) * 4,
        [SM, VM, VM],
        [meta, jnp.swapaxes(adapter_out_down, 1, 2), adapter_out_up],
        after=[first_kv],
    )
    out_received = exchange_quarters(out_quarters)

    partial_low, ups = call(
        low_kernel,
        "low",
        (shape((96, rows), F32), shape((64, 1024))),
        [SM] + [VM] * 6,
        [meta, *token_chunks, *pieces],
        [pltpu.VMEM((4, 64, width), BF16)],
        after=[first_kv],
    )
    chip_low = partial_low + core(partial_low)
    low = chip_low + across(chip_low)
    second_q, second_kv = project(1, chip_low)
    own_kv = [first_kv, second_kv]
    kv_prev = [up(kv) for kv in own_kv]
    kv_prev2 = [up(after(kv_prev[0], chip_low)), up(kv_prev[1])]
    low_kv = low[32:96].astype(BF16)
    low_prev = up(low_kv)
    low_prev2 = up(low_kv, 2)

    out_quarter = call(sum_kernel, "out_sum", shape((16, 1920)), [VM] * 4, out_received, after=[second_kv])
    out_pieces = share_quarter(out_quarter)

    window_scratch = [pltpu.VMEM((3 * rows, 256), BF16), pltpu.VMEM((256, 3 * rows), BF16)]
    q_rot, num, den = call(
        attend_near_kernel,
        "attend_near",
        (shape((cols, rows)), shape((cols, rows), F32), shape((8, rows), F32)),
        [SM] + [VM] * 13,
        [meta, first_q, second_q, *own_kv, *kv_prev, low, low_prev, ups, q_gain, k_gain, cosine, sine],
        window_scratch,
    )
    attended = call(
        attend_far_kernel,
        "attend_far",
        shape((cols + 64, rows)),
        [SM] + [VM] * 14,
        [meta, q_rot, num, den, *kv_prev2, low_prev2, ups, k_gain, cosine, sine, *out_pieces],
        window_scratch + [pltpu.VMEM((4, 16, 1920), BF16)],
    )

    att_far = across(attended)
    att_core = core(attended)
    att_far_core = core(att_far)
    out_weights = output_matrix.T
    out_scratch = [pltpu.VMEM((2, width, cols), BF16), pltpu.SemaphoreType.DMA((2, 2))]
    out_part, out_low = call(
        out_near_kernel,
        "out_near",
        (shape((width, rows), F32), shape((64, rows), F32)),
        [SM, VM, VM, FAR],
        [meta, attended, att_core, out_weights],
        out_scratch,
    )
    return call(
        out_far_kernel,
        "out_far",
        shape((width, rows)),
        [SM, VM, VM, FAR] + [VM] * 6,
        [meta, att_far, att_far_core, out_weights, out_part, out_low, *out_pieces],
        [pltpu.VMEM((4, 16, 1920), BF16)] + out_scratch,
    ).T


def plain_sizes(mesh):
    return mesh.shape["seq"] == 4 and mesh.shape["head"] == 2 and mesh.shape["rep"] == 2


def solution(mesh):
    return jax.shard_map(
        per_device if plain_sizes(mesh) else per_device_general,
        mesh=mesh,
        in_specs=(
            P(("groups", "seq"), ("head", "rep")),
            P(None, ("head", "rep")),
            P(None, "head"),
            P(None, "head"),
            P(None, ("head", "rep")),
            P(),
            P(),
            P("seq", ("head", "rep"), None),
            P("seq", None, ("head", "rep")),
            P("seq", None, None, "head"),
            P("seq", ("head", "rep"), None),
            P("seq", None, ("head", "rep")),
            P("groups"),
            P("groups"),
        ),
        out_specs=P(("groups", "seq"), ("head", "rep")),
        check_vma=False,
    )
```

```python
import functools
import math

import jax
import jax.numpy as jnp
from jax import lax
from jax.experimental import pallas as pl
from jax.experimental.pallas import tpu as pltpu
from jax.sharding import PartitionSpec as P

HEAD_SIZE = 128
ADAPTER_RANK = 32
KEY_WINDOW = 1024
BLOCK = 128


norm_epsilon = 1e-06
rope_base = 10000.0
score_scale = 168.0 ** (-0.5)
adapter_scale = 2.0


def shifted(value, axis, by):
    size = lax.axis_size(axis)
    pairs = [(i, i + by) for i in range(size) if 0 <= i + by < size]
    return lax.ppermute(value, axis, pairs)


def per_head_norm(values, scale_gain):
    mean_square = jnp.mean(values * values, axis=-1, keepdims=True)
    return values * lax.rsqrt(mean_square + norm_epsilon) * scale_gain


def rope_tables(positions, head_dim):
    half_dim = head_dim // 2
    frequency = jnp.power(rope_base, -jnp.arange(half_dim, dtype=jnp.float32) * 2.0 / head_dim)
    angles = positions.astype(jnp.float32)[:, None] * frequency[None, :]
    return (jnp.cos(angles), jnp.sin(angles))


def rotate_feature_pairs(values, cosine_table, sine_values):
    half_dim = values.shape[-1] // 2
    first_half = values[..., :half_dim]
    second_half = values[..., half_dim:]
    cosine_table = cosine_table[:, None, :]
    sine_values = sine_values[:, None, :]
    return jnp.concatenate(
        [
            first_half * cosine_table - second_half * sine_values,
            second_half * cosine_table + first_half * sine_values,
        ],
        axis=-1,
    )


def request_starts(block_requests, all_requests):
    earlier = (all_requests[None, :] < block_requests[:, None]).astype(jnp.int32)
    return jnp.sum(earlier, axis=1) * BLOCK


def per_device_general(
    tokens,
    query_matrix,
    key_matrix,
    value_matrix,
    output_matrix,
    query_gain,
    key_norm_gain,
    adapter_down,
    adapter_up_query,
    key_value_up_panels,
    adapter_out_down,
    adapter_out_up,
    request_of_block,
    adapter_of_request,
):
    tok_rows, width_part = tokens.shape
    query_cols = query_matrix.shape[1]
    key_cols = key_matrix.shape[1]
    query_heads = query_cols // HEAD_SIZE
    block_count = tok_rows // BLOCK
    all_blocks = request_of_block.shape[0]
    request_total = adapter_of_request.shape[0]
    seq_index = lax.axis_index("seq")
    rep_index = lax.axis_index("rep")
    first_row = seq_index * tok_rows
    own_requests = lax.dynamic_slice_in_dim(
        request_of_block, seq_index * block_count, block_count, 0
    )
    request_match = own_requests[:, None] == jnp.arange(request_total, dtype=jnp.int32)[None, :]
    own_adapters = jnp.sum(jnp.where(request_match, adapter_of_request[None, :], 0), axis=1)
    pool_part = (
        lax.all_gather(adapter_down, "seq", axis=0, tiled=True),
        lax.all_gather(adapter_up_query, "seq", axis=0, tiled=True),
        lax.all_gather(key_value_up_panels, "seq", axis=0, tiled=True),
        lax.all_gather(adapter_out_down, "seq", axis=0, tiled=True),
        lax.all_gather(adapter_out_up, "seq", axis=0, tiled=True),
    )
    held_count = pool_part[0].shape[0]
    select = (own_adapters[:, None] == jnp.arange(held_count, dtype=jnp.int32)[None, :]).astype(
        jnp.bfloat16
    )
    (
        picked_down_panels,
        picked_query_panels,
        picked_key_panels,
        chosen_out_down,
        picked_output_up,
    ) = tuple(
        (
            jnp.einsum(
                "bn,n...->b...", select, panel_part, preferred_element_type=jnp.float32
            ).astype(jnp.bfloat16)
            for panel_part in pool_part
        )
    )
    token_block_list = tokens.reshape(block_count, BLOCK, width_part)
    partial_low = jnp.einsum(
        "myj,mjc->myc", token_block_list, picked_down_panels, preferred_element_type=jnp.float32
    ).reshape(tok_rows, 3 * ADAPTER_RANK)
    reduced_rank_rows = (
        lax.psum(partial_low, ("head", "rep"))
        .astype(jnp.bfloat16)
        .reshape(block_count, BLOCK, 3 * ADAPTER_RANK)
    )
    feature_part = lax.all_gather(tokens, ("head", "rep"), axis=1, tiled=True)
    query_add = jnp.dot(feature_part, query_matrix, preferred_element_type=jnp.float32)
    key_add = jnp.dot(feature_part, key_matrix, preferred_element_type=jnp.float32)
    value_add = jnp.dot(feature_part, value_matrix, preferred_element_type=jnp.float32)
    query_linear = query_add
    key_linear = key_add
    value_linear = value_add
    query_linear = query_linear + adapter_scale * jnp.einsum(
        "tlq,tqo->tlo",
        reduced_rank_rows[..., :ADAPTER_RANK],
        picked_query_panels,
        preferred_element_type=jnp.float32,
    ).reshape(tok_rows, query_cols)
    key_linear = key_linear + adapter_scale * jnp.einsum(
        "tlq,tqo->tlo",
        reduced_rank_rows[..., ADAPTER_RANK : 2 * ADAPTER_RANK],
        picked_key_panels[:, 0],
        preferred_element_type=jnp.float32,
    ).reshape(tok_rows, key_cols)
    value_linear = value_linear + adapter_scale * jnp.einsum(
        "tlq,tqo->tlo",
        reduced_rank_rows[..., 2 * ADAPTER_RANK :],
        picked_key_panels[:, 1],
        preferred_element_type=jnp.float32,
    ).reshape(tok_rows, key_cols)
    key_full = key_linear.astype(jnp.bfloat16)
    value_full = value_linear.astype(jnp.bfloat16)
    key_heads = key_cols // HEAD_SIZE
    token_index = first_row + jnp.arange(tok_rows, dtype=jnp.int32)
    token_request = jnp.repeat(own_requests, BLOCK)
    token_start = jnp.repeat(request_starts(own_requests, request_of_block), BLOCK)
    cosine_table, sine_values = rope_tables(token_index - token_start, HEAD_SIZE)
    query_rows = (
        rotate_feature_pairs(
            per_head_norm(query_linear.reshape(tok_rows, query_heads, HEAD_SIZE), query_gain),
            cosine_table,
            sine_values,
        )
        * score_scale
    ).astype(jnp.bfloat16)
    rotated_keys = rotate_feature_pairs(
        per_head_norm(
            key_full.astype(jnp.float32).reshape(tok_rows, key_heads, HEAD_SIZE), key_norm_gain
        ),
        cosine_table,
        sine_values,
    ).astype(jnp.bfloat16)
    group_heads = max(query_heads // 2, 1)
    group_size = query_heads // group_heads
    head_first = rep_index * query_heads // 2
    keys_used = lax.dynamic_slice_in_dim(rotated_keys, head_first, group_heads, 1).reshape(
        tok_rows, group_heads * HEAD_SIZE
    )
    values_used = lax.dynamic_slice_in_dim(
        value_full.reshape(tok_rows, key_heads, HEAD_SIZE), head_first, group_heads, 1
    ).reshape(tok_rows, group_heads * HEAD_SIZE)
    query_groups = query_rows.reshape(tok_rows, group_heads, group_size, HEAD_SIZE)
    block_table = jnp.arange(all_blocks, dtype=jnp.int32)
    empty_state = (
        jnp.zeros((tok_rows, group_heads, group_size, HEAD_SIZE), jnp.float32),
        jnp.zeros((group_heads, group_size, tok_rows), jnp.float32),
    )
    reach_blocks = KEY_WINDOW // tok_rows
    stacked = jnp.stack((keys_used, values_used))
    earlier = []
    for step_back in range(reach_blocks, 0, -1):
        earlier.append(shifted(stacked, "seq", step_back))
    window_stack = jnp.concatenate(earlier + [stacked], axis=1)
    fold_state = empty_state
    offset = first_row - reach_blocks * tok_rows
    key_block = window_stack[0]
    value_block = window_stack[1]
    key_length = key_block.shape[0]
    step_length = math.gcd(key_length, 512)
    steps_count = key_length // step_length
    key_steps = key_block.reshape(steps_count, step_length, group_heads, HEAD_SIZE)
    value_steps = value_block.reshape(steps_count, step_length, group_heads, HEAD_SIZE)

    def one_step(carry_state, step_inputs):
        step_keys, step_values, step_index = step_inputs
        key_position = offset + step_index * step_length + jnp.arange(step_length, dtype=jnp.int32)
        key_block_id = jnp.clip(key_position, 0, all_blocks * BLOCK - 1) // BLOCK
        key_request = jnp.sum(
            jnp.where(key_block_id[:, None] == block_table[None, :], request_of_block[None, :], 0),
            axis=1,
        )
        distance = token_index[:, None] - key_position[None, :]
        allowed = (
            (key_position[None, :] >= 0)
            & (distance >= 0)
            & (distance < KEY_WINDOW)
            & (token_request[:, None] == key_request[None, :])
        )
        scores = jnp.einsum(
            "tcpd,kcd->cptk", query_groups, step_keys, preferred_element_type=jnp.float32
        )
        weights = jnp.where(allowed[None, None], jnp.exp(scores), 0.0)
        numerator, denominator = carry_state
        denominator = denominator + jnp.sum(weights, axis=-1)
        numerator = numerator + jnp.einsum(
            "cptk,kcd->tcpd",
            weights.astype(jnp.bfloat16),
            step_values,
            preferred_element_type=jnp.float32,
        )
        return ((numerator, denominator), None)

    fold_state, unused_out = lax.scan(
        one_step, fold_state, (key_steps, value_steps, jnp.arange(steps_count, dtype=jnp.int32))
    )
    numerator, denominator = fold_state
    attention_result = (
        (numerator / jnp.transpose(denominator, (2, 0, 1))[..., None])
        .astype(jnp.bfloat16)
        .reshape(tok_rows, query_cols)
    )
    output_zero = (
        jnp.zeros((tok_rows, width_part), jnp.float32),
        jnp.zeros((tok_rows, ADAPTER_RANK), jnp.float32),
    )
    projected_rows = jnp.dot(
        lax.all_gather(attention_result, ("head", "rep"), axis=1, tiled=True),
        output_matrix,
        preferred_element_type=jnp.float32,
    )
    projected_rows, lowered = (projected_rows, output_zero[1])
    local_low = jnp.einsum(
        "bkc,bcr->bkr",
        attention_result.reshape(block_count, BLOCK, query_cols),
        chosen_out_down,
        preferred_element_type=jnp.float32,
    ).reshape(tok_rows, ADAPTER_RANK)
    output_reduced_rank = lax.psum(local_low, ("head", "rep")).astype(jnp.bfloat16)
    result = projected_rows + adapter_scale * jnp.einsum(
        "zch,zhp->zcp",
        output_reduced_rank.reshape(block_count, BLOCK, ADAPTER_RANK),
        picked_output_up,
        preferred_element_type=jnp.float32,
    ).reshape(tok_rows, width_part)
    return result.astype(jnp.bfloat16)


F32 = jnp.float32
BF16 = jnp.bfloat16
VMEM_SMALL = 20 * 1024 * 1024
VMEM_LARGE = 56 * 1024 * 1024
SWAP = [(0, 1), (1, 0)]
SHARD_BLOCKS = 4
CHUNK = 256
CHUNK_BLOCKS = CHUNK // BLOCK
META_ADAPTER = 3
META_REQUEST = 5


def dot(a, b):
    return lax.dot_general(a, b, (((1,), (0,)), ((), ())), preferred_element_type=F32)


def dot_t(a, b):
    return lax.dot_general(a, b, (((0,), (0,)), ((), ())), preferred_element_type=F32)


VM = pl.BlockSpec(memory_space=pltpu.VMEM)
SM = pl.BlockSpec(memory_space=pltpu.SMEM)
HB = pl.BlockSpec(memory_space=pl.ANY)
FAR = pl.BlockSpec(memory_space=pltpu.HBM)


def in_hbm(value):
    return pltpu.with_memory_space_constraint(value, pltpu.HBM)


def shape(dims, dtype=BF16):
    return jax.ShapeDtypeStruct(dims, dtype)


def call(kernel, name, out_shape, in_specs, args, scratch=(), out_specs=None, grid=None, after=(), aliases=None):
    count = len(in_specs)

    def body(*refs):
        kernel(*refs[:count], *refs[count + len(after) :])

    outs = out_specs
    if outs is None:
        outs = VM if isinstance(out_shape, jax.ShapeDtypeStruct) else tuple(VM for _ in out_shape)
    more = dict(grid=grid) if grid else {}
    return pl.pallas_call(
        body,
        out_shape=out_shape,
        in_specs=list(in_specs) + [HB] * len(after),
        out_specs=outs,
        scratch_shapes=list(scratch),
        input_output_aliases=aliases or {},
        compiler_params=pltpu.CompilerParams(vmem_limit_bytes=VMEM_SMALL),
        cost_estimate=pl.CostEstimate(flops=1000, bytes_accessed=1000, transcendentals=0),
        name=name,
        **more,
    )(*[in_hbm(a) if spec is FAR else a for a, spec in zip(args, in_specs)], *after)


def picked(adapters, held):
    me = lax.axis_index("seq").astype(jnp.int32)
    chosen = []
    for step in range(4):
        quarter = jnp.bitwise_xor(me, step)
        slot = adapters[lax.div(quarter, 2)] - me * held
        here = jnp.logical_and(slot >= 0, slot < held)
        keep = jnp.where(here, 1.0, 0.0).astype(F32)
        chosen.append((jnp.clip(slot, 0, held - 1), keep, lax.rem(quarter, 2)))
    return chosen


def bring(sources, targets, sems):
    copies = [pltpu.make_async_copy(a, b, sems.at[i]) for i, (a, b) in enumerate(zip(sources, targets))]
    for copy in copies:
        copy.start()
    for copy in copies:
        copy.wait()


def pack_kernel(adapters, down_far, up_q_far, up_kv_far, *refs):
    quarters, (down, up_q, up_kv, sems) = refs[:4], refs[4:]
    bring((down_far, up_q_far, up_kv_far), (down, up_q, up_kv), sems)
    rep = lax.axis_index("rep").astype(jnp.int32)
    half = up_kv.shape[3] // 2
    cols = up_q.shape[2]
    width = down.shape[2]
    for (slot, keep, part), out in zip(picked(adapters, down.shape[0]), quarters):
        rows = pl.ds(pl.multiple_of(part * 48, 16), 48)
        ranks = pl.ds(pl.multiple_of(part * 16, 16), 16)
        out[0:48, :] = (down[slot, rows, :].astype(F32) * keep).astype(BF16)
        out[48:64, 0:cols] = (up_q[slot, ranks, :].astype(F32) * keep).astype(BF16)
        for which in range(2):
            both = up_kv[slot, which, ranks, :].astype(F32) * keep
            mine = jnp.where(rep == 0, both[:, :half], both[:, half:])
            out[48:64, cols + which * half : cols + (which + 1) * half] = mine.astype(BF16)
        out[48:64, 1024:width] = jnp.zeros((16, width - 1024), BF16)


def pack_out_kernel(adapters, out_down_far, out_up_far, out, out_down, out_up, sems):
    bring((out_down_far, out_up_far), (out_down, out_up), sems)
    width = out_up.shape[2]
    held = out_up.shape[0]
    for request in range(2):
        slot = adapters[request] - lax.axis_index("seq").astype(jnp.int32) * held
        here = jnp.logical_and(slot >= 0, slot < held)
        keep = jnp.where(here, 1.0, 0.0).astype(F32)
        slot = jnp.clip(slot, 0, held - 1)
        rows = slice(request * 32, (request + 1) * 32)
        out[rows, 0:width] = (out_up[slot].astype(F32) * keep).astype(BF16)
        out[rows, width:1408] = jnp.zeros((32, 1408 - width), BF16)
        out[rows, 1408:1920] = (out_down[slot].astype(F32) * keep).astype(BF16)


def add_kernel(a, b, out):
    out[...] = a[...] + b[...]


def sum_kernel(a, b, c, d, out):
    out[...] = a[...] + b[...] + c[...] + d[...]


def place_quarters(meta, quarters, panel):
    me = meta[0]
    low_side = me < 2
    at = (me, jnp.bitwise_xor(me, 1), jnp.where(low_side, 2, 1), jnp.where(low_side, 3, 0))
    for index, quarter in zip(at, quarters):
        panel[index] = quarter[...]


def low_kernel(meta, tokens, p0, p1, p2, p3, low_t, ups, panel):
    place_quarters(meta, (p0, p1, p2, p3), panel)
    down = jnp.concatenate([panel[j, 0:48, :] for j in range(4)], axis=0)
    both = dot(down, tokens[...])
    for b in range(SHARD_BLOCKS):
        request = meta[META_REQUEST + meta[0] * SHARD_BLOCKS + b]
        at = slice(b * BLOCK, (b + 1) * BLOCK)
        fa = jnp.where(request == 0, 1.0, 0.0).astype(F32)
        low_t[:, at] = both[0:96, at] * fa + both[96:192, at] * (1.0 - fa)
    ups[...] = jnp.concatenate([panel[j, 48:64, 0:1024] for j in range(4)], axis=0)


def weight_copies(meta, weights, buffers, sems, chip, width):
    half = weights[0].shape[1] // 2
    lane = pl.ds(pl.multiple_of(meta[1] * half, BLOCK), half)
    copies = []
    for i, (w, buf) in enumerate(zip(weights, buffers)):
        lanes = lane if i < 2 else slice(None)
        for n, part in enumerate((chip + meta[1], chip + 1 - meta[1])):
            rows = pl.ds(pl.multiple_of(part * width, 16), width)
            copies.append(pltpu.make_async_copy(w.at[rows, lanes], buf.at[n], sems.at[i, n]))
    return copies


WEIGHT_AT = (slice(0, 256), slice(256, 512), slice(512, 1024))


def near_kernel(meta, own, other, wq, wk, wv, out0, out1, fk, fv, fq, bk, bv, bq, sems, far_sems):
    weights = (wk, wv, wq)
    width = other.shape[0]
    copies = weight_copies(meta, weights, (bk, bv, bq), sems, meta[2] * 2, width)
    later = weight_copies(meta, weights, (fk, fv, fq), far_sems, (1 - meta[2]) * 2, width)
    for copy in copies:
        copy.start()
    for i, (at, buf) in enumerate(zip(WEIGHT_AT, (bk, bv, bq))):
        copies[2 * i].wait()
        copies[2 * i + 1].wait()
        if i == 1:
            for copy in later:
                copy.start()
        for c, out in enumerate((out0, out1)):
            tok = slice(c * CHUNK, (c + 1) * CHUNK)
            out[:, at] = dot_t(own[:, tok], buf[0]) + dot_t(other[:, tok], buf[1])
    for copy in later:
        copy.wait()


def far_kernel(part, own, other, wk, wv, wq, q_out, kv_out):
    for i, (at, w) in enumerate(zip(WEIGHT_AT, (wk, wv, wq))):
        turned = jnp.transpose(part[:, at] + dot_t(own[...], w[0]) + dot_t(other[...], w[1]))
        if i == 2:
            q_out[...] = turned
        else:
            kv_out[at, :] = turned.astype(BF16)


def block_request(meta, block):
    return meta[META_REQUEST + jnp.maximum(block, 0)]


def by_request(meta, low, first_block):
    flags = []
    for b in range(SHARD_BLOCKS):
        request = block_request(meta, first_block + b)
        flags.append(jnp.full((1, BLOCK), jnp.where(request == 0, 1.0, 0.0).astype(F32)))
    flag = jnp.concatenate(flags, axis=1)
    rows = low.astype(BF16).astype(F32)
    return jnp.concatenate([rows * flag, rows * (1.0 - flag)], axis=0).astype(BF16)


def norm_rotate(x, gain, cosine, sine):
    mean_square = jnp.mean(x * x, axis=0, keepdims=True)
    u = x * lax.rsqrt(mean_square + norm_epsilon) * gain
    a = u[0:64]
    b = u[64:128]
    return jnp.concatenate([a * cosine - b * sine, b * cosine + a * sine], axis=0)


def gain_rows(gain):
    return jnp.transpose(jnp.broadcast_to(gain[...], (HEAD_SIZE, HEAD_SIZE)))


def finish_keys(meta, chunks, low_k, low_v, ups, gain, cosine, sine, keys, values, first, blocks):
    base = (meta[0] - 2) * SHARD_BLOCKS + first
    k_term = dot_t(ups[:, 512:768], by_request(meta, low_k, base))
    v_term = dot_t(ups[:, 768:1024], by_request(meta, low_v, base))
    for b in blocks:
        at = slice((first + b) * BLOCK, (first + b + 1) * BLOCK)
        here = slice(b * BLOCK, (b + 1) * BLOCK)
        chunk = chunks[b // CHUNK_BLOCKS]
        lanes = slice(b % CHUNK_BLOCKS * BLOCK, (b % CHUNK_BLOCKS + 1) * BLOCK)
        for g in range(2):
            head = slice(g * HEAD_SIZE, (g + 1) * HEAD_SIZE)
            k = chunk[head, lanes].astype(F32) + adapter_scale * k_term[head, here]
            k = k.astype(BF16).astype(F32)
            turned = norm_rotate(k, gain, cosine[:, at], sine[:, at])
            keys[here, head] = jnp.transpose(turned).astype(BF16)
        values[:, here] = (chunk[256:512, lanes].astype(F32) + adapter_scale * v_term[:, here]).astype(BF16)


def attend(meta, q_rot, keys, values, c, g, first, low_block, high_block):
    rows = slice(c * BLOCK, (c + 1) * BLOCK)
    heads = [slice((2 * g + h) * HEAD_SIZE, (2 * g + h + 1) * HEAD_SIZE) for h in range(2)]
    q = jnp.concatenate([q_rot[head, rows] for head in heads], axis=1)
    base = (meta[0] - 2) * SHARD_BLOCKS
    mine = block_request(meta, base + 8 + c)
    head = slice(g * HEAD_SIZE, (g + 1) * HEAD_SIZE)
    at = slice(low_block * BLOCK, (high_block + 1) * BLOCK)
    scores = dot(keys[at, head], q)
    key = lax.broadcasted_iota(jnp.int32, (BLOCK, 2 * BLOCK), 0)
    query = jnp.bitwise_and(lax.broadcasted_iota(jnp.int32, (BLOCK, 2 * BLOCK), 1), BLOCK - 1)
    den = jnp.zeros((BLOCK, 2 * BLOCK), F32)
    pieces = []
    for j in range(low_block, high_block + 1):
        block = base + first + j
        ok = jnp.logical_and(block >= 0, block_request(meta, block) == mine)
        piece = jnp.exp(scores[(j - low_block) * BLOCK : (j - low_block + 1) * BLOCK])
        piece = piece * jnp.where(ok, 1.0, 0.0).astype(F32)
        if first + j == c + 8:
            piece = jnp.where(query >= key, piece, 0.0)
        if first + j == c:
            piece = jnp.where(query < key, piece, 0.0)
        den = den + piece
        pieces.append(piece.astype(BF16))
    num = dot(values[head, at], jnp.concatenate(pieces, axis=0))
    return num, jnp.sum(den, axis=0, keepdims=True)


def attend_own_kernel(
    meta, q0, q1, o0, o1, low, ups, q_gain, k_gain, cosine, sine, weights,
    q_rot, num_out, den_out, weights_out, keys, values, sem,
):
    fetch = pltpu.make_async_copy(weights, weights_out, sem)
    fetch.start()
    finish_keys(
        meta, (o0, o1), low[32:64, :], low[64:96, :], ups, gain_rows(k_gain), cosine, sine, keys, values, 8, range(4)
    )
    gain = gain_rows(q_gain)
    q_term = dot_t(ups[:, 0:512], by_request(meta, low[0:32, :], meta[0] * SHARD_BLOCKS))
    for c in range(SHARD_BLOCKS):
        q = (q0, q1)[c // CHUNK_BLOCKS]
        lanes = slice(c % CHUNK_BLOCKS * BLOCK, (c % CHUNK_BLOCKS + 1) * BLOCK)
        rows = slice(c * BLOCK, (c + 1) * BLOCK)
        at = slice((8 + c) * BLOCK, (9 + c) * BLOCK)
        for h in range(4):
            head = slice(h * HEAD_SIZE, (h + 1) * HEAD_SIZE)
            x = q[head, lanes] + adapter_scale * q_term[head, rows]
            q_rot[head, rows] = (norm_rotate(x, gain, cosine[:, at], sine[:, at]) * score_scale).astype(BF16)
    for g in range(2):
        for c in range(SHARD_BLOCKS):
            rows = slice(c * BLOCK, (c + 1) * BLOCK)
            num, den = attend(meta, q_rot, keys, values, c, g, 8, 0, c)
            for h in range(2):
                n = 2 * g + h
                part = slice(h * BLOCK, (h + 1) * BLOCK)
                num_out[n * HEAD_SIZE : (n + 1) * HEAD_SIZE, rows] = num[:, part]
                den_out[n : n + 1, rows] = den[:, part]
    fetch.wait()


def attend_prev_kernel(
    meta, q_rot, num_in, den_in, h0, h1, low_h, ups, k_gain, cosine, sine, num_out, den_out, keys, values
):
    finish_keys(
        meta, (h0, h1), low_h[0:32, :], low_h[32:64, :], ups, gain_rows(k_gain), cosine, sine, keys, values, 4, range(4)
    )
    for g in range(2):
        for c in range(SHARD_BLOCKS):
            rows = slice(c * BLOCK, (c + 1) * BLOCK)
            num, den = attend(meta, q_rot, keys, values, c, g, 4, 0, 3)
            for h in range(2):
                n = 2 * g + h
                part = slice(h * BLOCK, (h + 1) * BLOCK)
                head = slice(n * HEAD_SIZE, (n + 1) * HEAD_SIZE)
                num_out[head, rows] = num_in[head, rows] + num[:, part]
                den_out[n : n + 1, rows] = den_in[n : n + 1, rows] + den[:, part]


def attend_far_kernel(chunk, meta, q_rot, num_in, den_in, *refs):
    count = CHUNK_BLOCKS - chunk
    kept, (low_h, ups, k_gain, cosine, sine, out, keys, values) = refs[:count], refs[count:]
    blocks = range(chunk * CHUNK_BLOCKS, SHARD_BLOCKS)
    finish_keys(
        meta, (None,) * chunk + tuple(kept), low_h[0:32, :], low_h[32:64, :], ups, gain_rows(k_gain), cosine, sine,
        keys, values, 0, blocks,
    )
    for g in range(2):
        for c in range(chunk * CHUNK_BLOCKS, (chunk + 1) * CHUNK_BLOCKS):
            rows = slice(c * BLOCK, (c + 1) * BLOCK)
            here = slice(c % CHUNK_BLOCKS * BLOCK, (c % CHUNK_BLOCKS + 1) * BLOCK)
            num, den = attend(meta, q_rot, keys, values, c, g, 0, c, 3)
            for h in range(2):
                n = 2 * g + h
                part = slice(h * BLOCK, (h + 1) * BLOCK)
                head = slice(n * HEAD_SIZE, (n + 1) * HEAD_SIZE)
                total = den_in[n : n + 1, rows] + den[:, part]
                out[head, here] = ((num_in[head, rows] + num[:, part]) / total).astype(BF16)


def request_flag(meta):
    flags = []
    for b in range(SHARD_BLOCKS):
        request = block_request(meta, meta[0] * SHARD_BLOCKS + b)
        flags.append(jnp.full((1, BLOCK), jnp.where(request == 0, 1.0, 0.0).astype(F32)))
    return jnp.concatenate(flags, axis=1)


def out_low_kernel(meta, att0, att1, panel_a, panel_b, low):
    down = panel_a[:, 1408:1920] + panel_b[:, 1408:1920]
    both = jnp.concatenate([dot(down, att0[...]), dot(down, att1[...])], axis=1)
    flag = request_flag(meta)
    low[...] = both[0:32] * flag + both[32:64] * (1.0 - flag)


def part_lanes(meta, chip, cols):
    return [pl.ds(pl.multiple_of(p * cols, BLOCK), cols) for p in (chip + meta[1], chip + 1 - meta[1])]


def out_near_kernel(meta, own, other, w, part):
    first, second = part_lanes(meta, meta[2] * 2, own.shape[0])
    part[...] = dot(w[:, first], own[...]) + dot(w[:, second], other[...])


def out_far_kernel(chunk, meta, own, other, w, part, low, panel_a, panel_b, *refs):
    out = refs[-1]
    tok = slice(chunk * CHUNK, (chunk + 1) * CHUNK)
    lows = low[:, tok].astype(BF16).astype(F32)
    flag = request_flag(meta)[:, tok]
    chosen = jnp.concatenate([lows * flag, lows * (1.0 - flag)], axis=0).astype(BF16)
    up = panel_a[:, 0 : w.shape[0]] + panel_b[:, 0 : w.shape[0]]
    first, second = part_lanes(meta, (1 - meta[2]) * 2, own.shape[0])
    total = part[...] + adapter_scale * dot_t(up, chosen)
    out[...] = (total + dot(w[:, first], own[...]) + dot(w[:, second], other[...])).astype(BF16)


def exchange_quarters(quarters):
    return [quarters[0]] + [lax.ppermute(quarters[s], "seq", [(j, j ^ s) for j in range(4)]) for s in (1, 2, 3)]


def share_quarter(total):
    beside = lax.ppermute(total, "seq", [(j, j ^ 1) for j in range(4)])
    middle = [(1, 2), (2, 1)]
    return [total, beside, lax.ppermute(total, "seq", middle), lax.ppermute(beside, "seq", middle)]


def per_device(
    tokens,
    query_matrix,
    key_matrix,
    value_matrix,
    output_matrix,
    query_gain,
    key_norm_gain,
    adapter_down,
    adapter_up_query,
    key_value_up_panels,
    adapter_out_down,
    adapter_out_up,
    request_of_block,
    adapter_of_request,
):
    rows, width = tokens.shape
    cols = query_matrix.shape[1]
    seq, rep, head = (lax.axis_index(name).astype(jnp.int32) for name in ("seq", "rep", "head"))
    meta = jnp.concatenate([jnp.stack([seq, rep, head]), adapter_of_request, request_of_block])
    tokens = tokens.T

    def across(value):
        return lax.ppermute(value, "head", SWAP)

    def core(value):
        return lax.ppermute(value, "rep", SWAP)

    def up(value, by=1):
        return lax.ppermute(value, "seq", [(i, (i + by) % 4) for i in range(4)])

    def after(value, *others):
        return lax.optimization_barrier((value, *others))[0]

    far_own = across(tokens)
    near_other = core(tokens)

    def swapped(value, by):
        return lax.ppermute(value, "seq", [(j, j ^ by) for j in range(4)])

    def pack(kernel, name, result, pools, order):
        return call(
            kernel,
            name,
            result,
            [SM] + [FAR] * len(pools),
            [adapter_of_request, *pools],
            [pltpu.VMEM(pool.shape, BF16) for pool in pools] + [pltpu.SemaphoreType.DMA((len(pools),))],
            after=order,
        )

    pools = [jnp.swapaxes(adapter_down, 1, 2), adapter_up_query, key_value_up_panels]
    quarters = pack(pack_kernel, "pack", (shape((64, width)),) * 4, pools, [])
    received = exchange_quarters(quarters)
    out_pools = [jnp.swapaxes(adapter_out_down, 1, 2), adapter_out_up]
    out_panel = pack(pack_out_kernel, "pack_out", shape((64, 1920)), out_pools, [quarters[0]])
    out_beside = swapped(out_panel, 1)

    chunks = rows // CHUNK
    weights = [query_matrix, key_matrix, value_matrix]
    weight_scratch = [
        pltpu.VMEM((2, width, 256), BF16),
        pltpu.VMEM((2, width, 256), BF16),
        pltpu.VMEM((2, width, cols), BF16),
        pltpu.SemaphoreType.DMA((3, 2)),
    ]
    weight_shapes = [(2, width, 256), (2, width, 256), (2, width, cols)]
    near0, near1, *far_weights = call(
        near_kernel,
        "near",
        (shape((CHUNK, 1024), F32),) * chunks + tuple(shape(dims) for dims in weight_shapes),
        [SM, VM, VM, FAR, FAR, FAR],
        [meta, tokens, near_other, *weights],
        [pltpu.VMEM(dims, BF16) for dims in weight_shapes] + [pltpu.SemaphoreType.DMA((3, 2))] * 2,
        after=[out_panel],
    )
    near = [near0, near1]

    def project(c, prior):
        mine = pl.BlockSpec((width, CHUNK), lambda i: (0, c))
        return call(
            far_kernel,
            "far",
            (shape((cols, CHUNK), F32), shape((512, CHUNK))),
            [VM, mine, mine, VM, VM, VM],
            [near[c], far_own, far_other, *far_weights],
            grid=(1,),
            after=[prior],
        )

    all_blocks = request_of_block.shape[0]
    window = jnp.arange(3 * rows, dtype=jnp.int32) + (seq - 2) * rows
    window = jnp.clip(window, 0, all_blocks * BLOCK - 1)
    second_start = jnp.sum((request_of_block < 1).astype(jnp.int32)) * BLOCK
    position = jnp.where(window >= second_start, window - second_start, window)
    half_dim = HEAD_SIZE // 2
    frequency = jnp.power(rope_base, -jnp.arange(half_dim, dtype=F32) * 2.0 / HEAD_SIZE)
    angles = frequency[:, None] * position.astype(F32)[None, :]
    cosine, sine = jnp.cos(angles), jnp.sin(angles)
    q_gain = query_gain.reshape(1, HEAD_SIZE)
    k_gain = key_norm_gain.reshape(1, HEAD_SIZE)

    quarter = call(sum_kernel, "sum", shape((64, width)), [VM] * 4, received, after=[near[0], cosine, sine])
    pieces = share_quarter(quarter)
    far_other = core(after(far_own, pieces[1], pieces[2]))
    late_q, late_kv = project(1, pieces[1])
    partial_low, ups = call(
        low_kernel,
        "low",
        (shape((96, rows), F32), shape((64, 1024))),
        [SM] + [VM] * 5,
        [meta, tokens, *pieces],
        [pltpu.VMEM((4, 64, width), BF16)],
        after=[late_kv],
    )
    chip_low = partial_low + core(partial_low)
    low = chip_low + across(chip_low)
    early_q, early_kv = project(0, chip_low)

    prev_late, prev_early = up(late_kv), up(early_kv)
    low_kv = low[32:96].astype(BF16)
    low_prev = up(low_kv)
    low_prev2 = up(low_kv, 2)
    prev2_late = up(after(prev_late, early_kv))

    shard_scratch = [pltpu.VMEM((rows, 256), BF16), pltpu.VMEM((256, rows), BF16)]
    sums = (shape((cols, rows), F32), shape((8, rows), F32))
    q_rot, num, den, out_weights = call(
        attend_own_kernel,
        "attend_own",
        (shape((cols, rows)), *sums, shape(output_matrix.T.shape)),
        [SM] + [VM] * 10 + [FAR],
        [meta, early_q, late_q, early_kv, late_kv, low, ups, q_gain, k_gain, cosine, sine, output_matrix.T],
        shard_scratch + [pltpu.SemaphoreType.DMA],
    )
    prev2_early = up(after(prev_early, low_prev, low_prev2, num))
    num, den = call(
        attend_prev_kernel,
        "attend_prev",
        sums,
        [SM] + [VM] * 10,
        [meta, q_rot, num, den, prev_early, prev_late, low_prev, ups, k_gain, cosine, sine],
        shard_scratch,
    )

    def attend_far(chunk, kept, order):
        return call(
            functools.partial(attend_far_kernel, chunk),
            "attend_far",
            shape((cols, CHUNK)),
            [SM] + [VM] * (8 + len(kept)),
            [meta, q_rot, num, den, *kept, low_prev2, ups, k_gain, cosine, sine],
            shard_scratch,
            after=order,
        )

    att_late = attend_far(1, [prev2_late], [])
    att_early = attend_far(0, [prev2_early, prev2_late], [att_late])

    out_pair = call(add_kernel, "out_add", shape((64, 1920)), [VM] * 2, [out_panel, out_beside], after=[early_kv])
    out_rest = swapped(out_pair, 2)
    out_low = call(
        out_low_kernel,
        "out_low",
        shape((32, rows), F32),
        [SM] + [VM] * 4,
        [meta, att_early, att_late, out_pair, out_rest],
    )
    out_low = out_low + core(out_low)
    out_low = out_low + across(out_low)

    result = []
    for chunk, att in ((1, att_late), (0, att_early)):
        att_far = across(att)
        part = call(
            out_near_kernel,
            "out_near",
            shape((width, CHUNK), F32),
            [SM] + [VM] * 3,
            [meta, att, core(att), out_weights],
            after=[att_early],
        )
        result = [
            call(
                functools.partial(out_far_kernel, chunk),
                "out_far",
                shape((width, rows)),
                [SM] + [VM] * 7 + [HB] * len(result),
                [meta, att_far, core(att_far), out_weights, part, out_low, out_pair, out_rest, *result],
                out_specs=pl.BlockSpec((width, CHUNK), lambda i, chunk=chunk: (0, chunk)),
                grid=(1,),
                aliases={8: 0} if result else {},
            )
        ]
    return result[0].T


def plain_sizes(mesh):
    return mesh.shape["seq"] == 4 and mesh.shape["head"] == 2 and mesh.shape["rep"] == 2


def solution(mesh):
    return jax.shard_map(
        per_device if plain_sizes(mesh) else per_device_general,
        mesh=mesh,
        in_specs=(
            P(("groups", "seq"), ("head", "rep")),
            P(None, ("head", "rep")),
            P(None, "head"),
            P(None, "head"),
            P(None, ("head", "rep")),
            P(),
            P(),
            P("seq", ("head", "rep"), None),
            P("seq", None, ("head", "rep")),
            P("seq", None, None, "head"),
            P("seq", ("head", "rep"), None),
            P("seq", None, ("head", "rep")),
            P("groups"),
            P("groups"),
        ),
        out_specs=P(("groups", "seq"), ("head", "rep")),
        check_vma=False,
    )
```

```python
import functools
import math

import jax
import jax.numpy as jnp
from jax import lax
from jax.experimental import pallas as pl
from jax.experimental.pallas import tpu as pltpu
from jax.sharding import PartitionSpec as P

HEAD_SIZE = 128
ADAPTER_RANK = 32
KEY_WINDOW = 1024
BLOCK = 128


norm_epsilon = 1e-06
rope_base = 10000.0
score_scale = 168.0 ** (-0.5)
adapter_scale = 2.0


def shifted(value, axis, by):
    size = lax.axis_size(axis)
    pairs = [(i, i + by) for i in range(size) if 0 <= i + by < size]
    return lax.ppermute(value, axis, pairs)


def per_head_norm(values, scale_gain):
    mean_square = jnp.mean(values * values, axis=-1, keepdims=True)
    return values * lax.rsqrt(mean_square + norm_epsilon) * scale_gain


def rope_tables(positions, head_dim):
    half_dim = head_dim // 2
    frequency = jnp.power(rope_base, -jnp.arange(half_dim, dtype=jnp.float32) * 2.0 / head_dim)
    angles = positions.astype(jnp.float32)[:, None] * frequency[None, :]
    return (jnp.cos(angles), jnp.sin(angles))


def rotate_feature_pairs(values, cosine_table, sine_values):
    half_dim = values.shape[-1] // 2
    first_half = values[..., :half_dim]
    second_half = values[..., half_dim:]
    cosine_table = cosine_table[:, None, :]
    sine_values = sine_values[:, None, :]
    return jnp.concatenate(
        [
            first_half * cosine_table - second_half * sine_values,
            second_half * cosine_table + first_half * sine_values,
        ],
        axis=-1,
    )


def request_starts(block_requests, all_requests):
    earlier = (all_requests[None, :] < block_requests[:, None]).astype(jnp.int32)
    return jnp.sum(earlier, axis=1) * BLOCK


def per_device_general(
    tokens,
    query_matrix,
    key_matrix,
    value_matrix,
    output_matrix,
    query_gain,
    key_norm_gain,
    adapter_down,
    adapter_up_query,
    key_value_up_panels,
    adapter_out_down,
    adapter_out_up,
    request_of_block,
    adapter_of_request,
):
    tok_rows, width_part = tokens.shape
    query_cols = query_matrix.shape[1]
    key_cols = key_matrix.shape[1]
    query_heads = query_cols // HEAD_SIZE
    block_count = tok_rows // BLOCK
    all_blocks = request_of_block.shape[0]
    request_total = adapter_of_request.shape[0]
    seq_index = lax.axis_index("seq")
    rep_index = lax.axis_index("rep")
    first_row = seq_index * tok_rows
    own_requests = lax.dynamic_slice_in_dim(
        request_of_block, seq_index * block_count, block_count, 0
    )
    request_match = own_requests[:, None] == jnp.arange(request_total, dtype=jnp.int32)[None, :]
    own_adapters = jnp.sum(jnp.where(request_match, adapter_of_request[None, :], 0), axis=1)
    pool_part = (
        lax.all_gather(adapter_down, "seq", axis=0, tiled=True),
        lax.all_gather(adapter_up_query, "seq", axis=0, tiled=True),
        lax.all_gather(key_value_up_panels, "seq", axis=0, tiled=True),
        lax.all_gather(adapter_out_down, "seq", axis=0, tiled=True),
        lax.all_gather(adapter_out_up, "seq", axis=0, tiled=True),
    )
    held_count = pool_part[0].shape[0]
    select = (own_adapters[:, None] == jnp.arange(held_count, dtype=jnp.int32)[None, :]).astype(
        jnp.bfloat16
    )
    (
        picked_down_panels,
        picked_query_panels,
        picked_key_panels,
        chosen_out_down,
        picked_output_up,
    ) = tuple(
        (
            jnp.einsum(
                "bn,n...->b...", select, panel_part, preferred_element_type=jnp.float32
            ).astype(jnp.bfloat16)
            for panel_part in pool_part
        )
    )
    token_block_list = tokens.reshape(block_count, BLOCK, width_part)
    partial_low = jnp.einsum(
        "myj,mjc->myc", token_block_list, picked_down_panels, preferred_element_type=jnp.float32
    ).reshape(tok_rows, 3 * ADAPTER_RANK)
    reduced_rank_rows = (
        lax.psum(partial_low, ("head", "rep"))
        .astype(jnp.bfloat16)
        .reshape(block_count, BLOCK, 3 * ADAPTER_RANK)
    )
    feature_part = lax.all_gather(tokens, ("head", "rep"), axis=1, tiled=True)
    query_add = jnp.dot(feature_part, query_matrix, preferred_element_type=jnp.float32)
    key_add = jnp.dot(feature_part, key_matrix, preferred_element_type=jnp.float32)
    value_add = jnp.dot(feature_part, value_matrix, preferred_element_type=jnp.float32)
    query_linear = query_add
    key_linear = key_add
    value_linear = value_add
    query_linear = query_linear + adapter_scale * jnp.einsum(
        "tlq,tqo->tlo",
        reduced_rank_rows[..., :ADAPTER_RANK],
        picked_query_panels,
        preferred_element_type=jnp.float32,
    ).reshape(tok_rows, query_cols)
    key_linear = key_linear + adapter_scale * jnp.einsum(
        "tlq,tqo->tlo",
        reduced_rank_rows[..., ADAPTER_RANK : 2 * ADAPTER_RANK],
        picked_key_panels[:, 0],
        preferred_element_type=jnp.float32,
    ).reshape(tok_rows, key_cols)
    value_linear = value_linear + adapter_scale * jnp.einsum(
        "tlq,tqo->tlo",
        reduced_rank_rows[..., 2 * ADAPTER_RANK :],
        picked_key_panels[:, 1],
        preferred_element_type=jnp.float32,
    ).reshape(tok_rows, key_cols)
    key_full = key_linear.astype(jnp.bfloat16)
    value_full = value_linear.astype(jnp.bfloat16)
    key_heads = key_cols // HEAD_SIZE
    token_index = first_row + jnp.arange(tok_rows, dtype=jnp.int32)
    token_request = jnp.repeat(own_requests, BLOCK)
    token_start = jnp.repeat(request_starts(own_requests, request_of_block), BLOCK)
    cosine_table, sine_values = rope_tables(token_index - token_start, HEAD_SIZE)
    query_rows = (
        rotate_feature_pairs(
            per_head_norm(query_linear.reshape(tok_rows, query_heads, HEAD_SIZE), query_gain),
            cosine_table,
            sine_values,
        )
        * score_scale
    ).astype(jnp.bfloat16)
    rotated_keys = rotate_feature_pairs(
        per_head_norm(
            key_full.astype(jnp.float32).reshape(tok_rows, key_heads, HEAD_SIZE), key_norm_gain
        ),
        cosine_table,
        sine_values,
    ).astype(jnp.bfloat16)
    group_heads = max(query_heads // 2, 1)
    group_size = query_heads // group_heads
    head_first = rep_index * query_heads // 2
    keys_used = lax.dynamic_slice_in_dim(rotated_keys, head_first, group_heads, 1).reshape(
        tok_rows, group_heads * HEAD_SIZE
    )
    values_used = lax.dynamic_slice_in_dim(
        value_full.reshape(tok_rows, key_heads, HEAD_SIZE), head_first, group_heads, 1
    ).reshape(tok_rows, group_heads * HEAD_SIZE)
    query_groups = query_rows.reshape(tok_rows, group_heads, group_size, HEAD_SIZE)
    block_table = jnp.arange(all_blocks, dtype=jnp.int32)
    empty_state = (
        jnp.zeros((tok_rows, group_heads, group_size, HEAD_SIZE), jnp.float32),
        jnp.zeros((group_heads, group_size, tok_rows), jnp.float32),
    )
    reach_blocks = KEY_WINDOW // tok_rows
    stacked = jnp.stack((keys_used, values_used))
    earlier = []
    for step_back in range(reach_blocks, 0, -1):
        earlier.append(shifted(stacked, "seq", step_back))
    window_stack = jnp.concatenate(earlier + [stacked], axis=1)
    fold_state = empty_state
    offset = first_row - reach_blocks * tok_rows
    key_block = window_stack[0]
    value_block = window_stack[1]
    key_length = key_block.shape[0]
    step_length = math.gcd(key_length, 512)
    steps_count = key_length // step_length
    key_steps = key_block.reshape(steps_count, step_length, group_heads, HEAD_SIZE)
    value_steps = value_block.reshape(steps_count, step_length, group_heads, HEAD_SIZE)

    def one_step(carry_state, step_inputs):
        step_keys, step_values, step_index = step_inputs
        key_position = offset + step_index * step_length + jnp.arange(step_length, dtype=jnp.int32)
        key_block_id = jnp.clip(key_position, 0, all_blocks * BLOCK - 1) // BLOCK
        key_request = jnp.sum(
            jnp.where(key_block_id[:, None] == block_table[None, :], request_of_block[None, :], 0),
            axis=1,
        )
        distance = token_index[:, None] - key_position[None, :]
        allowed = (
            (key_position[None, :] >= 0)
            & (distance >= 0)
            & (distance < KEY_WINDOW)
            & (token_request[:, None] == key_request[None, :])
        )
        scores = jnp.einsum(
            "tcpd,kcd->cptk", query_groups, step_keys, preferred_element_type=jnp.float32
        )
        weights = jnp.where(allowed[None, None], jnp.exp(scores), 0.0)
        numerator, denominator = carry_state
        denominator = denominator + jnp.sum(weights, axis=-1)
        numerator = numerator + jnp.einsum(
            "cptk,kcd->tcpd",
            weights.astype(jnp.bfloat16),
            step_values,
            preferred_element_type=jnp.float32,
        )
        return ((numerator, denominator), None)

    fold_state, unused_out = lax.scan(
        one_step, fold_state, (key_steps, value_steps, jnp.arange(steps_count, dtype=jnp.int32))
    )
    numerator, denominator = fold_state
    attention_result = (
        (numerator / jnp.transpose(denominator, (2, 0, 1))[..., None])
        .astype(jnp.bfloat16)
        .reshape(tok_rows, query_cols)
    )
    output_zero = (
        jnp.zeros((tok_rows, width_part), jnp.float32),
        jnp.zeros((tok_rows, ADAPTER_RANK), jnp.float32),
    )
    projected_rows = jnp.dot(
        lax.all_gather(attention_result, ("head", "rep"), axis=1, tiled=True),
        output_matrix,
        preferred_element_type=jnp.float32,
    )
    projected_rows, lowered = (projected_rows, output_zero[1])
    local_low = jnp.einsum(
        "bkc,bcr->bkr",
        attention_result.reshape(block_count, BLOCK, query_cols),
        chosen_out_down,
        preferred_element_type=jnp.float32,
    ).reshape(tok_rows, ADAPTER_RANK)
    output_reduced_rank = lax.psum(local_low, ("head", "rep")).astype(jnp.bfloat16)
    result = projected_rows + adapter_scale * jnp.einsum(
        "zch,zhp->zcp",
        output_reduced_rank.reshape(block_count, BLOCK, ADAPTER_RANK),
        picked_output_up,
        preferred_element_type=jnp.float32,
    ).reshape(tok_rows, width_part)
    return result.astype(jnp.bfloat16)


F32 = jnp.float32
BF16 = jnp.bfloat16
VMEM_SMALL = 20 * 1024 * 1024
VMEM_LARGE = 56 * 1024 * 1024
SWAP = [(0, 1), (1, 0)]
SHARD_BLOCKS = 4
CHUNK = 256
CHUNK_BLOCKS = CHUNK // BLOCK
META_ADAPTER = 3
META_REQUEST = 5


def dot(a, b):
    return lax.dot_general(a, b, (((1,), (0,)), ((), ())), preferred_element_type=F32)


def dot_t(a, b):
    return lax.dot_general(a, b, (((0,), (0,)), ((), ())), preferred_element_type=F32)


VM = pl.BlockSpec(memory_space=pltpu.VMEM)
SM = pl.BlockSpec(memory_space=pltpu.SMEM)
HB = pl.BlockSpec(memory_space=pl.ANY)
FAR = pl.BlockSpec(memory_space=pltpu.HBM)


def in_hbm(value):
    return pltpu.with_memory_space_constraint(value, pltpu.HBM)


def shape(dims, dtype=BF16):
    return jax.ShapeDtypeStruct(dims, dtype)


def call(kernel, name, out_shape, in_specs, args, scratch=(), out_specs=None, grid=None, after=(), aliases=None):
    count = len(in_specs)

    def body(*refs):
        kernel(*refs[:count], *refs[count + len(after) :])

    outs = out_specs
    if outs is None:
        outs = VM if isinstance(out_shape, jax.ShapeDtypeStruct) else tuple(VM for _ in out_shape)
    more = dict(grid=grid) if grid else {}
    return pl.pallas_call(
        body,
        out_shape=out_shape,
        in_specs=list(in_specs) + [HB] * len(after),
        out_specs=outs,
        scratch_shapes=list(scratch),
        input_output_aliases=aliases or {},
        compiler_params=pltpu.CompilerParams(vmem_limit_bytes=VMEM_SMALL),
        cost_estimate=pl.CostEstimate(flops=1000, bytes_accessed=1000, transcendentals=0),
        name=name,
        **more,
    )(*[in_hbm(a) if spec is FAR else a for a, spec in zip(args, in_specs)], *after)


def picked(adapters, held):
    me = lax.axis_index("seq").astype(jnp.int32)
    chosen = []
    for step in range(4):
        quarter = jnp.bitwise_xor(me, step)
        slot = adapters[lax.div(quarter, 2)] - me * held
        here = jnp.logical_and(slot >= 0, slot < held)
        keep = jnp.where(here, 1.0, 0.0).astype(F32)
        chosen.append((jnp.clip(slot, 0, held - 1), keep, lax.rem(quarter, 2)))
    return chosen


def bring(sources, targets, sems):
    copies = [pltpu.make_async_copy(a, b, sems.at[i]) for i, (a, b) in enumerate(zip(sources, targets))]
    for copy in copies:
        copy.start()
    for copy in copies:
        copy.wait()


def pack_kernel(adapters, down_far, up_q_far, up_kv_far, *refs):
    quarters, (down, up_q, up_kv, sems) = refs[:4], refs[4:]
    bring((down_far, up_q_far, up_kv_far), (down, up_q, up_kv), sems)
    rep = lax.axis_index("rep").astype(jnp.int32)
    half = up_kv.shape[3] // 2
    cols = up_q.shape[2]
    width = down.shape[2]
    for (slot, keep, part), out in zip(picked(adapters, down.shape[0]), quarters):
        rows = pl.ds(pl.multiple_of(part * 48, 16), 48)
        ranks = pl.ds(pl.multiple_of(part * 16, 16), 16)
        out[0:48, :] = (down[slot, rows, :].astype(F32) * keep).astype(BF16)
        out[48:64, 0:cols] = (up_q[slot, ranks, :].astype(F32) * keep).astype(BF16)
        for which in range(2):
            both = up_kv[slot, which, ranks, :].astype(F32) * keep
            mine = jnp.where(rep == 0, both[:, :half], both[:, half:])
            out[48:64, cols + which * half : cols + (which + 1) * half] = mine.astype(BF16)
        out[48:64, 1024:width] = jnp.zeros((16, width - 1024), BF16)


def pack_out_kernel(adapters, out_down_far, out_up_far, out, out_down, out_up, sems):
    bring((out_down_far, out_up_far), (out_down, out_up), sems)
    width = out_up.shape[2]
    held = out_up.shape[0]
    for request in range(2):
        slot = adapters[request] - lax.axis_index("seq").astype(jnp.int32) * held
        here = jnp.logical_and(slot >= 0, slot < held)
        keep = jnp.where(here, 1.0, 0.0).astype(F32)
        slot = jnp.clip(slot, 0, held - 1)
        rows = slice(request * 32, (request + 1) * 32)
        out[rows, 0:width] = (out_up[slot].astype(F32) * keep).astype(BF16)
        out[rows, width:1408] = jnp.zeros((32, 1408 - width), BF16)
        out[rows, 1408:1920] = (out_down[slot].astype(F32) * keep).astype(BF16)


def add_kernel(a, b, out):
    out[...] = a[...] + b[...]


def sum_kernel(a, b, c, d, out):
    out[...] = a[...] + b[...] + c[...] + d[...]


def place_quarters(meta, quarters, panel):
    me = meta[0]
    low_side = me < 2
    at = (me, jnp.bitwise_xor(me, 1), jnp.where(low_side, 2, 1), jnp.where(low_side, 3, 0))
    for index, quarter in zip(at, quarters):
        panel[index] = quarter[...]


def low_kernel(meta, tokens, p0, p1, p2, p3, low_t, ups, panel):
    place_quarters(meta, (p0, p1, p2, p3), panel)
    down = jnp.concatenate([panel[j, 0:48, :] for j in range(4)], axis=0)
    both = dot(down, tokens[...])
    for b in range(SHARD_BLOCKS):
        request = meta[META_REQUEST + meta[0] * SHARD_BLOCKS + b]
        at = slice(b * BLOCK, (b + 1) * BLOCK)
        fa = jnp.where(request == 0, 1.0, 0.0).astype(F32)
        low_t[:, at] = both[0:96, at] * fa + both[96:192, at] * (1.0 - fa)
    ups[...] = jnp.concatenate([panel[j, 48:64, 0:1024] for j in range(4)], axis=0)


def weight_copies(meta, weights, buffers, sems, chip, width):
    half = weights[0].shape[1] // 2
    lane = pl.ds(pl.multiple_of(meta[1] * half, BLOCK), half)
    copies = []
    for i, (w, buf) in enumerate(zip(weights, buffers)):
        lanes = lane if i < 2 else slice(None)
        for n, part in enumerate((chip + meta[1], chip + 1 - meta[1])):
            rows = pl.ds(pl.multiple_of(part * width, 16), width)
            copies.append(pltpu.make_async_copy(w.at[rows, lanes], buf.at[n], sems.at[i, n]))
    return copies


WEIGHT_AT = (slice(0, 256), slice(256, 512), slice(512, 1024))


def near_kernel(meta, own, other, wq, wk, wv, out0, out1, fk, fv, fq, bk, bv, bq, sems, far_sems):
    weights = (wk, wv, wq)
    width = other.shape[0]
    copies = weight_copies(meta, weights, (bk, bv, bq), sems, meta[2] * 2, width)
    later = weight_copies(meta, weights, (fk, fv, fq), far_sems, (1 - meta[2]) * 2, width)
    for copy in copies:
        copy.start()
    for i, (at, buf) in enumerate(zip(WEIGHT_AT, (bk, bv, bq))):
        copies[2 * i].wait()
        copies[2 * i + 1].wait()
        if i == 1:
            for copy in later:
                copy.start()
        for c, out in enumerate((out0, out1)):
            tok = slice(c * CHUNK, (c + 1) * CHUNK)
            out[:, at] = dot_t(own[:, tok], buf[0]) + dot_t(other[:, tok], buf[1])
    for copy in later:
        copy.wait()


def far_kernel(part, own, other, wk, wv, wq, q_out, kv_out):
    for i, (at, w) in enumerate(zip(WEIGHT_AT, (wk, wv, wq))):
        turned = jnp.transpose(part[:, at] + dot_t(own[...], w[0]) + dot_t(other[...], w[1]))
        if i == 2:
            q_out[...] = turned
        else:
            kv_out[at, :] = turned.astype(BF16)


def block_request(meta, block):
    return meta[META_REQUEST + jnp.maximum(block, 0)]


def by_request(meta, low, first_block):
    flags = []
    for b in range(SHARD_BLOCKS):
        request = block_request(meta, first_block + b)
        flags.append(jnp.full((1, BLOCK), jnp.where(request == 0, 1.0, 0.0).astype(F32)))
    flag = jnp.concatenate(flags, axis=1)
    rows = low.astype(BF16).astype(F32)
    return jnp.concatenate([rows * flag, rows * (1.0 - flag)], axis=0).astype(BF16)


def norm_rotate(x, gain, cosine, sine):
    mean_square = jnp.mean(x * x, axis=0, keepdims=True)
    u = x * lax.rsqrt(mean_square + norm_epsilon) * gain
    a = u[0:64]
    b = u[64:128]
    return jnp.concatenate([a * cosine - b * sine, b * cosine + a * sine], axis=0)


def gain_rows(gain):
    return jnp.transpose(jnp.broadcast_to(gain[...], (HEAD_SIZE, HEAD_SIZE)))


def finish_keys(meta, chunks, low_k, low_v, ups, gain, cosine, sine, keys, values, first, blocks):
    base = (meta[0] - 2) * SHARD_BLOCKS + first
    k_term = dot_t(ups[:, 512:768], by_request(meta, low_k, base))
    v_term = dot_t(ups[:, 768:1024], by_request(meta, low_v, base))
    for b in blocks:
        at = slice((first + b) * BLOCK, (first + b + 1) * BLOCK)
        here = slice(b * BLOCK, (b + 1) * BLOCK)
        chunk = chunks[b // CHUNK_BLOCKS]
        lanes = slice(b % CHUNK_BLOCKS * BLOCK, (b % CHUNK_BLOCKS + 1) * BLOCK)
        for g in range(2):
            head = slice(g * HEAD_SIZE, (g + 1) * HEAD_SIZE)
            k = chunk[head, lanes].astype(F32) + adapter_scale * k_term[head, here]
            k = k.astype(BF16).astype(F32)
            turned = norm_rotate(k, gain, cosine[:, at], sine[:, at])
            keys[here, head] = jnp.transpose(turned).astype(BF16)
        values[:, here] = (chunk[256:512, lanes].astype(F32) + adapter_scale * v_term[:, here]).astype(BF16)


def attend(meta, q_rot, keys, values, c, g, first, low_block, high_block):
    rows = slice(c * BLOCK, (c + 1) * BLOCK)
    heads = [slice((2 * g + h) * HEAD_SIZE, (2 * g + h + 1) * HEAD_SIZE) for h in range(2)]
    q = jnp.concatenate([q_rot[head, rows] for head in heads], axis=1)
    base = (meta[0] - 2) * SHARD_BLOCKS
    mine = block_request(meta, base + 8 + c)
    head = slice(g * HEAD_SIZE, (g + 1) * HEAD_SIZE)
    at = slice(low_block * BLOCK, (high_block + 1) * BLOCK)
    scores = dot(keys[at, head], q)
    key = lax.broadcasted_iota(jnp.int32, (BLOCK, 2 * BLOCK), 0)
    query = jnp.bitwise_and(lax.broadcasted_iota(jnp.int32, (BLOCK, 2 * BLOCK), 1), BLOCK - 1)
    den = jnp.zeros((BLOCK, 2 * BLOCK), F32)
    pieces = []
    for j in range(low_block, high_block + 1):
        block = base + first + j
        ok = jnp.logical_and(block >= 0, block_request(meta, block) == mine)
        piece = jnp.exp(scores[(j - low_block) * BLOCK : (j - low_block + 1) * BLOCK])
        piece = piece * jnp.where(ok, 1.0, 0.0).astype(F32)
        if first + j == c + 8:
            piece = jnp.where(query >= key, piece, 0.0)
        if first + j == c:
            piece = jnp.where(query < key, piece, 0.0)
        den = den + piece
        pieces.append(piece.astype(BF16))
    num = dot(values[head, at], jnp.concatenate(pieces, axis=0))
    return num, jnp.sum(den, axis=0, keepdims=True)


def attend_own_kernel(
    meta, q0, q1, o0, o1, low, ups, q_gain, k_gain, cosine, sine, weights,
    q_rot, num_out, den_out, weights_out, keys, values, sem,
):
    fetch = pltpu.make_async_copy(weights, weights_out, sem)
    fetch.start()
    finish_keys(
        meta, (o0, o1), low[32:64, :], low[64:96, :], ups, gain_rows(k_gain), cosine, sine, keys, values, 8, range(4)
    )
    gain = gain_rows(q_gain)
    q_term = dot_t(ups[:, 0:512], by_request(meta, low[0:32, :], meta[0] * SHARD_BLOCKS))
    for c in range(SHARD_BLOCKS):
        q = (q0, q1)[c // CHUNK_BLOCKS]
        lanes = slice(c % CHUNK_BLOCKS * BLOCK, (c % CHUNK_BLOCKS + 1) * BLOCK)
        rows = slice(c * BLOCK, (c + 1) * BLOCK)
        at = slice((8 + c) * BLOCK, (9 + c) * BLOCK)
        for h in range(4):
            head = slice(h * HEAD_SIZE, (h + 1) * HEAD_SIZE)
            x = q[head, lanes] + adapter_scale * q_term[head, rows]
            q_rot[head, rows] = (norm_rotate(x, gain, cosine[:, at], sine[:, at]) * score_scale).astype(BF16)
    for g in range(2):
        for c in range(SHARD_BLOCKS):
            rows = slice(c * BLOCK, (c + 1) * BLOCK)
            num, den = attend(meta, q_rot, keys, values, c, g, 8, 0, c)
            for h in range(2):
                n = 2 * g + h
                part = slice(h * BLOCK, (h + 1) * BLOCK)
                num_out[n * HEAD_SIZE : (n + 1) * HEAD_SIZE, rows] = num[:, part]
                den_out[n : n + 1, rows] = den[:, part]
    fetch.wait()


def attend_prev_kernel(
    meta, q_rot, num_in, den_in, h0, h1, low_h, ups, k_gain, cosine, sine, num_out, den_out, keys, values
):
    finish_keys(
        meta, (h0, h1), low_h[0:32, :], low_h[32:64, :], ups, gain_rows(k_gain), cosine, sine, keys, values, 4, range(4)
    )
    for g in range(2):
        for c in range(SHARD_BLOCKS):
            rows = slice(c * BLOCK, (c + 1) * BLOCK)
            num, den = attend(meta, q_rot, keys, values, c, g, 4, 0, 3)
            for h in range(2):
                n = 2 * g + h
                part = slice(h * BLOCK, (h + 1) * BLOCK)
                head = slice(n * HEAD_SIZE, (n + 1) * HEAD_SIZE)
                num_out[head, rows] = num_in[head, rows] + num[:, part]
                den_out[n : n + 1, rows] = den_in[n : n + 1, rows] + den[:, part]


def attend_far_kernel(chunk, meta, q_rot, num_in, den_in, *refs):
    count = CHUNK_BLOCKS - chunk
    kept, (low_h, ups, k_gain, cosine, sine, out, keys, values) = refs[:count], refs[count:]
    blocks = range(chunk * CHUNK_BLOCKS, SHARD_BLOCKS)
    finish_keys(
        meta, (None,) * chunk + tuple(kept), low_h[0:32, :], low_h[32:64, :], ups, gain_rows(k_gain), cosine, sine,
        keys, values, 0, blocks,
    )
    for g in range(2):
        for c in range(chunk * CHUNK_BLOCKS, (chunk + 1) * CHUNK_BLOCKS):
            rows = slice(c * BLOCK, (c + 1) * BLOCK)
            here = slice(c % CHUNK_BLOCKS * BLOCK, (c % CHUNK_BLOCKS + 1) * BLOCK)
            num, den = attend(meta, q_rot, keys, values, c, g, 0, c, 3)
            for h in range(2):
                n = 2 * g + h
                part = slice(h * BLOCK, (h + 1) * BLOCK)
                head = slice(n * HEAD_SIZE, (n + 1) * HEAD_SIZE)
                total = den_in[n : n + 1, rows] + den[:, part]
                out[head, here] = ((num_in[head, rows] + num[:, part]) / total).astype(BF16)


def request_flag(meta):
    flags = []
    for b in range(SHARD_BLOCKS):
        request = block_request(meta, meta[0] * SHARD_BLOCKS + b)
        flags.append(jnp.full((1, BLOCK), jnp.where(request == 0, 1.0, 0.0).astype(F32)))
    return jnp.concatenate(flags, axis=1)


def out_low_kernel(meta, att0, att1, panel_a, panel_b, low):
    down = panel_a[:, 1408:1920] + panel_b[:, 1408:1920]
    both = jnp.concatenate([dot(down, att0[...]), dot(down, att1[...])], axis=1)
    flag = request_flag(meta)
    low[...] = both[0:32] * flag + both[32:64] * (1.0 - flag)


def part_lanes(meta, chip, cols):
    return [pl.ds(pl.multiple_of(p * cols, BLOCK), cols) for p in (chip + meta[1], chip + 1 - meta[1])]


def out_near_kernel(meta, own, other, w, part):
    first, second = part_lanes(meta, meta[2] * 2, own.shape[0])
    part[...] = dot(w[:, first], own[...]) + dot(w[:, second], other[...])


def out_far_kernel(chunk, meta, own, other, w, part, low, panel_a, panel_b, *refs):
    out = refs[-1]
    tok = slice(chunk * CHUNK, (chunk + 1) * CHUNK)
    lows = low[:, tok].astype(BF16).astype(F32)
    flag = request_flag(meta)[:, tok]
    chosen = jnp.concatenate([lows * flag, lows * (1.0 - flag)], axis=0).astype(BF16)
    up = panel_a[:, 0 : w.shape[0]] + panel_b[:, 0 : w.shape[0]]
    first, second = part_lanes(meta, (1 - meta[2]) * 2, own.shape[0])
    total = part[...] + adapter_scale * dot_t(up, chosen)
    out[...] = (total + dot(w[:, first], own[...]) + dot(w[:, second], other[...])).astype(BF16)


def exchange_quarters(quarters):
    return [quarters[0]] + [lax.ppermute(quarters[s], "seq", [(j, j ^ s) for j in range(4)]) for s in (1, 2, 3)]


def share_quarter(total):
    beside = lax.ppermute(total, "seq", [(j, j ^ 1) for j in range(4)])
    middle = [(1, 2), (2, 1)]
    return [total, beside, lax.ppermute(total, "seq", middle), lax.ppermute(beside, "seq", middle)]


def per_device(
    tokens,
    query_matrix,
    key_matrix,
    value_matrix,
    output_matrix,
    query_gain,
    key_norm_gain,
    adapter_down,
    adapter_up_query,
    key_value_up_panels,
    adapter_out_down,
    adapter_out_up,
    request_of_block,
    adapter_of_request,
):
    rows, width = tokens.shape
    cols = query_matrix.shape[1]
    seq, rep, head = (lax.axis_index(name).astype(jnp.int32) for name in ("seq", "rep", "head"))
    meta = jnp.concatenate([jnp.stack([seq, rep, head]), adapter_of_request, request_of_block])
    tokens = tokens.T

    def across(value):
        return lax.ppermute(value, "head", SWAP)

    def core(value):
        return lax.ppermute(value, "rep", SWAP)

    def up(value, by=1):
        return lax.ppermute(value, "seq", [(i, (i + by) % 4) for i in range(4)])

    def after(value, *others):
        return lax.optimization_barrier((value, *others))[0]

    far_own = across(tokens)
    near_other = core(tokens)

    def swapped(value, by):
        return lax.ppermute(value, "seq", [(j, j ^ by) for j in range(4)])

    def pack(kernel, name, result, pools, order):
        return call(
            kernel,
            name,
            result,
            [SM] + [FAR] * len(pools),
            [adapter_of_request, *pools],
            [pltpu.VMEM(pool.shape, BF16) for pool in pools] + [pltpu.SemaphoreType.DMA((len(pools),))],
            after=order,
        )

    pools = [jnp.swapaxes(adapter_down, 1, 2), adapter_up_query, key_value_up_panels]
    quarters = pack(pack_kernel, "pack", (shape((64, width)),) * 4, pools, [])
    received = exchange_quarters(quarters)
    out_pools = [jnp.swapaxes(adapter_out_down, 1, 2), adapter_out_up]
    out_panel = pack(pack_out_kernel, "pack_out", shape((64, 1920)), out_pools, [quarters[0]])
    out_beside = swapped(out_panel, 1)

    chunks = rows // CHUNK
    weights = [query_matrix, key_matrix, value_matrix]
    weight_scratch = [
        pltpu.VMEM((2, width, 256), BF16),
        pltpu.VMEM((2, width, 256), BF16),
        pltpu.VMEM((2, width, cols), BF16),
        pltpu.SemaphoreType.DMA((3, 2)),
    ]
    weight_shapes = [(2, width, 256), (2, width, 256), (2, width, cols)]
    near0, near1, *far_weights = call(
        near_kernel,
        "near",
        (shape((CHUNK, 1024), F32),) * chunks + tuple(shape(dims) for dims in weight_shapes),
        [SM, VM, VM, FAR, FAR, FAR],
        [meta, tokens, near_other, *weights],
        [pltpu.VMEM(dims, BF16) for dims in weight_shapes] + [pltpu.SemaphoreType.DMA((3, 2))] * 2,
        after=[out_panel],
    )
    near = [near0, near1]

    def project(c, prior):
        mine = pl.BlockSpec((width, CHUNK), lambda i: (0, c))
        return call(
            far_kernel,
            "far",
            (shape((cols, CHUNK), F32), shape((512, CHUNK))),
            [VM, mine, mine, VM, VM, VM],
            [near[c], far_own, far_other, *far_weights],
            grid=(1,),
            after=[prior],
        )

    all_blocks = request_of_block.shape[0]
    window = jnp.arange(3 * rows, dtype=jnp.int32) + (seq - 2) * rows
    window = jnp.clip(window, 0, all_blocks * BLOCK - 1)
    second_start = jnp.sum((request_of_block < 1).astype(jnp.int32)) * BLOCK
    position = jnp.where(window >= second_start, window - second_start, window)
    half_dim = HEAD_SIZE // 2
    frequency = jnp.power(rope_base, -jnp.arange(half_dim, dtype=F32) * 2.0 / HEAD_SIZE)
    angles = frequency[:, None] * position.astype(F32)[None, :]
    cosine, sine = jnp.cos(angles), jnp.sin(angles)
    q_gain = query_gain.reshape(1, HEAD_SIZE)
    k_gain = key_norm_gain.reshape(1, HEAD_SIZE)

    quarter = call(sum_kernel, "sum", shape((64, width)), [VM] * 4, received, after=[near[0], cosine, sine])
    pieces = share_quarter(quarter)
    out_pair = call(add_kernel, "out_add", shape((64, 1920)), [VM] * 2, [out_panel, out_beside], after=[quarter])
    far_other = core(after(far_own, pieces[1], pieces[2], out_pair))
    late_q, late_kv = project(1, pieces[1])
    early_q, early_kv = project(0, late_kv)
    partial_low, ups = call(
        low_kernel,
        "low",
        (shape((96, rows), F32), shape((64, 1024))),
        [SM] + [VM] * 5,
        [meta, tokens, *pieces],
        [pltpu.VMEM((4, 64, width), BF16)],
        after=[early_kv],
    )
    chip_low = partial_low + core(partial_low)
    low = chip_low + across(chip_low)

    prev_late, prev_early = up(late_kv), up(early_kv)
    low_kv = low[32:96].astype(BF16)
    low_prev = up(low_kv)
    low_prev2 = up(low_prev)
    prev2_late = up(after(prev_late, early_kv))

    shard_scratch = [pltpu.VMEM((rows, 256), BF16), pltpu.VMEM((256, rows), BF16)]
    sums = (shape((cols, rows), F32), shape((8, rows), F32))
    q_rot, num, den, out_weights = call(
        attend_own_kernel,
        "attend_own",
        (shape((cols, rows)), *sums, shape(output_matrix.T.shape)),
        [SM] + [VM] * 10 + [FAR],
        [meta, early_q, late_q, early_kv, late_kv, low, ups, q_gain, k_gain, cosine, sine, output_matrix.T],
        shard_scratch + [pltpu.SemaphoreType.DMA],
    )
    prev2_early = up(after(prev_early, low_prev, num))
    num, den = call(
        attend_prev_kernel,
        "attend_prev",
        sums,
        [SM] + [VM] * 10,
        [meta, q_rot, num, den, prev_early, prev_late, low_prev, ups, k_gain, cosine, sine],
        shard_scratch,
    )

    def attend_far(chunk, kept, order):
        return call(
            functools.partial(attend_far_kernel, chunk),
            "attend_far",
            shape((cols, CHUNK)),
            [SM] + [VM] * (8 + len(kept)),
            [meta, q_rot, num, den, *kept, low_prev2, ups, k_gain, cosine, sine],
            shard_scratch,
            after=order,
        )

    att_late = attend_far(1, [prev2_late], [])
    att_early = attend_far(0, [prev2_early, prev2_late], [att_late])

    out_rest = swapped(out_pair, 2)
    out_low = call(
        out_low_kernel,
        "out_low",
        shape((32, rows), F32),
        [SM] + [VM] * 4,
        [meta, att_early, att_late, out_pair, out_rest],
    )
    out_low = out_low + core(out_low)
    out_low = out_low + across(out_low)

    result = []
    for chunk, att in ((1, att_late), (0, att_early)):
        att_far = across(att)
        part = call(
            out_near_kernel,
            "out_near",
            shape((width, CHUNK), F32),
            [SM] + [VM] * 3,
            [meta, att, core(att), out_weights],
            after=[att_early],
        )
        result = [
            call(
                functools.partial(out_far_kernel, chunk),
                "out_far",
                shape((width, rows)),
                [SM] + [VM] * 7 + [HB] * len(result),
                [meta, att_far, core(att_far), out_weights, part, out_low, out_pair, out_rest, *result],
                out_specs=pl.BlockSpec((width, CHUNK), lambda i, chunk=chunk: (0, chunk)),
                grid=(1,),
                aliases={8: 0} if result else {},
            )
        ]
    return result[0].T


def plain_sizes(mesh):
    return mesh.shape["seq"] == 4 and mesh.shape["head"] == 2 and mesh.shape["rep"] == 2


def solution(mesh):
    return jax.shard_map(
        per_device if plain_sizes(mesh) else per_device_general,
        mesh=mesh,
        in_specs=(
            P(("groups", "seq"), ("head", "rep")),
            P(None, ("head", "rep")),
            P(None, "head"),
            P(None, "head"),
            P(None, ("head", "rep")),
            P(),
            P(),
            P("seq", ("head", "rep"), None),
            P("seq", None, ("head", "rep")),
            P("seq", None, None, "head"),
            P("seq", ("head", "rep"), None),
            P("seq", None, ("head", "rep")),
            P("groups"),
            P("groups"),
        ),
        out_specs=P(("groups", "seq"), ("head", "rep")),
        check_vma=False,
    )
```

```python
import functools
import math

import jax
import jax.numpy as jnp
from jax import lax
from jax.experimental import pallas as pl
from jax.experimental.pallas import tpu as pltpu
from jax.sharding import PartitionSpec as P

HEAD_SIZE = 128
ADAPTER_RANK = 32
KEY_WINDOW = 1024
BLOCK = 128


norm_epsilon = 1e-06
rope_base = 10000.0
score_scale = 168.0 ** (-0.5)
adapter_scale = 2.0


def shifted(value, axis, by):
    size = lax.axis_size(axis)
    pairs = [(i, i + by) for i in range(size) if 0 <= i + by < size]
    return lax.ppermute(value, axis, pairs)


def per_head_norm(values, scale_gain):
    mean_square = jnp.mean(values * values, axis=-1, keepdims=True)
    return values * lax.rsqrt(mean_square + norm_epsilon) * scale_gain


def rope_tables(positions, head_dim):
    half_dim = head_dim // 2
    frequency = jnp.power(rope_base, -jnp.arange(half_dim, dtype=jnp.float32) * 2.0 / head_dim)
    angles = positions.astype(jnp.float32)[:, None] * frequency[None, :]
    return (jnp.cos(angles), jnp.sin(angles))


def rotate_feature_pairs(values, cosine_table, sine_values):
    half_dim = values.shape[-1] // 2
    first_half = values[..., :half_dim]
    second_half = values[..., half_dim:]
    cosine_table = cosine_table[:, None, :]
    sine_values = sine_values[:, None, :]
    return jnp.concatenate(
        [
            first_half * cosine_table - second_half * sine_values,
            second_half * cosine_table + first_half * sine_values,
        ],
        axis=-1,
    )


def request_starts(block_requests, all_requests):
    earlier = (all_requests[None, :] < block_requests[:, None]).astype(jnp.int32)
    return jnp.sum(earlier, axis=1) * BLOCK


def per_device_general(
    tokens,
    query_matrix,
    key_matrix,
    value_matrix,
    output_matrix,
    query_gain,
    key_norm_gain,
    adapter_down,
    adapter_up_query,
    key_value_up_panels,
    adapter_out_down,
    adapter_out_up,
    request_of_block,
    adapter_of_request,
):
    tok_rows, width_part = tokens.shape
    query_cols = query_matrix.shape[1]
    key_cols = key_matrix.shape[1]
    query_heads = query_cols // HEAD_SIZE
    block_count = tok_rows // BLOCK
    all_blocks = request_of_block.shape[0]
    request_total = adapter_of_request.shape[0]
    seq_index = lax.axis_index("seq")
    rep_index = lax.axis_index("rep")
    first_row = seq_index * tok_rows
    own_requests = lax.dynamic_slice_in_dim(
        request_of_block, seq_index * block_count, block_count, 0
    )
    request_match = own_requests[:, None] == jnp.arange(request_total, dtype=jnp.int32)[None, :]
    own_adapters = jnp.sum(jnp.where(request_match, adapter_of_request[None, :], 0), axis=1)
    pool_part = (
        lax.all_gather(adapter_down, "seq", axis=0, tiled=True),
        lax.all_gather(adapter_up_query, "seq", axis=0, tiled=True),
        lax.all_gather(key_value_up_panels, "seq", axis=0, tiled=True),
        lax.all_gather(adapter_out_down, "seq", axis=0, tiled=True),
        lax.all_gather(adapter_out_up, "seq", axis=0, tiled=True),
    )
    held_count = pool_part[0].shape[0]
    select = (own_adapters[:, None] == jnp.arange(held_count, dtype=jnp.int32)[None, :]).astype(
        jnp.bfloat16
    )
    (
        picked_down_panels,
        picked_query_panels,
        picked_key_panels,
        chosen_out_down,
        picked_output_up,
    ) = tuple(
        (
            jnp.einsum(
                "bn,n...->b...", select, panel_part, preferred_element_type=jnp.float32
            ).astype(jnp.bfloat16)
            for panel_part in pool_part
        )
    )
    token_block_list = tokens.reshape(block_count, BLOCK, width_part)
    partial_low = jnp.einsum(
        "myj,mjc->myc", token_block_list, picked_down_panels, preferred_element_type=jnp.float32
    ).reshape(tok_rows, 3 * ADAPTER_RANK)
    reduced_rank_rows = (
        lax.psum(partial_low, ("head", "rep"))
        .astype(jnp.bfloat16)
        .reshape(block_count, BLOCK, 3 * ADAPTER_RANK)
    )
    feature_part = lax.all_gather(tokens, ("head", "rep"), axis=1, tiled=True)
    query_add = jnp.dot(feature_part, query_matrix, preferred_element_type=jnp.float32)
    key_add = jnp.dot(feature_part, key_matrix, preferred_element_type=jnp.float32)
    value_add = jnp.dot(feature_part, value_matrix, preferred_element_type=jnp.float32)
    query_linear = query_add
    key_linear = key_add
    value_linear = value_add
    query_linear = query_linear + adapter_scale * jnp.einsum(
        "tlq,tqo->tlo",
        reduced_rank_rows[..., :ADAPTER_RANK],
        picked_query_panels,
        preferred_element_type=jnp.float32,
    ).reshape(tok_rows, query_cols)
    key_linear = key_linear + adapter_scale * jnp.einsum(
        "tlq,tqo->tlo",
        reduced_rank_rows[..., ADAPTER_RANK : 2 * ADAPTER_RANK],
        picked_key_panels[:, 0],
        preferred_element_type=jnp.float32,
    ).reshape(tok_rows, key_cols)
    value_linear = value_linear + adapter_scale * jnp.einsum(
        "tlq,tqo->tlo",
        reduced_rank_rows[..., 2 * ADAPTER_RANK :],
        picked_key_panels[:, 1],
        preferred_element_type=jnp.float32,
    ).reshape(tok_rows, key_cols)
    key_full = key_linear.astype(jnp.bfloat16)
    value_full = value_linear.astype(jnp.bfloat16)
    key_heads = key_cols // HEAD_SIZE
    token_index = first_row + jnp.arange(tok_rows, dtype=jnp.int32)
    token_request = jnp.repeat(own_requests, BLOCK)
    token_start = jnp.repeat(request_starts(own_requests, request_of_block), BLOCK)
    cosine_table, sine_values = rope_tables(token_index - token_start, HEAD_SIZE)
    query_rows = (
        rotate_feature_pairs(
            per_head_norm(query_linear.reshape(tok_rows, query_heads, HEAD_SIZE), query_gain),
            cosine_table,
            sine_values,
        )
        * score_scale
    ).astype(jnp.bfloat16)
    rotated_keys = rotate_feature_pairs(
        per_head_norm(
            key_full.astype(jnp.float32).reshape(tok_rows, key_heads, HEAD_SIZE), key_norm_gain
        ),
        cosine_table,
        sine_values,
    ).astype(jnp.bfloat16)
    group_heads = max(query_heads // 2, 1)
    group_size = query_heads // group_heads
    head_first = rep_index * query_heads // 2
    keys_used = lax.dynamic_slice_in_dim(rotated_keys, head_first, group_heads, 1).reshape(
        tok_rows, group_heads * HEAD_SIZE
    )
    values_used = lax.dynamic_slice_in_dim(
        value_full.reshape(tok_rows, key_heads, HEAD_SIZE), head_first, group_heads, 1
    ).reshape(tok_rows, group_heads * HEAD_SIZE)
    query_groups = query_rows.reshape(tok_rows, group_heads, group_size, HEAD_SIZE)
    block_table = jnp.arange(all_blocks, dtype=jnp.int32)
    empty_state = (
        jnp.zeros((tok_rows, group_heads, group_size, HEAD_SIZE), jnp.float32),
        jnp.zeros((group_heads, group_size, tok_rows), jnp.float32),
    )
    reach_blocks = KEY_WINDOW // tok_rows
    stacked = jnp.stack((keys_used, values_used))
    earlier = []
    for step_back in range(reach_blocks, 0, -1):
        earlier.append(shifted(stacked, "seq", step_back))
    window_stack = jnp.concatenate(earlier + [stacked], axis=1)
    fold_state = empty_state
    offset = first_row - reach_blocks * tok_rows
    key_block = window_stack[0]
    value_block = window_stack[1]
    key_length = key_block.shape[0]
    step_length = math.gcd(key_length, 512)
    steps_count = key_length // step_length
    key_steps = key_block.reshape(steps_count, step_length, group_heads, HEAD_SIZE)
    value_steps = value_block.reshape(steps_count, step_length, group_heads, HEAD_SIZE)

    def one_step(carry_state, step_inputs):
        step_keys, step_values, step_index = step_inputs
        key_position = offset + step_index * step_length + jnp.arange(step_length, dtype=jnp.int32)
        key_block_id = jnp.clip(key_position, 0, all_blocks * BLOCK - 1) // BLOCK
        key_request = jnp.sum(
            jnp.where(key_block_id[:, None] == block_table[None, :], request_of_block[None, :], 0),
            axis=1,
        )
        distance = token_index[:, None] - key_position[None, :]
        allowed = (
            (key_position[None, :] >= 0)
            & (distance >= 0)
            & (distance < KEY_WINDOW)
            & (token_request[:, None] == key_request[None, :])
        )
        scores = jnp.einsum(
            "tcpd,kcd->cptk", query_groups, step_keys, preferred_element_type=jnp.float32
        )
        weights = jnp.where(allowed[None, None], jnp.exp(scores), 0.0)
        numerator, denominator = carry_state
        denominator = denominator + jnp.sum(weights, axis=-1)
        numerator = numerator + jnp.einsum(
            "cptk,kcd->tcpd",
            weights.astype(jnp.bfloat16),
            step_values,
            preferred_element_type=jnp.float32,
        )
        return ((numerator, denominator), None)

    fold_state, unused_out = lax.scan(
        one_step, fold_state, (key_steps, value_steps, jnp.arange(steps_count, dtype=jnp.int32))
    )
    numerator, denominator = fold_state
    attention_result = (
        (numerator / jnp.transpose(denominator, (2, 0, 1))[..., None])
        .astype(jnp.bfloat16)
        .reshape(tok_rows, query_cols)
    )
    output_zero = (
        jnp.zeros((tok_rows, width_part), jnp.float32),
        jnp.zeros((tok_rows, ADAPTER_RANK), jnp.float32),
    )
    projected_rows = jnp.dot(
        lax.all_gather(attention_result, ("head", "rep"), axis=1, tiled=True),
        output_matrix,
        preferred_element_type=jnp.float32,
    )
    projected_rows, lowered = (projected_rows, output_zero[1])
    local_low = jnp.einsum(
        "bkc,bcr->bkr",
        attention_result.reshape(block_count, BLOCK, query_cols),
        chosen_out_down,
        preferred_element_type=jnp.float32,
    ).reshape(tok_rows, ADAPTER_RANK)
    output_reduced_rank = lax.psum(local_low, ("head", "rep")).astype(jnp.bfloat16)
    result = projected_rows + adapter_scale * jnp.einsum(
        "zch,zhp->zcp",
        output_reduced_rank.reshape(block_count, BLOCK, ADAPTER_RANK),
        picked_output_up,
        preferred_element_type=jnp.float32,
    ).reshape(tok_rows, width_part)
    return result.astype(jnp.bfloat16)


F32 = jnp.float32
BF16 = jnp.bfloat16
VMEM_SMALL = 20 * 1024 * 1024
VMEM_LARGE = 56 * 1024 * 1024
SWAP = [(0, 1), (1, 0)]
SHARD_BLOCKS = 4
CHUNK = 256
CHUNK_BLOCKS = CHUNK // BLOCK
META_ADAPTER = 3
META_REQUEST = 5


def dot(a, b):
    return lax.dot_general(a, b, (((1,), (0,)), ((), ())), preferred_element_type=F32)


def dot_t(a, b):
    return lax.dot_general(a, b, (((0,), (0,)), ((), ())), preferred_element_type=F32)


VM = pl.BlockSpec(memory_space=pltpu.VMEM)
SM = pl.BlockSpec(memory_space=pltpu.SMEM)
HB = pl.BlockSpec(memory_space=pl.ANY)
FAR = pl.BlockSpec(memory_space=pltpu.HBM)


def in_hbm(value):
    return pltpu.with_memory_space_constraint(value, pltpu.HBM)


def shape(dims, dtype=BF16):
    return jax.ShapeDtypeStruct(dims, dtype)


def call(kernel, name, out_shape, in_specs, args, scratch=(), out_specs=None, grid=None, after=(), aliases=None):
    count = len(in_specs)

    def body(*refs):
        kernel(*refs[:count], *refs[count + len(after) :])

    outs = out_specs
    if outs is None:
        outs = VM if isinstance(out_shape, jax.ShapeDtypeStruct) else tuple(VM for _ in out_shape)
    more = dict(grid=grid) if grid else {}
    return pl.pallas_call(
        body,
        out_shape=out_shape,
        in_specs=list(in_specs) + [HB] * len(after),
        out_specs=outs,
        scratch_shapes=list(scratch),
        input_output_aliases=aliases or {},
        compiler_params=pltpu.CompilerParams(vmem_limit_bytes=VMEM_SMALL),
        cost_estimate=pl.CostEstimate(flops=1000, bytes_accessed=1000, transcendentals=0),
        name=name,
        **more,
    )(*[in_hbm(a) if spec is FAR else a for a, spec in zip(args, in_specs)], *after)


def picked(adapters, held):
    me = lax.axis_index("seq").astype(jnp.int32)
    chosen = []
    for step in range(4):
        quarter = jnp.bitwise_xor(me, step)
        slot = adapters[lax.div(quarter, 2)] - me * held
        here = jnp.logical_and(slot >= 0, slot < held)
        keep = jnp.where(here, 1.0, 0.0).astype(F32)
        chosen.append((jnp.clip(slot, 0, held - 1), keep, lax.rem(quarter, 2)))
    return chosen


def bring(sources, targets, sems):
    copies = [pltpu.make_async_copy(a, b, sems.at[i]) for i, (a, b) in enumerate(zip(sources, targets))]
    for copy in copies:
        copy.start()
    for copy in copies:
        copy.wait()


def pack_kernel(adapters, down_far, up_q_far, up_kv_far, *refs):
    quarters, (down, up_q, up_kv, sems) = refs[:4], refs[4:]
    bring((down_far, up_q_far, up_kv_far), (down, up_q, up_kv), sems)
    rep = lax.axis_index("rep").astype(jnp.int32)
    half = up_kv.shape[3] // 2
    cols = up_q.shape[2]
    width = down.shape[2]
    for (slot, keep, part), out in zip(picked(adapters, down.shape[0]), quarters):
        rows = pl.ds(pl.multiple_of(part * 48, 16), 48)
        ranks = pl.ds(pl.multiple_of(part * 16, 16), 16)
        out[0:48, :] = (down[slot, rows, :].astype(F32) * keep).astype(BF16)
        out[48:64, 0:cols] = (up_q[slot, ranks, :].astype(F32) * keep).astype(BF16)
        for which in range(2):
            both = up_kv[slot, which, ranks, :].astype(F32) * keep
            mine = jnp.where(rep == 0, both[:, :half], both[:, half:])
            out[48:64, cols + which * half : cols + (which + 1) * half] = mine.astype(BF16)
        out[48:64, 1024:width] = jnp.zeros((16, width - 1024), BF16)


def pack_out_kernel(adapters, out_down_far, out_up_far, out, out_down, out_up, sems):
    bring((out_down_far, out_up_far), (out_down, out_up), sems)
    width = out_up.shape[2]
    held = out_up.shape[0]
    for request in range(2):
        slot = adapters[request] - lax.axis_index("seq").astype(jnp.int32) * held
        here = jnp.logical_and(slot >= 0, slot < held)
        keep = jnp.where(here, 1.0, 0.0).astype(F32)
        slot = jnp.clip(slot, 0, held - 1)
        rows = slice(request * 32, (request + 1) * 32)
        out[rows, 0:width] = (out_up[slot].astype(F32) * keep).astype(BF16)
        out[rows, width:1408] = jnp.zeros((32, 1408 - width), BF16)
        out[rows, 1408:1920] = (out_down[slot].astype(F32) * keep).astype(BF16)


def add_kernel(a, b, up, down):
    width = up.shape[1]
    up[...] = a[:, 0:width] + b[:, 0:width]
    down[...] = a[:, 1408:1920] + b[:, 1408:1920]


def sum_kernel(a, b, c, d, out):
    out[...] = a[...] + b[...] + c[...] + d[...]


def place_quarters(meta, quarters, panel):
    me = meta[0]
    low_side = me < 2
    at = (me, jnp.bitwise_xor(me, 1), jnp.where(low_side, 2, 1), jnp.where(low_side, 3, 0))
    for index, quarter in zip(at, quarters):
        panel[index] = quarter[...]


def low_kernel(meta, tokens, p0, p1, p2, p3, low_t, ups, panel):
    place_quarters(meta, (p0, p1, p2, p3), panel)
    down = jnp.concatenate([panel[j, 0:48, :] for j in range(4)], axis=0)
    both = dot(down, tokens[...])
    for b in range(SHARD_BLOCKS):
        request = meta[META_REQUEST + meta[0] * SHARD_BLOCKS + b]
        at = slice(b * BLOCK, (b + 1) * BLOCK)
        fa = jnp.where(request == 0, 1.0, 0.0).astype(F32)
        low_t[:, at] = both[0:96, at] * fa + both[96:192, at] * (1.0 - fa)
    ups[...] = jnp.concatenate([panel[j, 48:64, 0:1024] for j in range(4)], axis=0)


def weight_copies(meta, weights, buffers, sems, chip, width):
    half = weights[0].shape[1] // 2
    lane = pl.ds(pl.multiple_of(meta[1] * half, BLOCK), half)
    copies = []
    for i, (w, buf) in enumerate(zip(weights, buffers)):
        lanes = lane if i < 2 else slice(None)
        for n, part in enumerate((chip + meta[1], chip + 1 - meta[1])):
            rows = pl.ds(pl.multiple_of(part * width, 16), width)
            copies.append(pltpu.make_async_copy(w.at[rows, lanes], buf.at[n], sems.at[i, n]))
    return copies


WEIGHT_AT = (slice(0, 256), slice(256, 512), slice(512, 1024))


def near_kernel(meta, own, other, wq, wk, wv, out0, out1, fk, fv, fq, bk, bv, bq, sems, far_sems):
    weights = (wk, wv, wq)
    width = other.shape[0]
    copies = weight_copies(meta, weights, (bk, bv, bq), sems, meta[2] * 2, width)
    later = weight_copies(meta, weights, (fk, fv, fq), far_sems, (1 - meta[2]) * 2, width)
    for copy in copies:
        copy.start()
    for i, (at, buf) in enumerate(zip(WEIGHT_AT, (bk, bv, bq))):
        copies[2 * i].wait()
        copies[2 * i + 1].wait()
        if i == 1:
            for copy in later:
                copy.start()
        for c, out in enumerate((out0, out1)):
            tok = slice(c * CHUNK, (c + 1) * CHUNK)
            out[:, at] = dot_t(own[:, tok], buf[0]) + dot_t(other[:, tok], buf[1])
    for copy in later:
        copy.wait()


def far_kernel(part, own, other, wk, wv, wq, q_out, kv_out):
    for i, (at, w) in enumerate(zip(WEIGHT_AT, (wk, wv, wq))):
        turned = jnp.transpose(part[:, at] + dot_t(own[...], w[0]) + dot_t(other[...], w[1]))
        if i == 2:
            q_out[...] = turned
        else:
            kv_out[at, :] = turned.astype(BF16)


def block_request(meta, block):
    return meta[META_REQUEST + jnp.maximum(block, 0)]


def by_request(meta, low, first_block):
    flags = []
    for b in range(SHARD_BLOCKS):
        request = block_request(meta, first_block + b)
        flags.append(jnp.full((1, BLOCK), jnp.where(request == 0, 1.0, 0.0).astype(F32)))
    flag = jnp.concatenate(flags, axis=1)
    rows = low.astype(BF16).astype(F32)
    return jnp.concatenate([rows * flag, rows * (1.0 - flag)], axis=0).astype(BF16)


def norm_rotate(x, gain, cosine, sine):
    mean_square = jnp.mean(x * x, axis=0, keepdims=True)
    u = x * lax.rsqrt(mean_square + norm_epsilon) * gain
    a = u[0:64]
    b = u[64:128]
    return jnp.concatenate([a * cosine - b * sine, b * cosine + a * sine], axis=0)


def gain_rows(gain):
    return jnp.transpose(jnp.broadcast_to(gain[...], (HEAD_SIZE, HEAD_SIZE)))


def finish_keys(meta, chunks, low_k, low_v, ups, gain, cosine, sine, keys, values, first, blocks):
    base = (meta[0] - 2) * SHARD_BLOCKS + first
    k_term = dot_t(ups[:, 512:768], by_request(meta, low_k, base))
    v_term = dot_t(ups[:, 768:1024], by_request(meta, low_v, base))
    for b in blocks:
        at = slice((first + b) * BLOCK, (first + b + 1) * BLOCK)
        here = slice(b * BLOCK, (b + 1) * BLOCK)
        chunk = chunks[b // CHUNK_BLOCKS]
        lanes = slice(b % CHUNK_BLOCKS * BLOCK, (b % CHUNK_BLOCKS + 1) * BLOCK)
        for g in range(2):
            head = slice(g * HEAD_SIZE, (g + 1) * HEAD_SIZE)
            k = chunk[head, lanes].astype(F32) + adapter_scale * k_term[head, here]
            k = k.astype(BF16).astype(F32)
            turned = norm_rotate(k, gain, cosine[:, at], sine[:, at])
            keys[here, head] = jnp.transpose(turned).astype(BF16)
        values[:, here] = (chunk[256:512, lanes].astype(F32) + adapter_scale * v_term[:, here]).astype(BF16)


def attend(meta, q_rot, keys, values, c, g, first, low_block, high_block):
    rows = slice(c * BLOCK, (c + 1) * BLOCK)
    heads = [slice((2 * g + h) * HEAD_SIZE, (2 * g + h + 1) * HEAD_SIZE) for h in range(2)]
    q = jnp.concatenate([q_rot[head, rows] for head in heads], axis=1)
    base = (meta[0] - 2) * SHARD_BLOCKS
    mine = block_request(meta, base + 8 + c)
    head = slice(g * HEAD_SIZE, (g + 1) * HEAD_SIZE)
    at = slice(low_block * BLOCK, (high_block + 1) * BLOCK)
    scores = dot(keys[at, head], q)
    key = lax.broadcasted_iota(jnp.int32, (BLOCK, 2 * BLOCK), 0)
    query = jnp.bitwise_and(lax.broadcasted_iota(jnp.int32, (BLOCK, 2 * BLOCK), 1), BLOCK - 1)
    den = jnp.zeros((BLOCK, 2 * BLOCK), F32)
    pieces = []
    for j in range(low_block, high_block + 1):
        block = base + first + j
        ok = jnp.logical_and(block >= 0, block_request(meta, block) == mine)
        piece = jnp.exp(scores[(j - low_block) * BLOCK : (j - low_block + 1) * BLOCK])
        piece = piece * jnp.where(ok, 1.0, 0.0).astype(F32)
        if first + j == c + 8:
            piece = jnp.where(query >= key, piece, 0.0)
        if first + j == c:
            piece = jnp.where(query < key, piece, 0.0)
        den = den + piece
        pieces.append(piece.astype(BF16))
    num = dot(values[head, at], jnp.concatenate(pieces, axis=0))
    return num, jnp.sum(den, axis=0, keepdims=True)


def attend_own_kernel(
    meta, q0, q1, o0, o1, low, ups, q_gain, k_gain, cosine, sine, weights,
    q_rot, num_out, den_out, weights_out, keys, values, sem,
):
    fetch = pltpu.make_async_copy(weights, weights_out, sem)
    fetch.start()
    finish_keys(
        meta, (o0, o1), low[32:64, :], low[64:96, :], ups, gain_rows(k_gain), cosine, sine, keys, values, 8, range(4)
    )
    gain = gain_rows(q_gain)
    q_term = dot_t(ups[:, 0:512], by_request(meta, low[0:32, :], meta[0] * SHARD_BLOCKS))
    for c in range(SHARD_BLOCKS):
        q = (q0, q1)[c // CHUNK_BLOCKS]
        lanes = slice(c % CHUNK_BLOCKS * BLOCK, (c % CHUNK_BLOCKS + 1) * BLOCK)
        rows = slice(c * BLOCK, (c + 1) * BLOCK)
        at = slice((8 + c) * BLOCK, (9 + c) * BLOCK)
        for h in range(4):
            head = slice(h * HEAD_SIZE, (h + 1) * HEAD_SIZE)
            x = q[head, lanes] + adapter_scale * q_term[head, rows]
            q_rot[head, rows] = (norm_rotate(x, gain, cosine[:, at], sine[:, at]) * score_scale).astype(BF16)
    for g in range(2):
        for c in range(SHARD_BLOCKS):
            rows = slice(c * BLOCK, (c + 1) * BLOCK)
            num, den = attend(meta, q_rot, keys, values, c, g, 8, 0, c)
            for h in range(2):
                n = 2 * g + h
                part = slice(h * BLOCK, (h + 1) * BLOCK)
                num_out[n * HEAD_SIZE : (n + 1) * HEAD_SIZE, rows] = num[:, part]
                den_out[n : n + 1, rows] = den[:, part]
    fetch.wait()


def attend_prev_kernel(
    meta, q_rot, num_in, den_in, h0, h1, low_h, ups, k_gain, cosine, sine, num_out, den_out, keys, values
):
    finish_keys(
        meta, (h0, h1), low_h[0:32, :], low_h[32:64, :], ups, gain_rows(k_gain), cosine, sine, keys, values, 4, range(4)
    )
    for g in range(2):
        for c in range(SHARD_BLOCKS):
            rows = slice(c * BLOCK, (c + 1) * BLOCK)
            num, den = attend(meta, q_rot, keys, values, c, g, 4, 0, 3)
            for h in range(2):
                n = 2 * g + h
                part = slice(h * BLOCK, (h + 1) * BLOCK)
                head = slice(n * HEAD_SIZE, (n + 1) * HEAD_SIZE)
                num_out[head, rows] = num_in[head, rows] + num[:, part]
                den_out[n : n + 1, rows] = den_in[n : n + 1, rows] + den[:, part]


def attend_far_kernel(chunk, meta, q_rot, num_in, den_in, *refs):
    count = CHUNK_BLOCKS - chunk
    kept, (low_h, ups, k_gain, cosine, sine, out, keys, values) = refs[:count], refs[count:]
    blocks = range(chunk * CHUNK_BLOCKS, SHARD_BLOCKS)
    finish_keys(
        meta, (None,) * chunk + tuple(kept), low_h[0:32, :], low_h[32:64, :], ups, gain_rows(k_gain), cosine, sine,
        keys, values, 0, blocks,
    )
    for g in range(2):
        for c in range(chunk * CHUNK_BLOCKS, (chunk + 1) * CHUNK_BLOCKS):
            rows = slice(c * BLOCK, (c + 1) * BLOCK)
            here = slice(c % CHUNK_BLOCKS * BLOCK, (c % CHUNK_BLOCKS + 1) * BLOCK)
            num, den = attend(meta, q_rot, keys, values, c, g, 0, c, 3)
            for h in range(2):
                n = 2 * g + h
                part = slice(h * BLOCK, (h + 1) * BLOCK)
                head = slice(n * HEAD_SIZE, (n + 1) * HEAD_SIZE)
                total = den_in[n : n + 1, rows] + den[:, part]
                out[head, here] = ((num_in[head, rows] + num[:, part]) / total).astype(BF16)


def request_flag(meta):
    flags = []
    for b in range(SHARD_BLOCKS):
        request = block_request(meta, meta[0] * SHARD_BLOCKS + b)
        flags.append(jnp.full((1, BLOCK), jnp.where(request == 0, 1.0, 0.0).astype(F32)))
    return jnp.concatenate(flags, axis=1)


def out_low_kernel(meta, att0, att1, panel_a, panel_b, low):
    down = panel_a[...] + panel_b[...]
    both = jnp.concatenate([dot(down, att0[...]), dot(down, att1[...])], axis=1)
    flag = request_flag(meta)
    low[...] = both[0:32] * flag + both[32:64] * (1.0 - flag)


def part_lanes(meta, chip, cols):
    return [pl.ds(pl.multiple_of(p * cols, BLOCK), cols) for p in (chip + meta[1], chip + 1 - meta[1])]


def out_near_kernel(meta, own, other, w, part):
    first, second = part_lanes(meta, meta[2] * 2, own.shape[0])
    part[...] = dot(w[:, first], own[...]) + dot(w[:, second], other[...])


def out_far_kernel(chunk, meta, own, other, w, part, low, panel_a, panel_b, *refs):
    out = refs[-1]
    tok = slice(chunk * CHUNK, (chunk + 1) * CHUNK)
    lows = low[:, tok].astype(BF16).astype(F32)
    flag = request_flag(meta)[:, tok]
    chosen = jnp.concatenate([lows * flag, lows * (1.0 - flag)], axis=0).astype(BF16)
    up = panel_a[...] + panel_b[...]
    first, second = part_lanes(meta, (1 - meta[2]) * 2, own.shape[0])
    total = part[...] + adapter_scale * dot_t(up, chosen)
    out[...] = (total + dot(w[:, first], own[...]) + dot(w[:, second], other[...])).astype(BF16)


def exchange_quarters(quarters):
    return [quarters[0]] + [lax.ppermute(quarters[s], "seq", [(j, j ^ s) for j in range(4)]) for s in (1, 2, 3)]


def share_quarter(total):
    beside = lax.ppermute(total, "seq", [(j, j ^ 1) for j in range(4)])
    middle = [(1, 2), (2, 1)]
    return [total, beside, lax.ppermute(total, "seq", middle), lax.ppermute(beside, "seq", middle)]


def per_device(
    tokens,
    query_matrix,
    key_matrix,
    value_matrix,
    output_matrix,
    query_gain,
    key_norm_gain,
    adapter_down,
    adapter_up_query,
    key_value_up_panels,
    adapter_out_down,
    adapter_out_up,
    request_of_block,
    adapter_of_request,
):
    rows, width = tokens.shape
    cols = query_matrix.shape[1]
    seq, rep, head = (lax.axis_index(name).astype(jnp.int32) for name in ("seq", "rep", "head"))
    meta = jnp.concatenate([jnp.stack([seq, rep, head]), adapter_of_request, request_of_block])
    tokens = tokens.T

    def across(value):
        return lax.ppermute(value, "head", SWAP)

    def core(value):
        return lax.ppermute(value, "rep", SWAP)

    def up(value, by=1):
        return lax.ppermute(value, "seq", [(i, (i + by) % 4) for i in range(4)])

    def after(value, *others):
        return lax.optimization_barrier((value, *others))[0]

    far_own = across(tokens)
    near_other = core(tokens)

    def swapped(value, by):
        return lax.ppermute(value, "seq", [(j, j ^ by) for j in range(4)])

    def pack(kernel, name, result, pools, order):
        return call(
            kernel,
            name,
            result,
            [SM] + [FAR] * len(pools),
            [adapter_of_request, *pools],
            [pltpu.VMEM(pool.shape, BF16) for pool in pools] + [pltpu.SemaphoreType.DMA((len(pools),))],
            after=order,
        )

    pools = [jnp.swapaxes(adapter_down, 1, 2), adapter_up_query, key_value_up_panels]
    quarters = pack(pack_kernel, "pack", (shape((64, width)),) * 4, pools, [])
    received = exchange_quarters(quarters)
    out_pools = [jnp.swapaxes(adapter_out_down, 1, 2), adapter_out_up]
    out_panel = pack(pack_out_kernel, "pack_out", shape((64, 1920)), out_pools, [quarters[0]])
    out_beside = swapped(out_panel, 1)

    chunks = rows // CHUNK
    weights = [query_matrix, key_matrix, value_matrix]
    weight_scratch = [
        pltpu.VMEM((2, width, 256), BF16),
        pltpu.VMEM((2, width, 256), BF16),
        pltpu.VMEM((2, width, cols), BF16),
        pltpu.SemaphoreType.DMA((3, 2)),
    ]
    weight_shapes = [(2, width, 256), (2, width, 256), (2, width, cols)]
    near0, near1, *far_weights = call(
        near_kernel,
        "near",
        (shape((CHUNK, 1024), F32),) * chunks + tuple(shape(dims) for dims in weight_shapes),
        [SM, VM, VM, FAR, FAR, FAR],
        [meta, tokens, near_other, *weights],
        [pltpu.VMEM(dims, BF16) for dims in weight_shapes] + [pltpu.SemaphoreType.DMA((3, 2))] * 2,
        after=[out_panel],
    )
    near = [near0, near1]

    def project(c, prior):
        mine = pl.BlockSpec((width, CHUNK), lambda i: (0, c))
        return call(
            far_kernel,
            "far",
            (shape((cols, CHUNK), F32), shape((512, CHUNK))),
            [VM, mine, mine, VM, VM, VM],
            [near[c], far_own, far_other, *far_weights],
            grid=(1,),
            after=[prior],
        )

    all_blocks = request_of_block.shape[0]
    window = jnp.arange(3 * rows, dtype=jnp.int32) + (seq - 2) * rows
    window = jnp.clip(window, 0, all_blocks * BLOCK - 1)
    second_start = jnp.sum((request_of_block < 1).astype(jnp.int32)) * BLOCK
    position = jnp.where(window >= second_start, window - second_start, window)
    half_dim = HEAD_SIZE // 2
    frequency = jnp.power(rope_base, -jnp.arange(half_dim, dtype=F32) * 2.0 / HEAD_SIZE)
    angles = frequency[:, None] * position.astype(F32)[None, :]
    cosine, sine = jnp.cos(angles), jnp.sin(angles)
    q_gain = query_gain.reshape(1, HEAD_SIZE)
    k_gain = key_norm_gain.reshape(1, HEAD_SIZE)

    quarter = call(sum_kernel, "sum", shape((64, width)), [VM] * 4, received, after=[near[0], cosine, sine])
    pieces = share_quarter(quarter)
    up_pair, down_pair = call(
        add_kernel,
        "out_add",
        (shape((64, width)), shape((64, cols))),
        [VM] * 2,
        [out_panel, out_beside],
        after=[quarter],
    )
    down_rest = swapped(down_pair, 2)
    far_other = core(after(far_own, pieces[1], pieces[2], down_pair))
    late_q, late_kv = project(1, pieces[1])
    early_q, early_kv = project(0, late_kv)
    partial_low, ups = call(
        low_kernel,
        "low",
        (shape((96, rows), F32), shape((64, 1024))),
        [SM] + [VM] * 5,
        [meta, tokens, *pieces],
        [pltpu.VMEM((4, 64, width), BF16)],
        after=[early_kv],
    )
    chip_low = partial_low + core(partial_low)
    low = chip_low + across(chip_low)

    prev_late, prev_early = up(late_kv), up(early_kv)
    low_kv = low[32:96].astype(BF16)
    low_prev = up(low_kv)
    low_prev2 = up(low_prev)
    prev2_late = up(after(prev_late, early_kv))

    shard_scratch = [pltpu.VMEM((rows, 256), BF16), pltpu.VMEM((256, rows), BF16)]
    sums = (shape((cols, rows), F32), shape((8, rows), F32))
    q_rot, num, den, out_weights = call(
        attend_own_kernel,
        "attend_own",
        (shape((cols, rows)), *sums, shape(output_matrix.T.shape)),
        [SM] + [VM] * 10 + [FAR],
        [meta, early_q, late_q, early_kv, late_kv, low, ups, q_gain, k_gain, cosine, sine, output_matrix.T],
        shard_scratch + [pltpu.SemaphoreType.DMA],
    )
    prev2_early = up(after(prev_early, low_prev, num))
    num, den = call(
        attend_prev_kernel,
        "attend_prev",
        sums,
        [SM] + [VM] * 10,
        [meta, q_rot, num, den, prev_early, prev_late, low_prev, ups, k_gain, cosine, sine],
        shard_scratch,
    )

    def attend_far(chunk, kept, order):
        return call(
            functools.partial(attend_far_kernel, chunk),
            "attend_far",
            shape((cols, CHUNK)),
            [SM] + [VM] * (8 + len(kept)),
            [meta, q_rot, num, den, *kept, low_prev2, ups, k_gain, cosine, sine],
            shard_scratch,
            after=order,
        )

    att_late = attend_far(1, [prev2_late], [down_rest])
    att_early = attend_far(0, [prev2_early, prev2_late], [att_late])

    up_rest = swapped(up_pair, 2)
    crossed = [(chunk, across(att)) for chunk, att in ((1, att_late), (0, att_early))]
    parts = []
    for att in (att_late, att_early):
        parts.append(
            call(
                out_near_kernel,
                "out_near",
                shape((width, CHUNK), F32),
                [SM] + [VM] * 3,
                [meta, att, core(att), out_weights],
                after=[att_early] + parts,
            )
        )
    out_low = call(
        out_low_kernel,
        "out_low",
        shape((32, rows), F32),
        [SM] + [VM] * 4,
        [meta, att_early, att_late, down_pair, down_rest],
        after=[parts[1]],
    )
    out_low = out_low + core(out_low)
    out_low = out_low + across(out_low)

    result = []
    for (chunk, att_far), part in zip(crossed, parts):
        result = [
            call(
                functools.partial(out_far_kernel, chunk),
                "out_far",
                shape((width, rows)),
                [SM] + [VM] * 7 + [HB] * len(result),
                [meta, att_far, core(after(att_far, out_low, up_rest)), out_weights, part, out_low, up_pair, up_rest, *result],
                out_specs=pl.BlockSpec((width, CHUNK), lambda i, chunk=chunk: (0, chunk)),
                grid=(1,),
                aliases={8: 0} if result else {},
            )
        ]
    return result[0].T


def plain_sizes(mesh):
    return mesh.shape["seq"] == 4 and mesh.shape["head"] == 2 and mesh.shape["rep"] == 2


def solution(mesh):
    return jax.shard_map(
        per_device if plain_sizes(mesh) else per_device_general,
        mesh=mesh,
        in_specs=(
            P(("groups", "seq"), ("head", "rep")),
            P(None, ("head", "rep")),
            P(None, "head"),
            P(None, "head"),
            P(None, ("head", "rep")),
            P(),
            P(),
            P("seq", ("head", "rep"), None),
            P("seq", None, ("head", "rep")),
            P("seq", None, None, "head"),
            P("seq", ("head", "rep"), None),
            P("seq", None, ("head", "rep")),
            P("groups"),
            P("groups"),
        ),
        out_specs=P(("groups", "seq"), ("head", "rep")),
        check_vma=False,
    )
```

```python
import functools
import math

import jax
import jax.numpy as jnp
from jax import lax
from jax.experimental import pallas as pl
from jax.experimental.pallas import tpu as pltpu
from jax.sharding import PartitionSpec as P

HEAD_SIZE = 128
ADAPTER_RANK = 32
KEY_WINDOW = 1024
BLOCK = 128


norm_epsilon = 1e-06
rope_base = 10000.0
score_scale = 168.0 ** (-0.5)
adapter_scale = 2.0


def shifted(value, axis, by):
    size = lax.axis_size(axis)
    pairs = [(i, i + by) for i in range(size) if 0 <= i + by < size]
    return lax.ppermute(value, axis, pairs)


def per_head_norm(values, scale_gain):
    mean_square = jnp.mean(values * values, axis=-1, keepdims=True)
    return values * lax.rsqrt(mean_square + norm_epsilon) * scale_gain


def rope_tables(positions, head_dim):
    half_dim = head_dim // 2
    frequency = jnp.power(rope_base, -jnp.arange(half_dim, dtype=jnp.float32) * 2.0 / head_dim)
    angles = positions.astype(jnp.float32)[:, None] * frequency[None, :]
    return (jnp.cos(angles), jnp.sin(angles))


def rotate_feature_pairs(values, cosine_table, sine_values):
    half_dim = values.shape[-1] // 2
    first_half = values[..., :half_dim]
    second_half = values[..., half_dim:]
    cosine_table = cosine_table[:, None, :]
    sine_values = sine_values[:, None, :]
    return jnp.concatenate(
        [
            first_half * cosine_table - second_half * sine_values,
            second_half * cosine_table + first_half * sine_values,
        ],
        axis=-1,
    )


def request_starts(block_requests, all_requests):
    earlier = (all_requests[None, :] < block_requests[:, None]).astype(jnp.int32)
    return jnp.sum(earlier, axis=1) * BLOCK


def per_device_general(
    tokens,
    query_matrix,
    key_matrix,
    value_matrix,
    output_matrix,
    query_gain,
    key_norm_gain,
    adapter_down,
    adapter_up_query,
    key_value_up_panels,
    adapter_out_down,
    adapter_out_up,
    request_of_block,
    adapter_of_request,
):
    tok_rows, width_part = tokens.shape
    query_cols = query_matrix.shape[1]
    key_cols = key_matrix.shape[1]
    query_heads = query_cols // HEAD_SIZE
    block_count = tok_rows // BLOCK
    all_blocks = request_of_block.shape[0]
    request_total = adapter_of_request.shape[0]
    seq_index = lax.axis_index("seq")
    rep_index = lax.axis_index("rep")
    first_row = seq_index * tok_rows
    own_requests = lax.dynamic_slice_in_dim(
        request_of_block, seq_index * block_count, block_count, 0
    )
    request_match = own_requests[:, None] == jnp.arange(request_total, dtype=jnp.int32)[None, :]
    own_adapters = jnp.sum(jnp.where(request_match, adapter_of_request[None, :], 0), axis=1)
    pool_part = (
        lax.all_gather(adapter_down, "seq", axis=0, tiled=True),
        lax.all_gather(adapter_up_query, "seq", axis=0, tiled=True),
        lax.all_gather(key_value_up_panels, "seq", axis=0, tiled=True),
        lax.all_gather(adapter_out_down, "seq", axis=0, tiled=True),
        lax.all_gather(adapter_out_up, "seq", axis=0, tiled=True),
    )
    held_count = pool_part[0].shape[0]
    select = (own_adapters[:, None] == jnp.arange(held_count, dtype=jnp.int32)[None, :]).astype(
        jnp.bfloat16
    )
    (
        picked_down_panels,
        picked_query_panels,
        picked_key_panels,
        chosen_out_down,
        picked_output_up,
    ) = tuple(
        (
            jnp.einsum(
                "bn,n...->b...", select, panel_part, preferred_element_type=jnp.float32
            ).astype(jnp.bfloat16)
            for panel_part in pool_part
        )
    )
    token_block_list = tokens.reshape(block_count, BLOCK, width_part)
    partial_low = jnp.einsum(
        "myj,mjc->myc", token_block_list, picked_down_panels, preferred_element_type=jnp.float32
    ).reshape(tok_rows, 3 * ADAPTER_RANK)
    reduced_rank_rows = (
        lax.psum(partial_low, ("head", "rep"))
        .astype(jnp.bfloat16)
        .reshape(block_count, BLOCK, 3 * ADAPTER_RANK)
    )
    feature_part = lax.all_gather(tokens, ("head", "rep"), axis=1, tiled=True)
    query_add = jnp.dot(feature_part, query_matrix, preferred_element_type=jnp.float32)
    key_add = jnp.dot(feature_part, key_matrix, preferred_element_type=jnp.float32)
    value_add = jnp.dot(feature_part, value_matrix, preferred_element_type=jnp.float32)
    query_linear = query_add
    key_linear = key_add
    value_linear = value_add
    query_linear = query_linear + adapter_scale * jnp.einsum(
        "tlq,tqo->tlo",
        reduced_rank_rows[..., :ADAPTER_RANK],
        picked_query_panels,
        preferred_element_type=jnp.float32,
    ).reshape(tok_rows, query_cols)
    key_linear = key_linear + adapter_scale * jnp.einsum(
        "tlq,tqo->tlo",
        reduced_rank_rows[..., ADAPTER_RANK : 2 * ADAPTER_RANK],
        picked_key_panels[:, 0],
        preferred_element_type=jnp.float32,
    ).reshape(tok_rows, key_cols)
    value_linear = value_linear + adapter_scale * jnp.einsum(
        "tlq,tqo->tlo",
        reduced_rank_rows[..., 2 * ADAPTER_RANK :],
        picked_key_panels[:, 1],
        preferred_element_type=jnp.float32,
    ).reshape(tok_rows, key_cols)
    key_full = key_linear.astype(jnp.bfloat16)
    value_full = value_linear.astype(jnp.bfloat16)
    key_heads = key_cols // HEAD_SIZE
    token_index = first_row + jnp.arange(tok_rows, dtype=jnp.int32)
    token_request = jnp.repeat(own_requests, BLOCK)
    token_start = jnp.repeat(request_starts(own_requests, request_of_block), BLOCK)
    cosine_table, sine_values = rope_tables(token_index - token_start, HEAD_SIZE)
    query_rows = (
        rotate_feature_pairs(
            per_head_norm(query_linear.reshape(tok_rows, query_heads, HEAD_SIZE), query_gain),
            cosine_table,
            sine_values,
        )
        * score_scale
    ).astype(jnp.bfloat16)
    rotated_keys = rotate_feature_pairs(
        per_head_norm(
            key_full.astype(jnp.float32).reshape(tok_rows, key_heads, HEAD_SIZE), key_norm_gain
        ),
        cosine_table,
        sine_values,
    ).astype(jnp.bfloat16)
    group_heads = max(query_heads // 2, 1)
    group_size = query_heads // group_heads
    head_first = rep_index * query_heads // 2
    keys_used = lax.dynamic_slice_in_dim(rotated_keys, head_first, group_heads, 1).reshape(
        tok_rows, group_heads * HEAD_SIZE
    )
    values_used = lax.dynamic_slice_in_dim(
        value_full.reshape(tok_rows, key_heads, HEAD_SIZE), head_first, group_heads, 1
    ).reshape(tok_rows, group_heads * HEAD_SIZE)
    query_groups = query_rows.reshape(tok_rows, group_heads, group_size, HEAD_SIZE)
    block_table = jnp.arange(all_blocks, dtype=jnp.int32)
    empty_state = (
        jnp.zeros((tok_rows, group_heads, group_size, HEAD_SIZE), jnp.float32),
        jnp.zeros((group_heads, group_size, tok_rows), jnp.float32),
    )
    reach_blocks = KEY_WINDOW // tok_rows
    stacked = jnp.stack((keys_used, values_used))
    earlier = []
    for step_back in range(reach_blocks, 0, -1):
        earlier.append(shifted(stacked, "seq", step_back))
    window_stack = jnp.concatenate(earlier + [stacked], axis=1)
    fold_state = empty_state
    offset = first_row - reach_blocks * tok_rows
    key_block = window_stack[0]
    value_block = window_stack[1]
    key_length = key_block.shape[0]
    step_length = math.gcd(key_length, 512)
    steps_count = key_length // step_length
    key_steps = key_block.reshape(steps_count, step_length, group_heads, HEAD_SIZE)
    value_steps = value_block.reshape(steps_count, step_length, group_heads, HEAD_SIZE)

    def one_step(carry_state, step_inputs):
        step_keys, step_values, step_index = step_inputs
        key_position = offset + step_index * step_length + jnp.arange(step_length, dtype=jnp.int32)
        key_block_id = jnp.clip(key_position, 0, all_blocks * BLOCK - 1) // BLOCK
        key_request = jnp.sum(
            jnp.where(key_block_id[:, None] == block_table[None, :], request_of_block[None, :], 0),
            axis=1,
        )
        distance = token_index[:, None] - key_position[None, :]
        allowed = (
            (key_position[None, :] >= 0)
            & (distance >= 0)
            & (distance < KEY_WINDOW)
            & (token_request[:, None] == key_request[None, :])
        )
        scores = jnp.einsum(
            "tcpd,kcd->cptk", query_groups, step_keys, preferred_element_type=jnp.float32
        )
        weights = jnp.where(allowed[None, None], jnp.exp(scores), 0.0)
        numerator, denominator = carry_state
        denominator = denominator + jnp.sum(weights, axis=-1)
        numerator = numerator + jnp.einsum(
            "cptk,kcd->tcpd",
            weights.astype(jnp.bfloat16),
            step_values,
            preferred_element_type=jnp.float32,
        )
        return ((numerator, denominator), None)

    fold_state, unused_out = lax.scan(
        one_step, fold_state, (key_steps, value_steps, jnp.arange(steps_count, dtype=jnp.int32))
    )
    numerator, denominator = fold_state
    attention_result = (
        (numerator / jnp.transpose(denominator, (2, 0, 1))[..., None])
        .astype(jnp.bfloat16)
        .reshape(tok_rows, query_cols)
    )
    output_zero = (
        jnp.zeros((tok_rows, width_part), jnp.float32),
        jnp.zeros((tok_rows, ADAPTER_RANK), jnp.float32),
    )
    projected_rows = jnp.dot(
        lax.all_gather(attention_result, ("head", "rep"), axis=1, tiled=True),
        output_matrix,
        preferred_element_type=jnp.float32,
    )
    projected_rows, lowered = (projected_rows, output_zero[1])
    local_low = jnp.einsum(
        "bkc,bcr->bkr",
        attention_result.reshape(block_count, BLOCK, query_cols),
        chosen_out_down,
        preferred_element_type=jnp.float32,
    ).reshape(tok_rows, ADAPTER_RANK)
    output_reduced_rank = lax.psum(local_low, ("head", "rep")).astype(jnp.bfloat16)
    result = projected_rows + adapter_scale * jnp.einsum(
        "zch,zhp->zcp",
        output_reduced_rank.reshape(block_count, BLOCK, ADAPTER_RANK),
        picked_output_up,
        preferred_element_type=jnp.float32,
    ).reshape(tok_rows, width_part)
    return result.astype(jnp.bfloat16)


F32 = jnp.float32
BF16 = jnp.bfloat16
VMEM_SMALL = 20 * 1024 * 1024
VMEM_LARGE = 56 * 1024 * 1024
SWAP = [(0, 1), (1, 0)]
SHARD_BLOCKS = 4
CHUNK = 256
CHUNK_BLOCKS = CHUNK // BLOCK
META_ADAPTER = 3
META_REQUEST = 5


def dot(a, b):
    return lax.dot_general(a, b, (((1,), (0,)), ((), ())), preferred_element_type=F32)


def dot_t(a, b):
    return lax.dot_general(a, b, (((0,), (0,)), ((), ())), preferred_element_type=F32)


VM = pl.BlockSpec(memory_space=pltpu.VMEM)
SM = pl.BlockSpec(memory_space=pltpu.SMEM)
HB = pl.BlockSpec(memory_space=pl.ANY)
FAR = pl.BlockSpec(memory_space=pltpu.HBM)


def in_hbm(value):
    return pltpu.with_memory_space_constraint(value, pltpu.HBM)


def shape(dims, dtype=BF16):
    return jax.ShapeDtypeStruct(dims, dtype)


def call(kernel, name, out_shape, in_specs, args, scratch=(), out_specs=None, grid=None, after=(), aliases=None):
    count = len(in_specs)

    def body(*refs):
        kernel(*refs[:count], *refs[count + len(after) :])

    outs = out_specs
    if outs is None:
        outs = VM if isinstance(out_shape, jax.ShapeDtypeStruct) else tuple(VM for _ in out_shape)
    more = dict(grid=grid) if grid else {}
    return pl.pallas_call(
        body,
        out_shape=out_shape,
        in_specs=list(in_specs) + [HB] * len(after),
        out_specs=outs,
        scratch_shapes=list(scratch),
        input_output_aliases=aliases or {},
        compiler_params=pltpu.CompilerParams(vmem_limit_bytes=VMEM_SMALL),
        cost_estimate=pl.CostEstimate(flops=1000, bytes_accessed=1000, transcendentals=0),
        name=name,
        **more,
    )(*[in_hbm(a) if spec is FAR else a for a, spec in zip(args, in_specs)], *after)


def picked(adapters, held):
    me = lax.axis_index("seq").astype(jnp.int32)
    chosen = []
    for step in range(4):
        quarter = jnp.bitwise_xor(me, step)
        slot = adapters[lax.div(quarter, 2)] - me * held
        here = jnp.logical_and(slot >= 0, slot < held)
        keep = jnp.where(here, 1.0, 0.0).astype(F32)
        chosen.append((jnp.clip(slot, 0, held - 1), keep, lax.rem(quarter, 2)))
    return chosen


def bring(sources, targets, sems):
    copies = [pltpu.make_async_copy(a, b, sems.at[i]) for i, (a, b) in enumerate(zip(sources, targets))]
    for copy in copies:
        copy.start()
    for copy in copies:
        copy.wait()


def pack_kernel(adapters, down_far, up_q_far, up_kv_far, *refs):
    quarters, (down, up_q, up_kv, sems) = refs[:4], refs[4:]
    bring((down_far, up_q_far, up_kv_far), (down, up_q, up_kv), sems)
    rep = lax.axis_index("rep").astype(jnp.int32)
    half = up_kv.shape[3] // 2
    cols = up_q.shape[2]
    width = down.shape[2]
    for (slot, keep, part), out in zip(picked(adapters, down.shape[0]), quarters):
        rows = pl.ds(pl.multiple_of(part * 48, 16), 48)
        ranks = pl.ds(pl.multiple_of(part * 16, 16), 16)
        out[0:48, :] = (down[slot, rows, :].astype(F32) * keep).astype(BF16)
        out[48:64, 0:cols] = (up_q[slot, ranks, :].astype(F32) * keep).astype(BF16)
        for which in range(2):
            both = up_kv[slot, which, ranks, :].astype(F32) * keep
            mine = jnp.where(rep == 0, both[:, :half], both[:, half:])
            out[48:64, cols + which * half : cols + (which + 1) * half] = mine.astype(BF16)
        out[48:64, 1024:width] = jnp.zeros((16, width - 1024), BF16)


def pack_out_kernel(adapters, out_down_far, out_up_far, out, out_down, out_up, sems):
    bring((out_down_far, out_up_far), (out_down, out_up), sems)
    width = out_up.shape[2]
    held = out_up.shape[0]
    for request in range(2):
        slot = adapters[request] - lax.axis_index("seq").astype(jnp.int32) * held
        here = jnp.logical_and(slot >= 0, slot < held)
        keep = jnp.where(here, 1.0, 0.0).astype(F32)
        slot = jnp.clip(slot, 0, held - 1)
        rows = slice(request * 32, (request + 1) * 32)
        out[rows, 0:width] = (out_up[slot].astype(F32) * keep).astype(BF16)
        out[rows, width:1408] = jnp.zeros((32, 1408 - width), BF16)
        out[rows, 1408:1920] = (out_down[slot].astype(F32) * keep).astype(BF16)


def add_kernel(a, b, up, down):
    width = up.shape[1]
    up[...] = a[:, 0:width] + b[:, 0:width]
    down[...] = a[:, 1408:1920] + b[:, 1408:1920]


def sum_kernel(a, b, c, d, out):
    out[...] = a[...] + b[...] + c[...] + d[...]


def place_quarters(meta, quarters, panel):
    me = meta[0]
    low_side = me < 2
    at = (me, jnp.bitwise_xor(me, 1), jnp.where(low_side, 2, 1), jnp.where(low_side, 3, 0))
    for index, quarter in zip(at, quarters):
        panel[index] = quarter[...]


def low_kernel(meta, tokens, p0, p1, p2, p3, low_t, ups, panel):
    place_quarters(meta, (p0, p1, p2, p3), panel)
    down = jnp.concatenate([panel[j, 0:48, :] for j in range(4)], axis=0)
    both = dot(down, tokens[...])
    for b in range(SHARD_BLOCKS):
        request = meta[META_REQUEST + meta[0] * SHARD_BLOCKS + b]
        at = slice(b * BLOCK, (b + 1) * BLOCK)
        fa = jnp.where(request == 0, 1.0, 0.0).astype(F32)
        low_t[:, at] = both[0:96, at] * fa + both[96:192, at] * (1.0 - fa)
    ups[...] = jnp.concatenate([panel[j, 48:64, 0:1024] for j in range(4)], axis=0)


def weight_copies(meta, weights, buffers, sems, chip, width):
    half = weights[0].shape[1] // 2
    lane = pl.ds(pl.multiple_of(meta[1] * half, BLOCK), half)
    copies = []
    for i, (w, buf) in enumerate(zip(weights, buffers)):
        lanes = lane if i < 2 else slice(None)
        for n, part in enumerate((chip + meta[1], chip + 1 - meta[1])):
            rows = pl.ds(pl.multiple_of(part * width, 16), width)
            copies.append(pltpu.make_async_copy(w.at[rows, lanes], buf.at[n], sems.at[i, n]))
    return copies


WEIGHT_AT = (slice(0, 256), slice(256, 512), slice(512, 1024))


def near_kernel(meta, own, other, wq, wk, wv, out0, out1, fk, fv, fq, bk, bv, bq, sems, far_sems):
    weights = (wk, wv, wq)
    width = other.shape[0]
    copies = weight_copies(meta, weights, (bk, bv, bq), sems, meta[2] * 2, width)
    later = weight_copies(meta, weights, (fk, fv, fq), far_sems, (1 - meta[2]) * 2, width)
    for copy in copies:
        copy.start()
    for i, (at, buf) in enumerate(zip(WEIGHT_AT, (bk, bv, bq))):
        copies[2 * i].wait()
        copies[2 * i + 1].wait()
        if i == 1:
            for copy in later:
                copy.start()
        for c, out in enumerate((out0, out1)):
            tok = slice(c * CHUNK, (c + 1) * CHUNK)
            out[:, at] = dot_t(own[:, tok], buf[0]) + dot_t(other[:, tok], buf[1])
    for copy in later:
        copy.wait()


def far_kernel(part, own, other, wk, wv, wq, q_out, kv_out):
    for i, (at, w) in enumerate(zip(WEIGHT_AT, (wk, wv, wq))):
        turned = jnp.transpose(part[:, at] + dot_t(own[...], w[0]) + dot_t(other[...], w[1]))
        if i == 2:
            q_out[...] = turned
        else:
            kv_out[at, :] = turned.astype(BF16)


def block_request(meta, block):
    return meta[META_REQUEST + jnp.maximum(block, 0)]


def by_request(meta, low, first_block):
    flags = []
    for b in range(SHARD_BLOCKS):
        request = block_request(meta, first_block + b)
        flags.append(jnp.full((1, BLOCK), jnp.where(request == 0, 1.0, 0.0).astype(F32)))
    flag = jnp.concatenate(flags, axis=1)
    rows = low.astype(BF16).astype(F32)
    return jnp.concatenate([rows * flag, rows * (1.0 - flag)], axis=0).astype(BF16)


def norm_rotate(x, gain, cosine, sine):
    mean_square = jnp.mean(x * x, axis=0, keepdims=True)
    u = x * lax.rsqrt(mean_square + norm_epsilon) * gain
    a = u[0:64]
    b = u[64:128]
    return jnp.concatenate([a * cosine - b * sine, b * cosine + a * sine], axis=0)


def gain_rows(gain):
    return jnp.transpose(jnp.broadcast_to(gain[...], (HEAD_SIZE, HEAD_SIZE)))


def finish_keys(meta, chunks, low_k, low_v, ups, gain, cosine, sine, keys, values, first, blocks):
    base = (meta[0] - 2) * SHARD_BLOCKS + first
    k_term = dot_t(ups[:, 512:768], by_request(meta, low_k, base))
    v_term = dot_t(ups[:, 768:1024], by_request(meta, low_v, base))
    for b in blocks:
        at = slice((first + b) * BLOCK, (first + b + 1) * BLOCK)
        here = slice(b * BLOCK, (b + 1) * BLOCK)
        chunk = chunks[b // CHUNK_BLOCKS]
        lanes = slice(b % CHUNK_BLOCKS * BLOCK, (b % CHUNK_BLOCKS + 1) * BLOCK)
        for g in range(2):
            head = slice(g * HEAD_SIZE, (g + 1) * HEAD_SIZE)
            k = chunk[head, lanes].astype(F32) + adapter_scale * k_term[head, here]
            k = k.astype(BF16).astype(F32)
            turned = norm_rotate(k, gain, cosine[:, at], sine[:, at])
            keys[here, head] = jnp.transpose(turned).astype(BF16)
        values[:, here] = (chunk[256:512, lanes].astype(F32) + adapter_scale * v_term[:, here]).astype(BF16)


def attend(meta, q_rot, keys, values, c, g, first, low_block, high_block):
    rows = slice(c * BLOCK, (c + 1) * BLOCK)
    heads = [slice((2 * g + h) * HEAD_SIZE, (2 * g + h + 1) * HEAD_SIZE) for h in range(2)]
    q = jnp.concatenate([q_rot[head, rows] for head in heads], axis=1)
    base = (meta[0] - 2) * SHARD_BLOCKS
    mine = block_request(meta, base + 8 + c)
    head = slice(g * HEAD_SIZE, (g + 1) * HEAD_SIZE)
    at = slice(low_block * BLOCK, (high_block + 1) * BLOCK)
    scores = dot(keys[at, head], q)
    key = lax.broadcasted_iota(jnp.int32, (BLOCK, 2 * BLOCK), 0)
    query = jnp.bitwise_and(lax.broadcasted_iota(jnp.int32, (BLOCK, 2 * BLOCK), 1), BLOCK - 1)
    den = jnp.zeros((BLOCK, 2 * BLOCK), F32)
    pieces = []
    for j in range(low_block, high_block + 1):
        block = base + first + j
        ok = jnp.logical_and(block >= 0, block_request(meta, block) == mine)
        piece = jnp.exp(scores[(j - low_block) * BLOCK : (j - low_block + 1) * BLOCK])
        piece = piece * jnp.where(ok, 1.0, 0.0).astype(F32)
        if first + j == c + 8:
            piece = jnp.where(query >= key, piece, 0.0)
        if first + j == c:
            piece = jnp.where(query < key, piece, 0.0)
        den = den + piece
        pieces.append(piece.astype(BF16))
    num = dot(values[head, at], jnp.concatenate(pieces, axis=0))
    return num, jnp.sum(den, axis=0, keepdims=True)


def attend_own_kernel(
    meta, q0, q1, o0, o1, low, ups, q_gain, k_gain, cosine, sine, weights,
    q_rot, num_out, den_out, weights_out, keys, values, sem,
):
    fetch = pltpu.make_async_copy(weights, weights_out, sem)
    fetch.start()
    finish_keys(
        meta, (o0, o1), low[32:64, :], low[64:96, :], ups, gain_rows(k_gain), cosine, sine, keys, values, 8, range(4)
    )
    gain = gain_rows(q_gain)
    q_term = dot_t(ups[:, 0:512], by_request(meta, low[0:32, :], meta[0] * SHARD_BLOCKS))
    for c in range(SHARD_BLOCKS):
        q = (q0, q1)[c // CHUNK_BLOCKS]
        lanes = slice(c % CHUNK_BLOCKS * BLOCK, (c % CHUNK_BLOCKS + 1) * BLOCK)
        rows = slice(c * BLOCK, (c + 1) * BLOCK)
        at = slice((8 + c) * BLOCK, (9 + c) * BLOCK)
        for h in range(4):
            head = slice(h * HEAD_SIZE, (h + 1) * HEAD_SIZE)
            x = q[head, lanes] + adapter_scale * q_term[head, rows]
            q_rot[head, rows] = (norm_rotate(x, gain, cosine[:, at], sine[:, at]) * score_scale).astype(BF16)
    for g in range(2):
        for c in range(SHARD_BLOCKS):
            rows = slice(c * BLOCK, (c + 1) * BLOCK)
            num, den = attend(meta, q_rot, keys, values, c, g, 8, 0, c)
            for h in range(2):
                n = 2 * g + h
                part = slice(h * BLOCK, (h + 1) * BLOCK)
                num_out[n * HEAD_SIZE : (n + 1) * HEAD_SIZE, rows] = num[:, part]
                den_out[n : n + 1, rows] = den[:, part]
    fetch.wait()


def attend_prev_kernel(
    meta, q_rot, num_in, den_in, h0, h1, low_h, ups, k_gain, cosine, sine, num_out, den_out, keys, values
):
    finish_keys(
        meta, (h0, h1), low_h[0:32, :], low_h[32:64, :], ups, gain_rows(k_gain), cosine, sine, keys, values, 4, range(4)
    )
    for g in range(2):
        for c in range(SHARD_BLOCKS):
            rows = slice(c * BLOCK, (c + 1) * BLOCK)
            num, den = attend(meta, q_rot, keys, values, c, g, 4, 0, 3)
            for h in range(2):
                n = 2 * g + h
                part = slice(h * BLOCK, (h + 1) * BLOCK)
                head = slice(n * HEAD_SIZE, (n + 1) * HEAD_SIZE)
                num_out[head, rows] = num_in[head, rows] + num[:, part]
                den_out[n : n + 1, rows] = den_in[n : n + 1, rows] + den[:, part]


def attend_far_kernel(chunk, meta, q_rot, num_in, den_in, *refs):
    count = CHUNK_BLOCKS - chunk
    kept, (low_h, ups, k_gain, cosine, sine, out, keys, values) = refs[:count], refs[count:]
    blocks = range(chunk * CHUNK_BLOCKS, SHARD_BLOCKS)
    finish_keys(
        meta, (None,) * chunk + tuple(kept), low_h[0:32, :], low_h[32:64, :], ups, gain_rows(k_gain), cosine, sine,
        keys, values, 0, blocks,
    )
    for g in range(2):
        for c in range(chunk * CHUNK_BLOCKS, (chunk + 1) * CHUNK_BLOCKS):
            rows = slice(c * BLOCK, (c + 1) * BLOCK)
            here = slice(c % CHUNK_BLOCKS * BLOCK, (c % CHUNK_BLOCKS + 1) * BLOCK)
            num, den = attend(meta, q_rot, keys, values, c, g, 0, c, 3)
            for h in range(2):
                n = 2 * g + h
                part = slice(h * BLOCK, (h + 1) * BLOCK)
                head = slice(n * HEAD_SIZE, (n + 1) * HEAD_SIZE)
                total = den_in[n : n + 1, rows] + den[:, part]
                out[head, here] = ((num_in[head, rows] + num[:, part]) / total).astype(BF16)


def request_flag(meta):
    flags = []
    for b in range(SHARD_BLOCKS):
        request = block_request(meta, meta[0] * SHARD_BLOCKS + b)
        flags.append(jnp.full((1, BLOCK), jnp.where(request == 0, 1.0, 0.0).astype(F32)))
    return jnp.concatenate(flags, axis=1)


def out_low_kernel(meta, att0, att1, panel_a, panel_b, low):
    down = panel_a[...] + panel_b[...]
    both = jnp.concatenate([dot(down, att0[...]), dot(down, att1[...])], axis=1)
    flag = request_flag(meta)
    low[...] = both[0:32] * flag + both[32:64] * (1.0 - flag)


def part_lanes(meta, chip, cols):
    return [pl.ds(pl.multiple_of(p * cols, BLOCK), cols) for p in (chip + meta[1], chip + 1 - meta[1])]


def out_near_kernel(meta, own, other, w, part):
    first, second = part_lanes(meta, meta[2] * 2, own.shape[0])
    part[...] = dot(w[:, first], own[...]) + dot(w[:, second], other[...])


def out_far_kernel(chunk, meta, own, other, w, part, low, panel_a, panel_b, *refs):
    out = refs[-1]
    tok = slice(chunk * CHUNK, (chunk + 1) * CHUNK)
    lows = low[:, tok].astype(BF16).astype(F32)
    flag = request_flag(meta)[:, tok]
    chosen = jnp.concatenate([lows * flag, lows * (1.0 - flag)], axis=0).astype(BF16)
    up = panel_a[...] + panel_b[...]
    first, second = part_lanes(meta, (1 - meta[2]) * 2, own.shape[0])
    total = part[...] + adapter_scale * dot_t(up, chosen)
    out[...] = (total + dot(w[:, first], own[...]) + dot(w[:, second], other[...])).astype(BF16)


def exchange_quarters(quarters):
    return [quarters[0]] + [lax.ppermute(quarters[s], "seq", [(j, j ^ s) for j in range(4)]) for s in (1, 2, 3)]


def share_quarter(total):
    beside = lax.ppermute(total, "seq", [(j, j ^ 1) for j in range(4)])
    middle = [(1, 2), (2, 1)]
    return [total, beside, lax.ppermute(total, "seq", middle), lax.ppermute(beside, "seq", middle)]


def per_device(
    tokens,
    query_matrix,
    key_matrix,
    value_matrix,
    output_matrix,
    query_gain,
    key_norm_gain,
    adapter_down,
    adapter_up_query,
    key_value_up_panels,
    adapter_out_down,
    adapter_out_up,
    request_of_block,
    adapter_of_request,
):
    rows, width = tokens.shape
    cols = query_matrix.shape[1]
    seq, rep, head = (lax.axis_index(name).astype(jnp.int32) for name in ("seq", "rep", "head"))
    meta = jnp.concatenate([jnp.stack([seq, rep, head]), adapter_of_request, request_of_block])
    tokens = tokens.T

    def across(value):
        return lax.ppermute(value, "head", SWAP)

    def core(value):
        return lax.ppermute(value, "rep", SWAP)

    def up(value, by=1):
        return lax.ppermute(value, "seq", [(i, (i + by) % 4) for i in range(4)])

    def after(value, *others):
        return lax.optimization_barrier((value, *others))[0]

    far_own = across(tokens)
    near_other = core(tokens)

    def swapped(value, by):
        return lax.ppermute(value, "seq", [(j, j ^ by) for j in range(4)])

    def pack(kernel, name, result, pools, order):
        return call(
            kernel,
            name,
            result,
            [SM] + [FAR] * len(pools),
            [adapter_of_request, *pools],
            [pltpu.VMEM(pool.shape, BF16) for pool in pools] + [pltpu.SemaphoreType.DMA((len(pools),))],
            after=order,
        )

    pools = [jnp.swapaxes(adapter_down, 1, 2), adapter_up_query, key_value_up_panels]
    quarters = pack(pack_kernel, "pack", (shape((64, width)),) * 4, pools, [])
    received = exchange_quarters(quarters)
    out_pools = [jnp.swapaxes(adapter_out_down, 1, 2), adapter_out_up]
    out_panel = pack(pack_out_kernel, "pack_out", shape((64, 1920)), out_pools, [quarters[0]])
    out_beside = swapped(out_panel, 1)

    chunks = rows // CHUNK
    weights = [query_matrix, key_matrix, value_matrix]
    weight_scratch = [
        pltpu.VMEM((2, width, 256), BF16),
        pltpu.VMEM((2, width, 256), BF16),
        pltpu.VMEM((2, width, cols), BF16),
        pltpu.SemaphoreType.DMA((3, 2)),
    ]
    weight_shapes = [(2, width, 256), (2, width, 256), (2, width, cols)]
    near0, near1, *far_weights = call(
        near_kernel,
        "near",
        (shape((CHUNK, 1024), F32),) * chunks + tuple(shape(dims) for dims in weight_shapes),
        [SM, VM, VM, FAR, FAR, FAR],
        [meta, tokens, near_other, *weights],
        [pltpu.VMEM(dims, BF16) for dims in weight_shapes] + [pltpu.SemaphoreType.DMA((3, 2))] * 2,
        after=[out_panel],
    )
    near = [near0, near1]

    def project(c, prior):
        mine = pl.BlockSpec((width, CHUNK), lambda i: (0, c))
        return call(
            far_kernel,
            "far",
            (shape((cols, CHUNK), F32), shape((512, CHUNK))),
            [VM, mine, mine, VM, VM, VM],
            [near[c], far_own, far_other, *far_weights],
            grid=(1,),
            after=[prior],
        )

    all_blocks = request_of_block.shape[0]
    window = jnp.arange(3 * rows, dtype=jnp.int32) + (seq - 2) * rows
    window = jnp.clip(window, 0, all_blocks * BLOCK - 1)
    second_start = jnp.sum((request_of_block < 1).astype(jnp.int32)) * BLOCK
    position = jnp.where(window >= second_start, window - second_start, window)
    half_dim = HEAD_SIZE // 2
    frequency = jnp.power(rope_base, -jnp.arange(half_dim, dtype=F32) * 2.0 / HEAD_SIZE)
    angles = frequency[:, None] * position.astype(F32)[None, :]
    cosine, sine = jnp.cos(angles), jnp.sin(angles)
    q_gain = query_gain.reshape(1, HEAD_SIZE)
    k_gain = key_norm_gain.reshape(1, HEAD_SIZE)

    quarter = call(sum_kernel, "sum", shape((64, width)), [VM] * 4, received, after=[near[0], cosine, sine])
    pieces = share_quarter(quarter)
    up_pair, down_pair = call(
        add_kernel,
        "out_add",
        (shape((64, width)), shape((64, cols))),
        [VM] * 2,
        [out_panel, out_beside],
        after=[quarter],
    )
    down_rest = swapped(down_pair, 2)
    far_other = core(after(far_own, pieces[1], pieces[2], down_pair))
    late_q, late_kv = project(1, pieces[1])
    early_q, early_kv = project(0, late_kv)
    partial_low, ups = call(
        low_kernel,
        "low",
        (shape((96, rows), F32), shape((64, 1024))),
        [SM] + [VM] * 5,
        [meta, tokens, *pieces],
        [pltpu.VMEM((4, 64, width), BF16)],
        after=[early_kv],
    )
    chip_low = partial_low + core(partial_low)
    low = chip_low + across(chip_low)

    prev_late, prev_early = up(late_kv), up(early_kv)
    low_kv = low[32:96].astype(BF16)
    low_prev = up(low_kv)
    low_prev2 = up(low_prev)
    prev2_late = up(after(prev_late, early_kv))

    shard_scratch = [pltpu.VMEM((rows, 256), BF16), pltpu.VMEM((256, rows), BF16)]
    sums = (shape((cols, rows), F32), shape((8, rows), F32))
    q_rot, num, den, out_weights = call(
        attend_own_kernel,
        "attend_own",
        (shape((cols, rows)), *sums, shape(output_matrix.T.shape)),
        [SM] + [VM] * 10 + [FAR],
        [meta, early_q, late_q, early_kv, late_kv, low, ups, q_gain, k_gain, cosine, sine, output_matrix.T],
        shard_scratch + [pltpu.SemaphoreType.DMA],
    )
    prev2_early = up(after(prev_early, low_prev, num))
    num, den = call(
        attend_prev_kernel,
        "attend_prev",
        sums,
        [SM] + [VM] * 10,
        [meta, q_rot, num, den, prev_early, prev_late, low_prev, ups, k_gain, cosine, sine],
        shard_scratch,
    )

    def attend_far(chunk, kept, order):
        return call(
            functools.partial(attend_far_kernel, chunk),
            "attend_far",
            shape((cols, CHUNK)),
            [SM] + [VM] * (8 + len(kept)),
            [meta, q_rot, num, den, *kept, low_prev2, ups, k_gain, cosine, sine],
            shard_scratch,
            after=order,
        )

    att_late = attend_far(1, [prev2_late], [])
    att_early = attend_far(0, [prev2_early, prev2_late], [att_late, down_rest])

    up_rest = swapped(up_pair, 2)
    crossed = [(chunk, across(att)) for chunk, att in ((1, att_late), (0, att_early))]
    parts = []
    for att in (att_late, att_early):
        parts.append(
            call(
                out_near_kernel,
                "out_near",
                shape((width, CHUNK), F32),
                [SM] + [VM] * 3,
                [meta, att, core(att), out_weights],
                after=[att_early] + parts,
            )
        )
    out_low = call(
        out_low_kernel,
        "out_low",
        shape((32, rows), F32),
        [SM] + [VM] * 4,
        [meta, att_early, att_late, down_pair, down_rest],
        after=[parts[1]],
    )
    out_low = out_low + core(out_low)
    out_low = out_low + across(out_low)

    result = []
    for (chunk, att_far), part in zip(crossed, parts):
        result = [
            call(
                functools.partial(out_far_kernel, chunk),
                "out_far",
                shape((width, rows)),
                [SM] + [VM] * 7 + [HB] * len(result),
                [meta, att_far, core(after(att_far, out_low, up_rest)), out_weights, part, out_low, up_pair, up_rest, *result],
                out_specs=pl.BlockSpec((width, CHUNK), lambda i, chunk=chunk: (0, chunk)),
                grid=(1,),
                aliases={8: 0} if result else {},
            )
        ]
    return result[0].T


def plain_sizes(mesh):
    return mesh.shape["seq"] == 4 and mesh.shape["head"] == 2 and mesh.shape["rep"] == 2


def solution(mesh):
    return jax.shard_map(
        per_device if plain_sizes(mesh) else per_device_general,
        mesh=mesh,
        in_specs=(
            P(("groups", "seq"), ("head", "rep")),
            P(None, ("head", "rep")),
            P(None, "head"),
            P(None, "head"),
            P(None, ("head", "rep")),
            P(),
            P(),
            P("seq", ("head", "rep"), None),
            P("seq", None, ("head", "rep")),
            P("seq", None, None, "head"),
            P("seq", ("head", "rep"), None),
            P("seq", None, ("head", "rep")),
            P("groups"),
            P("groups"),
        ),
        out_specs=P(("groups", "seq"), ("head", "rep")),
        check_vma=False,
    )
```

```python
import functools
import math

import jax
import jax.numpy as jnp
from jax import lax
from jax.experimental import pallas as pl
from jax.experimental.pallas import tpu as pltpu
from jax.sharding import PartitionSpec as P

HEAD_SIZE = 128
ADAPTER_RANK = 32
KEY_WINDOW = 1024
BLOCK = 128


norm_epsilon = 1e-06
rope_base = 10000.0
score_scale = 168.0 ** (-0.5)
adapter_scale = 2.0


def shifted(value, axis, by):
    size = lax.axis_size(axis)
    pairs = [(i, i + by) for i in range(size) if 0 <= i + by < size]
    return lax.ppermute(value, axis, pairs)


def per_head_norm(values, scale_gain):
    mean_square = jnp.mean(values * values, axis=-1, keepdims=True)
    return values * lax.rsqrt(mean_square + norm_epsilon) * scale_gain


def rope_tables(positions, head_dim):
    half_dim = head_dim // 2
    frequency = jnp.power(rope_base, -jnp.arange(half_dim, dtype=jnp.float32) * 2.0 / head_dim)
    angles = positions.astype(jnp.float32)[:, None] * frequency[None, :]
    return (jnp.cos(angles), jnp.sin(angles))


def rotate_feature_pairs(values, cosine_table, sine_values):
    half_dim = values.shape[-1] // 2
    first_half = values[..., :half_dim]
    second_half = values[..., half_dim:]
    cosine_table = cosine_table[:, None, :]
    sine_values = sine_values[:, None, :]
    return jnp.concatenate(
        [
            first_half * cosine_table - second_half * sine_values,
            second_half * cosine_table + first_half * sine_values,
        ],
        axis=-1,
    )


def request_starts(block_requests, all_requests):
    earlier = (all_requests[None, :] < block_requests[:, None]).astype(jnp.int32)
    return jnp.sum(earlier, axis=1) * BLOCK


def per_device_general(
    tokens,
    query_matrix,
    key_matrix,
    value_matrix,
    output_matrix,
    query_gain,
    key_norm_gain,
    adapter_down,
    adapter_up_query,
    key_value_up_panels,
    adapter_out_down,
    adapter_out_up,
    request_of_block,
    adapter_of_request,
):
    tok_rows, width_part = tokens.shape
    query_cols = query_matrix.shape[1]
    key_cols = key_matrix.shape[1]
    query_heads = query_cols // HEAD_SIZE
    block_count = tok_rows // BLOCK
    all_blocks = request_of_block.shape[0]
    request_total = adapter_of_request.shape[0]
    seq_index = lax.axis_index("seq")
    rep_index = lax.axis_index("rep")
    first_row = seq_index * tok_rows
    own_requests = lax.dynamic_slice_in_dim(
        request_of_block, seq_index * block_count, block_count, 0
    )
    request_match = own_requests[:, None] == jnp.arange(request_total, dtype=jnp.int32)[None, :]
    own_adapters = jnp.sum(jnp.where(request_match, adapter_of_request[None, :], 0), axis=1)
    pool_part = (
        lax.all_gather(adapter_down, "seq", axis=0, tiled=True),
        lax.all_gather(adapter_up_query, "seq", axis=0, tiled=True),
        lax.all_gather(key_value_up_panels, "seq", axis=0, tiled=True),
        lax.all_gather(adapter_out_down, "seq", axis=0, tiled=True),
        lax.all_gather(adapter_out_up, "seq", axis=0, tiled=True),
    )
    held_count = pool_part[0].shape[0]
    select = (own_adapters[:, None] == jnp.arange(held_count, dtype=jnp.int32)[None, :]).astype(
        jnp.bfloat16
    )
    (
        picked_down_panels,
        picked_query_panels,
        picked_key_panels,
        chosen_out_down,
        picked_output_up,
    ) = tuple(
        (
            jnp.einsum(
                "bn,n...->b...", select, panel_part, preferred_element_type=jnp.float32
            ).astype(jnp.bfloat16)
            for panel_part in pool_part
        )
    )
    token_block_list = tokens.reshape(block_count, BLOCK, width_part)
    partial_low = jnp.einsum(
        "myj,mjc->myc", token_block_list, picked_down_panels, preferred_element_type=jnp.float32
    ).reshape(tok_rows, 3 * ADAPTER_RANK)
    reduced_rank_rows = (
        lax.psum(partial_low, ("head", "rep"))
        .astype(jnp.bfloat16)
        .reshape(block_count, BLOCK, 3 * ADAPTER_RANK)
    )
    feature_part = lax.all_gather(tokens, ("head", "rep"), axis=1, tiled=True)
    query_add = jnp.dot(feature_part, query_matrix, preferred_element_type=jnp.float32)
    key_add = jnp.dot(feature_part, key_matrix, preferred_element_type=jnp.float32)
    value_add = jnp.dot(feature_part, value_matrix, preferred_element_type=jnp.float32)
    query_linear = query_add
    key_linear = key_add
    value_linear = value_add
    query_linear = query_linear + adapter_scale * jnp.einsum(
        "tlq,tqo->tlo",
        reduced_rank_rows[..., :ADAPTER_RANK],
        picked_query_panels,
        preferred_element_type=jnp.float32,
    ).reshape(tok_rows, query_cols)
    key_linear = key_linear + adapter_scale * jnp.einsum(
        "tlq,tqo->tlo",
        reduced_rank_rows[..., ADAPTER_RANK : 2 * ADAPTER_RANK],
        picked_key_panels[:, 0],
        preferred_element_type=jnp.float32,
    ).reshape(tok_rows, key_cols)
    value_linear = value_linear + adapter_scale * jnp.einsum(
        "tlq,tqo->tlo",
        reduced_rank_rows[..., 2 * ADAPTER_RANK :],
        picked_key_panels[:, 1],
        preferred_element_type=jnp.float32,
    ).reshape(tok_rows, key_cols)
    key_full = key_linear.astype(jnp.bfloat16)
    value_full = value_linear.astype(jnp.bfloat16)
    key_heads = key_cols // HEAD_SIZE
    token_index = first_row + jnp.arange(tok_rows, dtype=jnp.int32)
    token_request = jnp.repeat(own_requests, BLOCK)
    token_start = jnp.repeat(request_starts(own_requests, request_of_block), BLOCK)
    cosine_table, sine_values = rope_tables(token_index - token_start, HEAD_SIZE)
    query_rows = (
        rotate_feature_pairs(
            per_head_norm(query_linear.reshape(tok_rows, query_heads, HEAD_SIZE), query_gain),
            cosine_table,
            sine_values,
        )
        * score_scale
    ).astype(jnp.bfloat16)
    rotated_keys = rotate_feature_pairs(
        per_head_norm(
            key_full.astype(jnp.float32).reshape(tok_rows, key_heads, HEAD_SIZE), key_norm_gain
        ),
        cosine_table,
        sine_values,
    ).astype(jnp.bfloat16)
    group_heads = max(query_heads // 2, 1)
    group_size = query_heads // group_heads
    head_first = rep_index * query_heads // 2
    keys_used = lax.dynamic_slice_in_dim(rotated_keys, head_first, group_heads, 1).reshape(
        tok_rows, group_heads * HEAD_SIZE
    )
    values_used = lax.dynamic_slice_in_dim(
        value_full.reshape(tok_rows, key_heads, HEAD_SIZE), head_first, group_heads, 1
    ).reshape(tok_rows, group_heads * HEAD_SIZE)
    query_groups = query_rows.reshape(tok_rows, group_heads, group_size, HEAD_SIZE)
    block_table = jnp.arange(all_blocks, dtype=jnp.int32)
    empty_state = (
        jnp.zeros((tok_rows, group_heads, group_size, HEAD_SIZE), jnp.float32),
        jnp.zeros((group_heads, group_size, tok_rows), jnp.float32),
    )
    reach_blocks = KEY_WINDOW // tok_rows
    stacked = jnp.stack((keys_used, values_used))
    earlier = []
    for step_back in range(reach_blocks, 0, -1):
        earlier.append(shifted(stacked, "seq", step_back))
    window_stack = jnp.concatenate(earlier + [stacked], axis=1)
    fold_state = empty_state
    offset = first_row - reach_blocks * tok_rows
    key_block = window_stack[0]
    value_block = window_stack[1]
    key_length = key_block.shape[0]
    step_length = math.gcd(key_length, 512)
    steps_count = key_length // step_length
    key_steps = key_block.reshape(steps_count, step_length, group_heads, HEAD_SIZE)
    value_steps = value_block.reshape(steps_count, step_length, group_heads, HEAD_SIZE)

    def one_step(carry_state, step_inputs):
        step_keys, step_values, step_index = step_inputs
        key_position = offset + step_index * step_length + jnp.arange(step_length, dtype=jnp.int32)
        key_block_id = jnp.clip(key_position, 0, all_blocks * BLOCK - 1) // BLOCK
        key_request = jnp.sum(
            jnp.where(key_block_id[:, None] == block_table[None, :], request_of_block[None, :], 0),
            axis=1,
        )
        distance = token_index[:, None] - key_position[None, :]
        allowed = (
            (key_position[None, :] >= 0)
            & (distance >= 0)
            & (distance < KEY_WINDOW)
            & (token_request[:, None] == key_request[None, :])
        )
        scores = jnp.einsum(
            "tcpd,kcd->cptk", query_groups, step_keys, preferred_element_type=jnp.float32
        )
        weights = jnp.where(allowed[None, None], jnp.exp(scores), 0.0)
        numerator, denominator = carry_state
        denominator = denominator + jnp.sum(weights, axis=-1)
        numerator = numerator + jnp.einsum(
            "cptk,kcd->tcpd",
            weights.astype(jnp.bfloat16),
            step_values,
            preferred_element_type=jnp.float32,
        )
        return ((numerator, denominator), None)

    fold_state, unused_out = lax.scan(
        one_step, fold_state, (key_steps, value_steps, jnp.arange(steps_count, dtype=jnp.int32))
    )
    numerator, denominator = fold_state
    attention_result = (
        (numerator / jnp.transpose(denominator, (2, 0, 1))[..., None])
        .astype(jnp.bfloat16)
        .reshape(tok_rows, query_cols)
    )
    output_zero = (
        jnp.zeros((tok_rows, width_part), jnp.float32),
        jnp.zeros((tok_rows, ADAPTER_RANK), jnp.float32),
    )
    projected_rows = jnp.dot(
        lax.all_gather(attention_result, ("head", "rep"), axis=1, tiled=True),
        output_matrix,
        preferred_element_type=jnp.float32,
    )
    projected_rows, lowered = (projected_rows, output_zero[1])
    local_low = jnp.einsum(
        "bkc,bcr->bkr",
        attention_result.reshape(block_count, BLOCK, query_cols),
        chosen_out_down,
        preferred_element_type=jnp.float32,
    ).reshape(tok_rows, ADAPTER_RANK)
    output_reduced_rank = lax.psum(local_low, ("head", "rep")).astype(jnp.bfloat16)
    result = projected_rows + adapter_scale * jnp.einsum(
        "zch,zhp->zcp",
        output_reduced_rank.reshape(block_count, BLOCK, ADAPTER_RANK),
        picked_output_up,
        preferred_element_type=jnp.float32,
    ).reshape(tok_rows, width_part)
    return result.astype(jnp.bfloat16)


F32 = jnp.float32
BF16 = jnp.bfloat16
VMEM_SMALL = 20 * 1024 * 1024
VMEM_LARGE = 56 * 1024 * 1024
SWAP = [(0, 1), (1, 0)]
SHARD_BLOCKS = 4
CHUNK = 256
CHUNK_BLOCKS = CHUNK // BLOCK
META_ADAPTER = 3
META_REQUEST = 5


def dot(a, b):
    return lax.dot_general(a, b, (((1,), (0,)), ((), ())), preferred_element_type=F32)


def dot_t(a, b):
    return lax.dot_general(a, b, (((0,), (0,)), ((), ())), preferred_element_type=F32)


VM = pl.BlockSpec(memory_space=pltpu.VMEM)
SM = pl.BlockSpec(memory_space=pltpu.SMEM)
HB = pl.BlockSpec(memory_space=pl.ANY)
FAR = pl.BlockSpec(memory_space=pltpu.HBM)


def in_hbm(value):
    return pltpu.with_memory_space_constraint(value, pltpu.HBM)


def shape(dims, dtype=BF16):
    return jax.ShapeDtypeStruct(dims, dtype)


def call(kernel, name, out_shape, in_specs, args, scratch=(), out_specs=None, grid=None, after=(), aliases=None):
    count = len(in_specs)

    def body(*refs):
        kernel(*refs[:count], *refs[count + len(after) :])

    outs = out_specs
    if outs is None:
        outs = VM if isinstance(out_shape, jax.ShapeDtypeStruct) else tuple(VM for _ in out_shape)
    more = dict(grid=grid) if grid else {}
    return pl.pallas_call(
        body,
        out_shape=out_shape,
        in_specs=list(in_specs) + [HB] * len(after),
        out_specs=outs,
        scratch_shapes=list(scratch),
        input_output_aliases=aliases or {},
        compiler_params=pltpu.CompilerParams(vmem_limit_bytes=VMEM_SMALL),
        cost_estimate=pl.CostEstimate(flops=1000, bytes_accessed=1000, transcendentals=0),
        name=name,
        **more,
    )(*[in_hbm(a) if spec is FAR else a for a, spec in zip(args, in_specs)], *after)


def picked(adapters, held):
    me = lax.axis_index("seq").astype(jnp.int32)
    chosen = []
    for step in range(4):
        quarter = jnp.bitwise_xor(me, step)
        slot = adapters[lax.div(quarter, 2)] - me * held
        here = jnp.logical_and(slot >= 0, slot < held)
        keep = jnp.where(here, 1.0, 0.0).astype(F32)
        chosen.append((jnp.clip(slot, 0, held - 1), keep, lax.rem(quarter, 2)))
    return chosen


def bring(sources, targets, sems):
    copies = [pltpu.make_async_copy(a, b, sems.at[i]) for i, (a, b) in enumerate(zip(sources, targets))]
    for copy in copies:
        copy.start()
    for copy in copies:
        copy.wait()


def pack_kernel(adapters, down_far, up_q_far, up_kv_far, *refs):
    quarters, (down, up_q, up_kv, sems) = refs[:4], refs[4:]
    bring((down_far, up_q_far, up_kv_far), (down, up_q, up_kv), sems)
    rep = lax.axis_index("rep").astype(jnp.int32)
    half = up_kv.shape[3] // 2
    cols = up_q.shape[2]
    width = down.shape[2]
    for (slot, keep, part), out in zip(picked(adapters, down.shape[0]), quarters):
        rows = pl.ds(pl.multiple_of(part * 48, 16), 48)
        ranks = pl.ds(pl.multiple_of(part * 16, 16), 16)
        out[0:48, :] = (down[slot, rows, :].astype(F32) * keep).astype(BF16)
        out[48:64, 0:cols] = (up_q[slot, ranks, :].astype(F32) * keep).astype(BF16)
        for which in range(2):
            both = up_kv[slot, which, ranks, :].astype(F32) * keep
            mine = jnp.where(rep == 0, both[:, :half], both[:, half:])
            out[48:64, cols + which * half : cols + (which + 1) * half] = mine.astype(BF16)
        out[48:64, 1024:width] = jnp.zeros((16, width - 1024), BF16)


def pack_out_kernel(adapters, out_down_far, out_up_far, out, out_down, out_up, sems):
    bring((out_down_far, out_up_far), (out_down, out_up), sems)
    width = out_up.shape[2]
    held = out_up.shape[0]
    for request in range(2):
        slot = adapters[request] - lax.axis_index("seq").astype(jnp.int32) * held
        here = jnp.logical_and(slot >= 0, slot < held)
        keep = jnp.where(here, 1.0, 0.0).astype(F32)
        slot = jnp.clip(slot, 0, held - 1)
        rows = slice(request * 32, (request + 1) * 32)
        out[rows, 0:width] = (out_up[slot].astype(F32) * keep).astype(BF16)
        out[rows, width:1408] = jnp.zeros((32, 1408 - width), BF16)
        out[rows, 1408:1920] = (out_down[slot].astype(F32) * keep).astype(BF16)


def add_kernel(a, b, up, down):
    width = up.shape[1]
    up[...] = a[:, 0:width] + b[:, 0:width]
    down[...] = a[:, 1408:1920] + b[:, 1408:1920]


def sum_kernel(a, b, c, d, out):
    out[...] = a[...] + b[...] + c[...] + d[...]


def place_quarters(meta, quarters, panel):
    me = meta[0]
    low_side = me < 2
    at = (me, jnp.bitwise_xor(me, 1), jnp.where(low_side, 2, 1), jnp.where(low_side, 3, 0))
    for index, quarter in zip(at, quarters):
        panel[index] = quarter[...]


def low_kernel(meta, tokens, p0, p1, p2, p3, low_t, ups, panel):
    place_quarters(meta, (p0, p1, p2, p3), panel)
    down = jnp.concatenate([panel[j, 0:48, :] for j in range(4)], axis=0)
    both = dot(down, tokens[...])
    for b in range(SHARD_BLOCKS):
        request = meta[META_REQUEST + meta[0] * SHARD_BLOCKS + b]
        at = slice(b * BLOCK, (b + 1) * BLOCK)
        fa = jnp.where(request == 0, 1.0, 0.0).astype(F32)
        low_t[:, at] = both[0:96, at] * fa + both[96:192, at] * (1.0 - fa)
    ups[...] = jnp.concatenate([panel[j, 48:64, 0:1024] for j in range(4)], axis=0)


def weight_copies(meta, weights, buffers, sems, chip, width):
    half = weights[0].shape[1] // 2
    lane = pl.ds(pl.multiple_of(meta[1] * half, BLOCK), half)
    copies = []
    for i, (w, buf) in enumerate(zip(weights, buffers)):
        lanes = lane if i < 2 else slice(None)
        for n, part in enumerate((chip + meta[1], chip + 1 - meta[1])):
            rows = pl.ds(pl.multiple_of(part * width, 16), width)
            copies.append(pltpu.make_async_copy(w.at[rows, lanes], buf.at[n], sems.at[i, n]))
    return copies


WEIGHT_AT = (slice(0, 256), slice(256, 512), slice(512, 1024))


def near_kernel(meta, own, other, wq, wk, wv, out0, out1, fk, fv, fq, bk, bv, bq, sems, far_sems):
    weights = (wk, wv, wq)
    width = other.shape[0]
    copies = weight_copies(meta, weights, (bk, bv, bq), sems, meta[2] * 2, width)
    later = weight_copies(meta, weights, (fk, fv, fq), far_sems, (1 - meta[2]) * 2, width)
    for copy in copies:
        copy.start()
    for i, (at, buf) in enumerate(zip(WEIGHT_AT, (bk, bv, bq))):
        copies[2 * i].wait()
        copies[2 * i + 1].wait()
        if i == 1:
            for copy in later:
                copy.start()
        for c, out in enumerate((out0, out1)):
            tok = slice(c * CHUNK, (c + 1) * CHUNK)
            out[:, at] = dot_t(own[:, tok], buf[0]) + dot_t(other[:, tok], buf[1])
    for copy in later:
        copy.wait()


def far_kernel(part, own, other, wk, wv, wq, q_out, kv_out):
    for i, (at, w) in enumerate(zip(WEIGHT_AT, (wk, wv, wq))):
        turned = jnp.transpose(part[:, at] + dot_t(own[...], w[0]) + dot_t(other[...], w[1]))
        if i == 2:
            q_out[...] = turned
        else:
            kv_out[at, :] = turned.astype(BF16)


def block_request(meta, block):
    return meta[META_REQUEST + jnp.maximum(block, 0)]


def by_request(meta, low, first_block):
    flags = []
    for b in range(SHARD_BLOCKS):
        request = block_request(meta, first_block + b)
        flags.append(jnp.full((1, BLOCK), jnp.where(request == 0, 1.0, 0.0).astype(F32)))
    flag = jnp.concatenate(flags, axis=1)
    rows = low.astype(BF16).astype(F32)
    return jnp.concatenate([rows * flag, rows * (1.0 - flag)], axis=0).astype(BF16)


def norm_rotate(x, gain, cosine, sine):
    mean_square = jnp.mean(x * x, axis=0, keepdims=True)
    u = x * lax.rsqrt(mean_square + norm_epsilon) * gain
    a = u[0:64]
    b = u[64:128]
    return jnp.concatenate([a * cosine - b * sine, b * cosine + a * sine], axis=0)


def gain_rows(gain):
    return jnp.transpose(jnp.broadcast_to(gain[...], (HEAD_SIZE, HEAD_SIZE)))


def finish_keys(meta, chunks, low_k, low_v, ups, gain, cosine, sine, keys, values, first, blocks):
    base = (meta[0] - 2) * SHARD_BLOCKS + first
    k_term = dot_t(ups[:, 512:768], by_request(meta, low_k, base))
    v_term = dot_t(ups[:, 768:1024], by_request(meta, low_v, base))
    for b in blocks:
        at = slice((first + b) * BLOCK, (first + b + 1) * BLOCK)
        here = slice(b * BLOCK, (b + 1) * BLOCK)
        chunk = chunks[b // CHUNK_BLOCKS]
        lanes = slice(b % CHUNK_BLOCKS * BLOCK, (b % CHUNK_BLOCKS + 1) * BLOCK)
        for g in range(2):
            head = slice(g * HEAD_SIZE, (g + 1) * HEAD_SIZE)
            k = chunk[head, lanes].astype(F32) + adapter_scale * k_term[head, here]
            k = k.astype(BF16).astype(F32)
            turned = norm_rotate(k, gain, cosine[:, at], sine[:, at])
            keys[here, head] = jnp.transpose(turned).astype(BF16)
        values[:, here] = (chunk[256:512, lanes].astype(F32) + adapter_scale * v_term[:, here]).astype(BF16)


def attend(meta, q_rot, keys, values, c, g, first, low_block, high_block):
    rows = slice(c * BLOCK, (c + 1) * BLOCK)
    heads = [slice((2 * g + h) * HEAD_SIZE, (2 * g + h + 1) * HEAD_SIZE) for h in range(2)]
    q = jnp.concatenate([q_rot[head, rows] for head in heads], axis=1)
    base = (meta[0] - 2) * SHARD_BLOCKS
    mine = block_request(meta, base + 8 + c)
    head = slice(g * HEAD_SIZE, (g + 1) * HEAD_SIZE)
    at = slice(low_block * BLOCK, (high_block + 1) * BLOCK)
    scores = dot(keys[at, head], q)
    key = lax.broadcasted_iota(jnp.int32, (BLOCK, 2 * BLOCK), 0)
    query = jnp.bitwise_and(lax.broadcasted_iota(jnp.int32, (BLOCK, 2 * BLOCK), 1), BLOCK - 1)
    den = jnp.zeros((BLOCK, 2 * BLOCK), F32)
    pieces = []
    for j in range(low_block, high_block + 1):
        block = base + first + j
        ok = jnp.logical_and(block >= 0, block_request(meta, block) == mine)
        piece = jnp.exp(scores[(j - low_block) * BLOCK : (j - low_block + 1) * BLOCK])
        piece = piece * jnp.where(ok, 1.0, 0.0).astype(F32)
        if first + j == c + 8:
            piece = jnp.where(query >= key, piece, 0.0)
        if first + j == c:
            piece = jnp.where(query < key, piece, 0.0)
        den = den + piece
        pieces.append(piece.astype(BF16))
    num = dot(values[head, at], jnp.concatenate(pieces, axis=0))
    return num, jnp.sum(den, axis=0, keepdims=True)


def attend_own_kernel(
    meta, q0, q1, o0, o1, low, ups, q_gain, k_gain, cosine, sine, weights,
    q_rot, num_out, den_out, weights_out, keys, values, sem,
):
    fetch = pltpu.make_async_copy(weights, weights_out, sem)
    fetch.start()
    finish_keys(
        meta, (o0, o1), low[32:64, :], low[64:96, :], ups, gain_rows(k_gain), cosine, sine, keys, values, 8, range(4)
    )
    gain = gain_rows(q_gain)
    q_term = dot_t(ups[:, 0:512], by_request(meta, low[0:32, :], meta[0] * SHARD_BLOCKS))
    for c in range(SHARD_BLOCKS):
        q = (q0, q1)[c // CHUNK_BLOCKS]
        lanes = slice(c % CHUNK_BLOCKS * BLOCK, (c % CHUNK_BLOCKS + 1) * BLOCK)
        rows = slice(c * BLOCK, (c + 1) * BLOCK)
        at = slice((8 + c) * BLOCK, (9 + c) * BLOCK)
        for h in range(4):
            head = slice(h * HEAD_SIZE, (h + 1) * HEAD_SIZE)
            x = q[head, lanes] + adapter_scale * q_term[head, rows]
            q_rot[head, rows] = (norm_rotate(x, gain, cosine[:, at], sine[:, at]) * score_scale).astype(BF16)
    for g in range(2):
        for c in range(SHARD_BLOCKS):
            rows = slice(c * BLOCK, (c + 1) * BLOCK)
            num, den = attend(meta, q_rot, keys, values, c, g, 8, 0, c)
            for h in range(2):
                n = 2 * g + h
                part = slice(h * BLOCK, (h + 1) * BLOCK)
                num_out[n * HEAD_SIZE : (n + 1) * HEAD_SIZE, rows] = num[:, part]
                den_out[n : n + 1, rows] = den[:, part]
    fetch.wait()


def attend_prev_kernel(
    meta, q_rot, num_in, den_in, h0, h1, low_h, ups, k_gain, cosine, sine, num_out, den_out, keys, values
):
    finish_keys(
        meta, (h0, h1), low_h[0:32, :], low_h[32:64, :], ups, gain_rows(k_gain), cosine, sine, keys, values, 4, range(4)
    )
    for g in range(2):
        for c in range(SHARD_BLOCKS):
            rows = slice(c * BLOCK, (c + 1) * BLOCK)
            num, den = attend(meta, q_rot, keys, values, c, g, 4, 0, 3)
            for h in range(2):
                n = 2 * g + h
                part = slice(h * BLOCK, (h + 1) * BLOCK)
                head = slice(n * HEAD_SIZE, (n + 1) * HEAD_SIZE)
                num_out[head, rows] = num_in[head, rows] + num[:, part]
                den_out[n : n + 1, rows] = den_in[n : n + 1, rows] + den[:, part]


def attend_far_kernel(chunk, meta, q_rot, num_in, den_in, *refs):
    count = CHUNK_BLOCKS - chunk
    kept, (low_h, ups, k_gain, cosine, sine, out, keys, values) = refs[:count], refs[count:]
    blocks = range(chunk * CHUNK_BLOCKS, SHARD_BLOCKS)
    finish_keys(
        meta, (None,) * chunk + tuple(kept), low_h[0:32, :], low_h[32:64, :], ups, gain_rows(k_gain), cosine, sine,
        keys, values, 0, blocks,
    )
    for g in range(2):
        for c in range(chunk * CHUNK_BLOCKS, (chunk + 1) * CHUNK_BLOCKS):
            rows = slice(c * BLOCK, (c + 1) * BLOCK)
            here = slice(c % CHUNK_BLOCKS * BLOCK, (c % CHUNK_BLOCKS + 1) * BLOCK)
            num, den = attend(meta, q_rot, keys, values, c, g, 0, c, 3)
            for h in range(2):
                n = 2 * g + h
                part = slice(h * BLOCK, (h + 1) * BLOCK)
                head = slice(n * HEAD_SIZE, (n + 1) * HEAD_SIZE)
                total = den_in[n : n + 1, rows] + den[:, part]
                out[head, here] = ((num_in[head, rows] + num[:, part]) / total).astype(BF16)


def request_flag(meta):
    flags = []
    for b in range(SHARD_BLOCKS):
        request = block_request(meta, meta[0] * SHARD_BLOCKS + b)
        flags.append(jnp.full((1, BLOCK), jnp.where(request == 0, 1.0, 0.0).astype(F32)))
    return jnp.concatenate(flags, axis=1)


def out_low_kernel(meta, att0, att1, panel_a, panel_b, low):
    down = panel_a[...] + panel_b[...]
    both = jnp.concatenate([dot(down, att0[...]), dot(down, att1[...])], axis=1)
    flag = request_flag(meta)
    low[...] = both[0:32] * flag + both[32:64] * (1.0 - flag)


def part_lanes(meta, chip, cols):
    return [pl.ds(pl.multiple_of(p * cols, BLOCK), cols) for p in (chip + meta[1], chip + 1 - meta[1])]


def out_near_kernel(meta, own, other, w, part):
    first, second = part_lanes(meta, meta[2] * 2, own.shape[0])
    part[...] = dot(w[:, first], own[...]) + dot(w[:, second], other[...])


def out_far_kernel(chunk, meta, own, other, w, part, low, panel_a, panel_b, *refs):
    out = refs[-1]
    tok = slice(chunk * CHUNK, (chunk + 1) * CHUNK)
    lows = low[:, tok].astype(BF16).astype(F32)
    flag = request_flag(meta)[:, tok]
    chosen = jnp.concatenate([lows * flag, lows * (1.0 - flag)], axis=0).astype(BF16)
    up = panel_a[...] + panel_b[...]
    first, second = part_lanes(meta, (1 - meta[2]) * 2, own.shape[0])
    total = part[...] + adapter_scale * dot_t(up, chosen)
    out[...] = (total + dot(w[:, first], own[...]) + dot(w[:, second], other[...])).astype(BF16)


def exchange_quarters(quarters):
    return [quarters[0]] + [lax.ppermute(quarters[s], "seq", [(j, j ^ s) for j in range(4)]) for s in (1, 2, 3)]


def share_quarter(total):
    beside = lax.ppermute(total, "seq", [(j, j ^ 1) for j in range(4)])
    middle = [(1, 2), (2, 1)]
    return [total, beside, lax.ppermute(total, "seq", middle), lax.ppermute(beside, "seq", middle)]


def per_device(
    tokens,
    query_matrix,
    key_matrix,
    value_matrix,
    output_matrix,
    query_gain,
    key_norm_gain,
    adapter_down,
    adapter_up_query,
    key_value_up_panels,
    adapter_out_down,
    adapter_out_up,
    request_of_block,
    adapter_of_request,
):
    rows, width = tokens.shape
    cols = query_matrix.shape[1]
    seq, rep, head = (lax.axis_index(name).astype(jnp.int32) for name in ("seq", "rep", "head"))
    meta = jnp.concatenate([jnp.stack([seq, rep, head]), adapter_of_request, request_of_block])
    tokens = tokens.T

    def across(value):
        return lax.ppermute(value, "head", SWAP)

    def core(value):
        return lax.ppermute(value, "rep", SWAP)

    def up(value, by=1):
        return lax.ppermute(value, "seq", [(i, (i + by) % 4) for i in range(4)])

    def after(value, *others):
        return lax.optimization_barrier((value, *others))[0]

    far_own = across(tokens)
    near_other = core(tokens)

    def swapped(value, by):
        return lax.ppermute(value, "seq", [(j, j ^ by) for j in range(4)])

    def pack(kernel, name, result, pools, order):
        return call(
            kernel,
            name,
            result,
            [SM] + [FAR] * len(pools),
            [adapter_of_request, *pools],
            [pltpu.VMEM(pool.shape, BF16) for pool in pools] + [pltpu.SemaphoreType.DMA((len(pools),))],
            after=order,
        )

    pools = [jnp.swapaxes(adapter_down, 1, 2), adapter_up_query, key_value_up_panels]
    quarters = pack(pack_kernel, "pack", (shape((64, width)),) * 4, pools, [])
    received = exchange_quarters(quarters)
    out_pools = [jnp.swapaxes(adapter_out_down, 1, 2), adapter_out_up]
    out_panel = pack(pack_out_kernel, "pack_out", shape((64, 1920)), out_pools, [quarters[0]])
    out_beside = swapped(out_panel, 1)

    chunks = rows // CHUNK
    weights = [query_matrix, key_matrix, value_matrix]
    weight_scratch = [
        pltpu.VMEM((2, width, 256), BF16),
        pltpu.VMEM((2, width, 256), BF16),
        pltpu.VMEM((2, width, cols), BF16),
        pltpu.SemaphoreType.DMA((3, 2)),
    ]
    weight_shapes = [(2, width, 256), (2, width, 256), (2, width, cols)]
    near0, near1, *far_weights = call(
        near_kernel,
        "near",
        (shape((CHUNK, 1024), F32),) * chunks + tuple(shape(dims) for dims in weight_shapes),
        [SM, VM, VM, FAR, FAR, FAR],
        [meta, tokens, near_other, *weights],
        [pltpu.VMEM(dims, BF16) for dims in weight_shapes] + [pltpu.SemaphoreType.DMA((3, 2))] * 2,
        after=[out_panel],
    )
    near = [near0, near1]

    def project(c, prior):
        mine = pl.BlockSpec((width, CHUNK), lambda i: (0, c))
        return call(
            far_kernel,
            "far",
            (shape((cols, CHUNK), F32), shape((512, CHUNK))),
            [VM, mine, mine, VM, VM, VM],
            [near[c], far_own, far_other, *far_weights],
            grid=(1,),
            after=[prior],
        )

    all_blocks = request_of_block.shape[0]
    window = jnp.arange(3 * rows, dtype=jnp.int32) + (seq - 2) * rows
    window = jnp.clip(window, 0, all_blocks * BLOCK - 1)
    second_start = jnp.sum((request_of_block < 1).astype(jnp.int32)) * BLOCK
    position = jnp.where(window >= second_start, window - second_start, window)
    half_dim = HEAD_SIZE // 2
    frequency = jnp.power(rope_base, -jnp.arange(half_dim, dtype=F32) * 2.0 / HEAD_SIZE)
    angles = frequency[:, None] * position.astype(F32)[None, :]
    cosine, sine = jnp.cos(angles), jnp.sin(angles)
    q_gain = query_gain.reshape(1, HEAD_SIZE)
    k_gain = key_norm_gain.reshape(1, HEAD_SIZE)

    quarter = call(sum_kernel, "sum", shape((64, width)), [VM] * 4, received, after=[near[0], cosine, sine])
    pieces = share_quarter(quarter)
    up_pair, down_pair = call(
        add_kernel,
        "out_add",
        (shape((64, width)), shape((64, cols))),
        [VM] * 2,
        [out_panel, out_beside],
        after=[quarter],
    )
    down_rest = swapped(down_pair, 2)
    far_other = core(after(far_own, pieces[1], pieces[2], down_pair))
    late_q, late_kv = project(1, pieces[1])
    partial_low, ups = call(
        low_kernel,
        "low",
        (shape((96, rows), F32), shape((64, 1024))),
        [SM] + [VM] * 5,
        [meta, tokens, *pieces],
        [pltpu.VMEM((4, 64, width), BF16)],
        after=[late_kv],
    )
    chip_low = partial_low + core(partial_low)
    early_q, early_kv = project(0, chip_low)
    low = chip_low + across(chip_low)

    prev_late, prev_early = up(late_kv), up(early_kv)
    low_kv = low[32:96].astype(BF16)
    low_prev = up(low_kv)
    low_prev2 = up(low_prev)
    prev2_late = up(after(prev_late, early_kv))

    shard_scratch = [pltpu.VMEM((rows, 256), BF16), pltpu.VMEM((256, rows), BF16)]
    sums = (shape((cols, rows), F32), shape((8, rows), F32))
    q_rot, num, den, out_weights = call(
        attend_own_kernel,
        "attend_own",
        (shape((cols, rows)), *sums, shape(output_matrix.T.shape)),
        [SM] + [VM] * 10 + [FAR],
        [meta, early_q, late_q, early_kv, late_kv, low, ups, q_gain, k_gain, cosine, sine, output_matrix.T],
        shard_scratch + [pltpu.SemaphoreType.DMA],
    )
    prev2_early = up(after(prev_early, low_prev, num))
    num, den = call(
        attend_prev_kernel,
        "attend_prev",
        sums,
        [SM] + [VM] * 10,
        [meta, q_rot, num, den, prev_early, prev_late, low_prev, ups, k_gain, cosine, sine],
        shard_scratch,
    )

    def attend_far(chunk, kept, order):
        return call(
            functools.partial(attend_far_kernel, chunk),
            "attend_far",
            shape((cols, CHUNK)),
            [SM] + [VM] * (8 + len(kept)),
            [meta, q_rot, num, den, *kept, low_prev2, ups, k_gain, cosine, sine],
            shard_scratch,
            after=order,
        )

    att_late = attend_far(1, [prev2_late], [])
    att_early = attend_far(0, [prev2_early, prev2_late], [att_late, down_rest])

    up_rest = swapped(up_pair, 2)
    crossed = [(chunk, across(att)) for chunk, att in ((1, att_late), (0, att_early))]
    parts = []
    for att in (att_late, att_early):
        parts.append(
            call(
                out_near_kernel,
                "out_near",
                shape((width, CHUNK), F32),
                [SM] + [VM] * 3,
                [meta, att, core(att), out_weights],
                after=[att_early] + parts,
            )
        )
    out_low = call(
        out_low_kernel,
        "out_low",
        shape((32, rows), F32),
        [SM] + [VM] * 4,
        [meta, att_early, att_late, down_pair, down_rest],
        after=[parts[1]],
    )
    out_low = out_low + core(out_low)
    out_low = out_low + across(out_low)

    result = []
    for (chunk, att_far), part in zip(crossed, parts):
        result = [
            call(
                functools.partial(out_far_kernel, chunk),
                "out_far",
                shape((width, rows)),
                [SM] + [VM] * 7 + [HB] * len(result),
                [meta, att_far, core(after(att_far, out_low, up_rest)), out_weights, part, out_low, up_pair, up_rest, *result],
                out_specs=pl.BlockSpec((width, CHUNK), lambda i, chunk=chunk: (0, chunk)),
                grid=(1,),
                aliases={8: 0} if result else {},
            )
        ]
    return result[0].T


def plain_sizes(mesh):
    return mesh.shape["seq"] == 4 and mesh.shape["head"] == 2 and mesh.shape["rep"] == 2


def solution(mesh):
    return jax.shard_map(
        per_device if plain_sizes(mesh) else per_device_general,
        mesh=mesh,
        in_specs=(
            P(("groups", "seq"), ("head", "rep")),
            P(None, ("head", "rep")),
            P(None, "head"),
            P(None, "head"),
            P(None, ("head", "rep")),
            P(),
            P(),
            P("seq", ("head", "rep"), None),
            P("seq", None, ("head", "rep")),
            P("seq", None, None, "head"),
            P("seq", ("head", "rep"), None),
            P("seq", None, ("head", "rep")),
            P("groups"),
            P("groups"),
        ),
        out_specs=P(("groups", "seq"), ("head", "rep")),
        check_vma=False,
    )
```
